32 devices in a mesh: fsdp: 4 (over y, x), heads: 2 (over core), tensor: 4 (over z).
Axes of the slice: x: 2, y: 2, z: 4, core: 2. Of those that a mesh axis runs over, the one named last changes fastest.
Arguments:
- inputs: float32 [32, 729, 1152], P(('fsdp', 'heads', 'tensor')), may hold values from -6 to 6
- cotangent: float32 [32, 729, 1152], P(('fsdp', 'heads', 'tensor')), may hold values from -6 to 6
- image_adapter_index: int32 [32], replicated, may hold values from 0 to 7
- first_norm_gain: float32 [1152], replicated, may hold values from 0.5 to 1.5
- first_norm_bias: float32 [1152], replicated, may hold values from -3 to 3
- second_norm_gain: float32 [1152], replicated, may hold values from 0.5 to 1.5
- second_norm_bias: float32 [1152], replicated, may hold values from -3 to 3
- query_key_value_weight: bfloat16 [1152, 3, 1152], P('fsdp', None, 'heads'), may hold values from -0.1875 to 0.1875
- attention_output_weight: bfloat16 [1152, 1152], P('fsdp', 'heads'), may hold values from -3 to 3
- up_weight: bfloat16 [1152, 4304], P('fsdp', 'tensor'), may hold values from -0.1875 to 0.1875
- down_weight: bfloat16 [1152, 4304], P('fsdp', 'tensor'), may hold values from -0.09375 to 0.09375
- up_projection_bias: bfloat16 [4304], P('tensor'), may hold values from -3 to 3
- down_projection_bias: bfloat16 [1152], replicated, may hold values from -3 to 3
- query_key_value_adapter_first: bfloat16 [3, 8, 1152, 16], replicated, may hold values from -0.1875 to 0.1875
- query_key_value_adapter_second: bfloat16 [3, 8, 16, 1152], P(None, None, None, 'heads'), may hold values from -0.75 to 0.75
- projection_adapter_first: bfloat16 [8, 1152, 16], P(None, 'heads'), may hold values from -3 to 3
- projection_adapter_second: bfloat16 [8, 16, 1152], replicated, may hold values from -0.75 to 0.75
- up_adapter_first: bfloat16 [8, 1152, 16], replicated, may hold values from -0.1875 to 0.1875
- up_adapter_second: bfloat16 [8, 16, 4304], P(None, None, 'tensor'), may hold values from -0.75 to 0.75
- down_adapter_first: bfloat16 [8, 16, 4304], P(None, None, 'tensor'), may hold values from -0.09375 to 0.09375
- down_adapter_second: bfloat16 [8, 16, 1152], replicated, may hold values from -0.75 to 0.75
Outputs:
- layer_output: float32 [32, 729, 1152], P(('fsdp', 'heads', 'tensor'))
- grad_input: float32 [32, 729, 1152], P(('fsdp', 'heads', 'tensor'))
- grad_qkv_in: float32 [3, 8, 1152, 16], replicated
- grad_qkv_out: float32 [3, 8, 16, 1152], P(None, None, None, 'heads')
- grad_proj_in: float32 [8, 1152, 16], P(None, 'heads')
- grad_proj_out: float32 [8, 16, 1152], replicated
- grad_up_in: float32 [8, 1152, 16], replicated
- grad_up_out: float32 [8, 16, 4304], P(None, None, 'tensor')
- grad_down_in: float32 [8, 16, 4304], P(None, None, 'tensor')
- grad_down_out: float32 [8, 16, 1152], replicated
The draws below stay inside these ranges and needn't reach their ends.
All inputs are finite; a program needn't handle non-finite values.
Results may differ from the reference program's by a relative error of at most 0.02.
Values may be sent and summed in bfloat16 or wider, within the bound.
A program may use at most 256 MiB of HBM per device.

```python
import math
import jax
import jax.numpy as jnp
import numpy as np
from jax import lax

MODEL_WIDTH = 1152
HEADS = 16
HEAD_DIM = 72
FEEDFORWARD_UNITS = 4304
SEQ = 729
ADAPTER_RANK = 16
ADAPTER_COUNT = 8
IMAGES = 32


def place_ends(drawn, own_key, smallest, high):
    dims = drawn.shape
    place = [jax.random.randint(jax.random.fold_in(own_key, axis), (), 0, dims[axis]) for axis in range(len(dims))]
    drawn = drawn.at[tuple(place)].set(smallest)
    longest = dims.index(max(dims))
    place[longest] = (place[longest] + 1) % dims[longest]
    return drawn.at[tuple(place)].set(high)


def block_levels(own_key, extent, split, low, largest):
    def one(axis_at, parts):
        draws = jax.random.uniform(jax.random.fold_in(jax.random.fold_in(own_key, 6), axis_at), (parts,), jnp.float32, low / len(split), largest / len(split))
        return jnp.repeat(jnp.exp(draws), extent[axis_at] // parts).reshape((-1,) + (1,) * (len(extent) - axis_at - 1))

    level = one(*split[0])
    for cut in split[1:]:
        level = level * one(*cut)
    return level


def cumulative_ranks(count, skew):
    portions = [(1 << 20) // math.isqrt(rank ** skew) + 1 for rank in range(1, count + 1)]
    scale = 1 + sum(portions) // (1 << 30)
    return np.cumsum(np.array([max(1, weight // scale) for weight in portions]))


def skewed_ids(key, extent, number_of, skew):
    table = cumulative_ranks(number_of, skew)
    lot = jax.random.randint(jax.random.fold_in(key, 1), extent, 0, int(table[number_of - 1]))
    rank = jnp.searchsorted(jnp.asarray(table, jnp.int32), lot, side="right")
    return jax.random.permutation(jax.random.fold_in(key, 2), number_of)[rank].astype(jnp.int32)


def scatter_about(rng, extent, spread, limit, cuts=(), dtype=jnp.bfloat16):
    factor_of = block_levels(rng, extent, cuts, -0.22, 0.18) if cuts else 1.0
    values = jax.random.normal(rng, extent, jnp.float32) * spread * factor_of
    return jnp.minimum(jnp.maximum(values, -limit), limit).astype(dtype)


def setup_inputs(seed: int = 0) -> dict:
    arg_keys = jax.random.split(jax.random.key(seed), 22)
    return {
        "inputs": scatter_about(arg_keys[0], (IMAGES, SEQ, MODEL_WIDTH), 1.0, 6.0, ((0, 32),), jnp.float32),
        "cotangent": scatter_about(arg_keys[1], (IMAGES, SEQ, MODEL_WIDTH), 1.0, 6.0, ((0, 32),), jnp.float32),
        "image_adapter_index": place_ends(skewed_ids(arg_keys[2], (IMAGES,), ADAPTER_COUNT, 2), jax.random.fold_in(arg_keys[2], 3), 0, ADAPTER_COUNT - 1).astype(jnp.int32),
        "first_norm_gain": jnp.clip(1.0 + 0.1 * jax.random.normal(arg_keys[3], (MODEL_WIDTH,), jnp.float32), 0.5, 1.5),
        "first_norm_bias": scatter_about(arg_keys[4], (MODEL_WIDTH,), 0.5, 3.0, (), jnp.float32),
        "second_norm_gain": jnp.clip(1.0 + 0.1 * jax.random.normal(arg_keys[5], (MODEL_WIDTH,), jnp.float32), 0.5, 1.5),
        "second_norm_bias": scatter_about(arg_keys[6], (MODEL_WIDTH,), 0.5, 3.0, (), jnp.float32),
        "query_key_value_weight": scatter_about(arg_keys[7], (MODEL_WIDTH, 3, MODEL_WIDTH), MODEL_WIDTH ** -0.5, 0.1875, ((0, 4), (2, 2))),
        "attention_output_weight": scatter_about(arg_keys[8], (MODEL_WIDTH, MODEL_WIDTH), (max(MODEL_WIDTH // 256, 1)) ** -0.5, 3.0, ((0, 4), (1, 2))),
        "up_weight": scatter_about(arg_keys[9], (MODEL_WIDTH, FEEDFORWARD_UNITS), MODEL_WIDTH ** -0.5, 0.1875, ((0, 4), (1, 4))),
        "down_weight": scatter_about(arg_keys[10], (MODEL_WIDTH, FEEDFORWARD_UNITS), FEEDFORWARD_UNITS ** -0.5, 0.09375, ((0, 4), (1, 4))),
        "up_projection_bias": scatter_about(arg_keys[11], (FEEDFORWARD_UNITS,), 0.5, 3.0, ((0, 4),)),
        "down_projection_bias": scatter_about(arg_keys[12], (MODEL_WIDTH,), 0.5, 3.0),
        "query_key_value_adapter_first": scatter_about(arg_keys[13], (3, ADAPTER_COUNT, MODEL_WIDTH, ADAPTER_RANK), MODEL_WIDTH ** -0.5, 0.1875),
        "query_key_value_adapter_second": scatter_about(arg_keys[14], (3, ADAPTER_COUNT, ADAPTER_RANK, MODEL_WIDTH), (4 * ADAPTER_RANK) ** -0.5, 0.75, ((3, 2),)),
        "projection_adapter_first": scatter_about(arg_keys[15], (ADAPTER_COUNT, MODEL_WIDTH, ADAPTER_RANK), (max(MODEL_WIDTH // 256, 1)) ** -0.5, 3.0, ((1, 2),)),
        "projection_adapter_second": scatter_about(arg_keys[16], (ADAPTER_COUNT, ADAPTER_RANK, MODEL_WIDTH), (4 * ADAPTER_RANK) ** -0.5, 0.75),
        "up_adapter_first": scatter_about(arg_keys[17], (ADAPTER_COUNT, MODEL_WIDTH, ADAPTER_RANK), MODEL_WIDTH ** -0.5, 0.1875),
        "up_adapter_second": scatter_about(arg_keys[18], (ADAPTER_COUNT, ADAPTER_RANK, FEEDFORWARD_UNITS), (4 * ADAPTER_RANK) ** -0.5, 0.75, ((2, 4),)),
        "down_adapter_first": scatter_about(arg_keys[19], (ADAPTER_COUNT, ADAPTER_RANK, FEEDFORWARD_UNITS), FEEDFORWARD_UNITS ** -0.5, 0.09375, ((2, 4),)),
        "down_adapter_second": scatter_about(arg_keys[20], (ADAPTER_COUNT, ADAPTER_RANK, MODEL_WIDTH), (4 * ADAPTER_RANK) ** -0.5, 0.75),
    }


@jax.custom_vjp
def reduced_precision(v):
    return lax.optimization_barrier(v.astype(jnp.bfloat16)).astype(jnp.float32)

@jax.custom_vjp
def low_back(v):
    return v

def low_keep(v):
    return (reduced_precision(v), None)

def low_pass(kept, grad):
    return (grad,)

def back_keep(v):
    return (v, None)

def back_low(kept, grad):
    return (reduced_precision(grad),)
reduced_precision.defvjp(low_keep, low_pass)
low_back.defvjp(back_keep, back_low)
highest_precision = lax.Precision.HIGHEST

def layer_norm(values, gain, bias):
    mean = lax.optimization_barrier(jnp.mean(values, axis=-1, keepdims=True))
    centred = values - mean
    variance = lax.optimization_barrier(jnp.mean(centred * centred, axis=-1, keepdims=True))
    return centred * lax.rsqrt(variance + 1e-06) * gain + bias

def attend_image(operands):
    query, keyed, valued = operands
    scores = jnp.einsum('qhd,khd->hqk', query, keyed, precision=highest_precision) * HEAD_DIM ** (-0.5)
    probs = jax.nn.softmax(low_back(scores), axis=-1)
    return jnp.einsum('hqk,khd->qhd', reduced_precision(probs), valued, precision=highest_precision)

def forward_pass(image_adapter_index, frozen_params, inputs, query_key_value_adapter_first, query_key_value_adapter_second, projection_adapter_first, projection_adapter_second, up_adapter_first, up_adapter_second, down_adapter_first, down_adapter_second):
    first_norm_gain, first_norm_bias, second_norm_gain, second_norm_bias, query_key_value_weight, attention_output_weight, up_weight, down_weight, up_projection_bias, down_projection_bias = frozen_params
    images = inputs.shape[0]
    first_norm = reduced_precision(layer_norm(inputs, first_norm_gain, first_norm_bias))
    query_key_value_middle = jnp.einsum('obl,holm->hobm', first_norm, query_key_value_adapter_first[:, image_adapter_index], precision=highest_precision)
    projected_output = jnp.einsum('isd,djf->jisf', first_norm, query_key_value_weight, precision=highest_precision)
    projected_output = projected_output + jnp.einsum('klty,klye->klte', query_key_value_middle, query_key_value_adapter_second[:, image_adapter_index], precision=highest_precision)
    projected_output = reduced_precision(low_back(projected_output))
    shaped = projected_output.reshape(3, images, SEQ, HEADS, HEAD_DIM)
    mixed_heads = lax.map(jax.checkpoint(attend_image), (shaped[0], shaped[1], shaped[2]))
    mixed_heads = reduced_precision(low_back(mixed_heads.reshape(images, SEQ, MODEL_WIDTH)))
    projection_adapter_middle = jnp.einsum('lby,lyg->lbg', mixed_heads, projection_adapter_first[image_adapter_index], precision=highest_precision)
    attention_branch = jnp.einsum('ise,de->isd', mixed_heads, attention_output_weight, precision=highest_precision)
    attention_branch = attention_branch + jnp.einsum('cmt,ctf->cmf', projection_adapter_middle, projection_adapter_second[image_adapter_index], precision=highest_precision)
    hidden = inputs + low_back(attention_branch)
    second_norm = reduced_precision(layer_norm(hidden, second_norm_gain, second_norm_bias))
    up_adapter_middle = reduced_precision(jnp.einsum('ego,eoh->egh', second_norm, up_adapter_first[image_adapter_index], precision=highest_precision))
    residual_before = jnp.einsum('isd,df->isf', second_norm, up_weight, precision=highest_precision) + up_projection_bias
    residual_before = residual_before + jnp.einsum('cbd,cdp->cbp', up_adapter_middle, up_adapter_second[image_adapter_index], precision=highest_precision)
    activated_hidden = reduced_precision(jax.nn.gelu(low_back(residual_before), approximate=True))
    down_adapter_middle = jnp.einsum('pco,pqo->pcq', activated_hidden, down_adapter_first[image_adapter_index], precision=highest_precision)
    feedforward_output = jnp.einsum('isf,df->isd', activated_hidden, down_weight, precision=highest_precision) + down_projection_bias
    feedforward_output = feedforward_output + jnp.einsum('cmt,ctf->cmf', down_adapter_middle, down_adapter_second[image_adapter_index], precision=highest_precision)
    return hidden + low_back(feedforward_output)

def reference(inputs, cotangent, image_adapter_index, first_norm_gain, first_norm_bias, second_norm_gain, second_norm_bias, query_key_value_weight, attention_output_weight, up_weight, down_weight, up_projection_bias, down_projection_bias, query_key_value_adapter_first, query_key_value_adapter_second, projection_adapter_first, projection_adapter_second, up_adapter_first, up_adapter_second, down_adapter_first, down_adapter_second):
    frozen_params = tuple((item.astype(jnp.float32) for item in (first_norm_gain, first_norm_bias, second_norm_gain, second_norm_bias, query_key_value_weight, attention_output_weight, up_weight, down_weight, up_projection_bias, down_projection_bias)))

    def run_layer(layer_input, qa, qb, pa, pb, ua, ub, da, db):
        return forward_pass(image_adapter_index, frozen_params, layer_input, qa, qb, pa, pb, ua, ub, da, db)
    layer_output, backward_function = jax.vjp(run_layer, inputs.astype(jnp.float32), query_key_value_adapter_first.astype(jnp.float32), query_key_value_adapter_second.astype(jnp.float32), projection_adapter_first.astype(jnp.float32), projection_adapter_second.astype(jnp.float32), up_adapter_first.astype(jnp.float32), up_adapter_second.astype(jnp.float32), down_adapter_first.astype(jnp.float32), down_adapter_second.astype(jnp.float32))
    grads = backward_function(cotangent.astype(jnp.float32))
    return (layer_output, grads[0], grads[1], grads[2], grads[3], grads[4], grads[5], grads[6], grads[7], grads[8])
```

```python
import functools
import jax
import jax.numpy as jnp
from jax import lax
from jax.experimental import pallas as pl
from jax.experimental.pallas import tpu as pltpu
from jax.sharding import PartitionSpec as P

HEAD_DIM = 72
norm_eps = 1e-06
f32 = jnp.float32
bf16 = jnp.bfloat16
MESH = pl.DeviceIdType.MESH


def bits_of(n):
    return n.bit_length() - 1


class Comm:
    def __init__(self, send, recv):
        self.send, self.recv, self.n = send, recv, 0

    def new(self):
        self.n += 1
        return self.n - 1

    def copy(self, i, src, dst, **where):
        return pltpu.make_async_remote_copy(
            src_ref=src,
            dst_ref=dst,
            send_sem=self.send.at[i],
            recv_sem=self.recv.at[i],
            device_id=where,
            device_id_type=MESH,
        )


def enter(axes_sizes, f, h, z):
    fn, hn, tn = axes_sizes
    barrier = pltpu.get_barrier_semaphore()
    count = 0
    for b in range(bits_of(fn)):
        pl.semaphore_signal(
            barrier, 1, device_id={"fsdp": f ^ (1 << b)}, device_id_type=MESH
        )
        count += 1
    pl.semaphore_signal(barrier, 1, device_id={"heads": 1 - h}, device_id_type=MESH)
    count += 1
    for d in range(1, tn):
        pl.semaphore_signal(
            barrier, 1, device_id={"tensor": lax.rem(z + d, tn)}, device_id_type=MESH
        )
        count += 1
    pl.semaphore_wait(barrier, count)


class Rows:
    def __init__(self, comm, fn, f, slot, rows, own):
        self.comm, self.fn, self.f, self.slot, self.own = comm, fn, f, slot, own
        self.nb = bits_of(fn)
        half = rows // 2 // 8 * 8
        self.parts = ((0, half, list(range(self.nb))), (half, rows - half, list(range(self.nb))[::-1]))
        self.first = [comm.new() for _ in range(self.nb)]
        self.later = {}
        for p, (_, _, order) in enumerate(self.parts):
            for m in range(1, fn):
                last = max(order.index(b) for b in range(self.nb) if m >> b & 1)
                for b in order[last + 1 :]:
                    self.later[p, m, b] = comm.new()
        self.sent = []

    def part(self, origin, p):
        start, size, _ = self.parts[p]
        return self.slot(origin, pl.ds(start, size))

    def begin(self):
        for b in range(self.nb):
            c = self.comm.copy(
                self.first[b], self.own, self.slot(self.f, None), fsdp=self.f ^ (1 << b)
            )
            c.start()
            self.sent.append(c)

    def _arrived(self, m, p):
        order = self.parts[p][2]
        last = max(order.index(b) for b in range(self.nb) if m >> b & 1)
        b = order[last]
        src = m ^ (1 << b)
        if src == 0:
            return None
        where = self.part(self.f ^ m, p)
        return self.comm.copy(self.later[p, src, b], where, where, fsdp=self.f ^ (1 << b))

    def forward(self, m):
        if m & (m - 1) == 0:
            b = bits_of(m)
            where = self.slot(self.f ^ m, None)
            self.comm.copy(self.first[b], where, where, fsdp=self.f ^ m).wait_recv()
        for p, (_, _, order) in enumerate(self.parts):
            if m & (m - 1):
                self._arrived(m, p).wait_recv()
            last = max(order.index(b) for b in range(self.nb) if m >> b & 1)
            for b in order[last + 1 :]:
                where = self.part(self.f ^ m, p)
                c = self.comm.copy(self.later[p, m, b], where, where, fsdp=self.f ^ (1 << b))
                c.start()
                self.sent.append(c)

    def masks(self):
        return sorted(range(1, self.fn), key=lambda m: (bin(m).count("1"), m))

    def drain(self):
        for c in self.sent:
            c.wait_send()


def gather_kernel(
    sizes, wq, wo, w2, aq, ap, au, ad, oq, oo, o2, oaq, oap, oau, oad, send, recv, local
):
    fn, hn, tn = sizes
    f, h, z = lax.axis_index("fsdp"), lax.axis_index("heads"), lax.axis_index("tensor")
    rows = wo.shape[0]
    comm = Comm(send, recv)
    nothing = slice(None)

    def rs(r):
        return nothing if r is None else r

    jobq = Rows(comm, fn, f, lambda o, r: oq.at[:, h, o, rs(r)], rows, wq)
    jobo = Rows(comm, fn, f, lambda o, r: oo.at[h, o, rs(r)], rows, wo)
    blocks = [lax.rem(z + s, tn) for s in range(tn)]
    job2 = []
    for s in range(tn):
        own = w2.at[h] if s == 0 else o2.at[h, blocks[s], f]
        job2.append(
            Rows(comm, fn, f, lambda o, r, s=s: o2.at[h, blocks[s], o, rs(r)], rows, own)
        )
    up = [comm.new() for _ in range(tn - 1)]
    down = [comm.new() for _ in range(tn - 1)]
    sib = [comm.new() for _ in range(4 + tn)]
    small = [comm.new() for _ in range(2 * (tn - 1))]
    enter(sizes, f, h, z)

    locals_ = [
        pltpu.make_async_copy(wq, oq.at[:, h, f], local.at[0]),
        pltpu.make_async_copy(wo, oo.at[h, f], local.at[1]),
        pltpu.make_async_copy(w2.at[h], o2.at[h, z, f], local.at[2]),
        pltpu.make_async_copy(aq.at[h], oaq.at[h], local.at[3]),
        pltpu.make_async_copy(ap.at[h], oap.at[h], local.at[4]),
        pltpu.make_async_copy(au.at[z], oau.at[z], local.at[5]),
        pltpu.make_async_copy(ad.at[z], oad.at[z], local.at[6]),
    ]
    jobq.begin()
    jobo.begin()

    def zcopy(sem, k, block, src, to):
        return comm.copy(sem, src, o2.at[h, block, f], tensor=to)

    @pl.when(z < tn - 1)
    def _():
        zcopy(up[0], 0, z, w2.at[h], z + 1).start()

    @pl.when(z > 0)
    def _():
        zcopy(down[0], 0, z, w2.at[h], z - 1).start()

    for c in locals_:
        c.start()
    other = []
    for d in range(1, tn):
        p = lax.rem(z + d, tn)
        other.append(comm.copy(small[2 * d - 2], au.at[p], oau.at[z], tensor=p))
        other.append(comm.copy(small[2 * d - 1], ad.at[p], oad.at[z], tensor=p))
    other.append(comm.copy(sib[0], aq.at[1 - h], oaq.at[h], heads=1 - h))
    other.append(comm.copy(sib[1], ap.at[1 - h], oap.at[h], heads=1 - h))
    for c in other:
        c.start()
    job2[0].begin()
    for m in jobq.masks():
        jobq.forward(m)
        jobo.forward(m)
    locals_[0].wait()
    locals_[1].wait()
    sibq = comm.copy(sib[2], oq.at[:, h], oq.at[:, h], heads=1 - h)
    sibq.start()
    sibo = comm.copy(sib[3], oo.at[h], oo.at[h], heads=1 - h)
    sibo.start()
    for k in range(tn - 1):
        @pl.when(z - 1 - k >= 0)
        def _():
            b = o2.at[h, z - 1 - k, f]
            comm.copy(up[k], b, b, tensor=z - 1).wait_recv()
            if k + 1 < tn - 1:

                @pl.when(z < tn - 1)
                def _():
                    zcopy(up[k + 1], k, z - 1 - k, b, z + 1).start()

        @pl.when(z + 1 + k < tn)
        def _():
            b = o2.at[h, z + 1 + k, f]
            comm.copy(down[k], b, b, tensor=z + 1).wait_recv()
            if k + 1 < tn - 1:

                @pl.when(z > 0)
                def _():
                    zcopy(down[k + 1], k, z + 1 + k, b, z - 1).start()

    for s in range(1, tn):
        job2[s].begin()
    locals_[2].wait()
    sib2 = []
    for s in range(tn):
        for m in job2[s].masks():
            job2[s].forward(m)
        c = comm.copy(
            sib[4 + s], o2.at[h, blocks[s]], o2.at[h, blocks[s]], heads=1 - h
        )
        c.start()
        sib2.append(c)
    for c in locals_[3:]:
        c.wait()
    for k in range(tn - 1):

        @pl.when((z < tn - 1) & (z - k >= 0))
        def _():
            zcopy(up[k], k, z, w2.at[h], z + 1).wait_send()

        @pl.when((z > 0) & (z + k < tn))
        def _():
            zcopy(down[k], k, z, w2.at[h], z - 1).wait_send()

    for j in [jobq, jobo] + job2:
        j.drain()
    for c in other + [sibq, sibo] + sib2:
        c.wait_send()
    for d in range(1, tn):
        p = lax.rem(z + tn - d, tn)
        comm.copy(small[2 * d - 2], au.at[p], oau.at[p], tensor=p).wait_recv()
        comm.copy(small[2 * d - 1], ad.at[p], oad.at[p], tensor=p).wait_recv()
    comm.copy(sib[0], aq.at[h], oaq.at[1 - h], heads=1 - h).wait_recv()
    comm.copy(sib[1], ap.at[h], oap.at[1 - h], heads=1 - h).wait_recv()
    comm.copy(sib[2], oq.at[:, h], oq.at[:, 1 - h], heads=1 - h).wait_recv()
    comm.copy(sib[3], oo.at[h], oo.at[1 - h], heads=1 - h).wait_recv()
    for s in range(tn):
        b = o2.at[1 - h, blocks[s]]
        comm.copy(sib[4 + s], b, b, heads=1 - h).wait_recv()


def gather(sizes, wq, wo, w2, aq, ap, au, ad):
    fn, hn, tn = sizes
    rows, half = wo.shape
    units = w2.shape[-1]
    any_ = pl.BlockSpec(memory_space=pl.ANY)
    rank = au.shape[1]
    nb = bits_of(fn)
    nsem = (2 + tn) * (nb + 2 * (fn - 1 - nb)) + 4 * (tn - 1) + 4 + tn
    return pl.pallas_call(
        functools.partial(gather_kernel, sizes),
        out_shape=(
            jax.ShapeDtypeStruct((3, hn, fn, rows, half), bf16),
            jax.ShapeDtypeStruct((hn, fn, rows, half), bf16),
            jax.ShapeDtypeStruct((2, tn, fn, rows, units), bf16),
            jax.ShapeDtypeStruct((hn, 3, rank, half), bf16),
            jax.ShapeDtypeStruct((hn, rank, half), bf16),
            jax.ShapeDtypeStruct((tn, rank, units), bf16),
            jax.ShapeDtypeStruct((tn, rank, units), bf16),
        ),
        in_specs=[any_] * 7,
        out_specs=(any_,) * 7,
        scratch_shapes=[
            pltpu.SemaphoreType.DMA((nsem,)),
            pltpu.SemaphoreType.DMA((nsem,)),
            pltpu.SemaphoreType.DMA((7,)),
        ],
        compiler_params=pltpu.CompilerParams(collective_id=0, has_side_effects=True),
        name="gather_weights",
    )(wq, wo, w2, aq, ap, au, ad)


def normalize(values, gain, bias):
    mean = jnp.mean(values, axis=-1, keepdims=True)
    centred = values - mean
    inverse = lax.rsqrt(jnp.mean(centred * centred, axis=-1, keepdims=True) + norm_eps)
    unit = centred * inverse
    return (unit * gain + bias, unit, inverse)


def normalize_back(grad_norm, unit, inverse, gain):
    scaled = grad_norm * gain
    return inverse * (
        scaled
        - jnp.mean(scaled, axis=-1, keepdims=True)
        - unit * jnp.mean(scaled * unit, axis=-1, keepdims=True)
    )


def dot(a, b, dims):
    return lax.dot_general(a, b, (dims, ((), ())), preferred_element_type=f32)


def mm(a, b):
    return dot(a, b, ((1,), (0,)))


def mmt(a, b):
    return dot(a, b, ((1,), (1,)))


def tmm(a, b):
    return dot(a, b, ((0,), (0,)))


def attend_forward(query, keyed, valued):
    scores = jnp.einsum("qhd,khd->hqk", query, keyed, preferred_element_type=f32) * HEAD_DIM ** (-0.5)
    top = jnp.max(scores, axis=-1, keepdims=True)
    weights = jnp.exp(scores - top)
    total = jnp.sum(weights, axis=-1, keepdims=True)
    probs = (weights / total).astype(bf16)
    mixed = jnp.einsum("hqk,khd->qhd", probs, valued, preferred_element_type=f32)
    return mixed.astype(bf16), (top + jnp.log(total))[..., 0]


def attend_back(query, keyed, valued, grad_mixed, log_total):
    scale = HEAD_DIM ** (-0.5)
    scores = jnp.einsum("qhd,khd->hqk", query, keyed, preferred_element_type=f32) * scale
    probs = jnp.exp(scores - log_total[..., None])
    grad_probs = jnp.einsum("qhd,khd->hqk", grad_mixed, valued, preferred_element_type=f32)
    grad_values = jnp.einsum("hqk,qhd->khd", probs.astype(bf16), grad_mixed, preferred_element_type=f32)
    inner = jnp.sum(probs * grad_probs, axis=-1, keepdims=True)
    grad_scores = (probs * (grad_probs - inner)).astype(bf16)
    grad_query = jnp.einsum("hqk,khd->qhd", grad_scores, keyed, preferred_element_type=f32) * scale
    grad_keys = jnp.einsum("hqk,qhd->khd", grad_scores, query, preferred_element_type=f32) * scale
    return grad_query, grad_keys, grad_values


def per_device(
    inputs,
    cotangent,
    image_adapter_index,
    first_norm_gain,
    first_norm_bias,
    second_norm_gain,
    second_norm_bias,
    query_key_value_weight,
    attention_output_weight,
    up_weight,
    down_weight,
    up_projection_bias,
    down_projection_bias,
    query_key_value_adapter_first,
    query_key_value_adapter_second,
    projection_adapter_first,
    projection_adapter_second,
    up_adapter_first,
    up_adapter_second,
    down_adapter_first,
    down_adapter_second,
):
    sizes = tuple(lax.axis_size(a) for a in ("fsdp", "heads", "tensor"))
    fn, hn, tn = sizes
    f, h, z = (lax.axis_index(a) for a in ("fsdp", "heads", "tensor"))
    images, length, width = inputs.shape
    assert images == 1
    heads_n = width // HEAD_DIM
    count = query_key_value_adapter_first.shape[1]
    own = (f * hn + h) * tn + z
    number = image_adapter_index[own]
    pair = image_adapter_index[(f * hn + jnp.arange(hn)) * tn + z]
    line = image_adapter_index[(f * hn + h) * tn + jnp.arange(tn)]
    aq = jnp.swapaxes(query_key_value_adapter_second[:, pair], 0, 1)
    ap = jnp.swapaxes(projection_adapter_first, 1, 2)[pair]
    au, ad = up_adapter_second[line], down_adapter_first[line]
    wq, wo, w2, aq, ap, au, ad = gather(
        sizes,
        jnp.swapaxes(query_key_value_weight, 0, 1),
        attention_output_weight,
        jnp.stack([up_weight, down_weight]),
        aq,
        ap,
        au,
        ad,
    )
    wq = jnp.moveaxis(wq.reshape(3, hn, width, width // hn), 1, 2).reshape(3, width, width)
    wo = jnp.moveaxis(wo.reshape(hn, width, width // hn), 0, 1).reshape(width, width)
    wu, wd = w2[0].reshape(tn, width, -1), w2[1].reshape(tn, width, -1)
    qkv_in = jnp.swapaxes(query_key_value_adapter_first[:, number], 1, 2)
    qkv_out = jnp.moveaxis(aq, 0, 2).reshape(3, -1, width)
    p_in = jnp.moveaxis(ap, 0, 1).reshape(-1, width)
    p_out = projection_adapter_second[number]
    u_in = up_adapter_first[number].T
    d_out = down_adapter_second[number]
    b_up = up_projection_bias
    b_up = lax.all_gather(b_up, "tensor").astype(f32)

    x, g = inputs[0], cotangent[0]
    n1, unit1, inv1 = normalize(x, first_norm_gain, first_norm_bias)
    ln1 = n1.astype(bf16)
    qkv_mid = jnp.stack([mmt(ln1, qkv_in[j]) for j in range(3)]).astype(bf16)
    proj = [(mm(ln1, wq[j]) + mm(qkv_mid[j], qkv_out[j])).astype(bf16) for j in range(3)]
    shaped = [p.reshape(length, heads_n, HEAD_DIM) for p in proj]
    mixed, log_total = attend_forward(*shaped)
    mixed = mixed.reshape(length, width)
    proj_mid = mmt(mixed, p_in).astype(bf16)
    hidden = x + mmt(mixed, wo) + mm(proj_mid, p_out)
    n2, unit2, inv2 = normalize(hidden, second_norm_gain, second_norm_bias)
    ln2 = n2.astype(bf16)
    up_mid = mmt(ln2, u_in).astype(bf16)
    g_mlp = g.astype(bf16)
    g_down_mid = mmt(g_mlp, d_out).astype(bf16)
    out, g_ln2, down_mid, g_up_mid = 0.0, 0.0, 0.0, 0.0
    g_up_out, g_down_in, kept = [], [], []
    for t in range(tn):
        before = mm(ln2, wu[t]) + mm(up_mid, au[t]) + b_up[t]
        act, pull = jax.vjp(lambda v: jax.nn.gelu(v, approximate=True), before)
        act = act.astype(bf16)
        g_act = mm(g_mlp, wd[t]) + mm(g_down_mid, ad[t])
        g_before = pull(g_act)[0].astype(bf16)
        out += mmt(act, wd[t])
        g_ln2 += mmt(g_before, wu[t])
        down_mid += mmt(act, ad[t])
        g_up_mid += mmt(g_before, au[t])
        g_up_out.append(tmm(up_mid, g_before))
        g_down_in.append(tmm(g_down_mid, act))
    down_mid, g_up_mid = down_mid.astype(bf16), g_up_mid.astype(bf16)
    layer_output = hidden + out + mm(down_mid, d_out) + down_projection_bias.astype(f32)
    g_ln2 += mm(g_up_mid, u_in)
    g_hidden = g + normalize_back(g_ln2, unit2, inv2, second_norm_gain)
    g_branch = g_hidden.astype(bf16)
    g_proj_mid = mmt(g_branch, p_out).astype(bf16)
    g_mixed = (mm(g_branch, wo) + mm(g_proj_mid, p_in)).astype(bf16)
    g3 = attend_back(*shaped, g_mixed.reshape(length, heads_n, HEAD_DIM), log_total)
    g_proj = [v.reshape(length, width).astype(bf16) for v in g3]
    g_qkv_mid = [mmt(g_proj[j], qkv_out[j]).astype(bf16) for j in range(3)]
    g_ln1 = sum(mmt(g_proj[j], wq[j]) + mm(g_qkv_mid[j], qkv_in[j]) for j in range(3))
    grad_input = g_hidden + normalize_back(g_ln1, unit1, inv1, first_norm_gain)

    hot = (jnp.arange(count) == number).astype(f32)

    def spread(v):
        return (hot.reshape((count,) + (1,) * v.ndim) * v[None]).astype(bf16)

    everyone = ("fsdp", "heads", "tensor")
    s1 = jnp.concatenate(
        [tmm(g_qkv_mid[j], ln1) for j in range(3)]
        + [tmm(proj_mid, g_branch), tmm(g_up_mid, ln2), tmm(down_mid, g_mlp)]
        + [tmm(qkv_mid[j], g_proj[j]) for j in range(3)]
        + [tmm(g_proj_mid, mixed)]
    )
    s1 = lax.psum(spread(s1), everyone).astype(f32)
    s3 = lax.psum(spread(jnp.stack([jnp.concatenate(g_up_out, 1), jnp.concatenate(g_down_in, 1)])), everyone)
    s3 = s3.astype(f32).reshape(count, 2, -1, tn, wu.shape[-1])[:, :, :, z]
    r = s1.shape[1] // 10

    def rows(i, k=1):
        return s1[:, i * r : (i + k) * r]

    def own_half(v):
        return lax.dynamic_slice_in_dim(v, h * (width // hn), width // hn, axis=-1)

    def three(v):
        return jnp.swapaxes(v.reshape(count, 3, r, -1), 0, 1)

    return (
        layer_output[None],
        grad_input[None],
        jnp.swapaxes(three(rows(0, 3)), 2, 3),
        own_half(three(rows(6, 3))),
        jnp.swapaxes(own_half(rows(9)), 1, 2),
        rows(3),
        jnp.swapaxes(rows(4), 1, 2),
        s3[:, 0],
        s3[:, 1],
        rows(5),
    )

def solution(mesh):
    in_specs = (
        P(("fsdp", "heads", "tensor"), None, None),
        P(("fsdp", "heads", "tensor"), None, None),
        P(),
        P(),
        P(),
        P(),
        P(),
        P("fsdp", None, "heads"),
        P("fsdp", "heads"),
        P("fsdp", "tensor"),
        P("fsdp", "tensor"),
        P("tensor"),
        P(),
        P(),
        P(None, None, None, "heads"),
        P(None, "heads", None),
        P(),
        P(),
        P(None, None, "tensor"),
        P(None, None, "tensor"),
        P(),
    )
    out_specs = (
        P(("fsdp", "heads", "tensor"), None, None),
        P(("fsdp", "heads", "tensor"), None, None),
        P(),
        P(None, None, None, "heads"),
        P(None, "heads", None),
        P(),
        P(),
        P(None, None, "tensor"),
        P(None, None, "tensor"),
        P(),
    )
    return jax.shard_map(
        per_device, mesh=mesh, in_specs=in_specs, out_specs=out_specs, check_vma=False
    )
```

```python
import functools
import jax
import jax.numpy as jnp
from jax import lax
from jax.experimental import pallas as pl
from jax.experimental.pallas import tpu as pltpu
from jax.sharding import PartitionSpec as P

HEAD_DIM = 72
norm_eps = 1e-06
f32 = jnp.float32
bf16 = jnp.bfloat16
MESH = pl.DeviceIdType.MESH


RANK = 16
EXTRA = 32


def padded(n):
    return -(-n // 16) * 16


def row_sums(v):
    return jnp.sum(v, axis=-1, keepdims=True)


class Tokens:
    def __init__(self, hbm, buf, tail, sems, out=False):
        self.length = hbm.shape[0]
        self.buf, self.tail, self.out = buf, tail, out
        self.whole = self.length // 8 * 8
        pairs = [(hbm.at[0 : self.whole, 0, :], buf.at[0 : self.whole, 0 : hbm.shape[-1]])]
        if self.whole < self.length:
            pairs.append((hbm.at[self.whole : self.length, 0, :], tail))
        self.copies = [
            pltpu.make_async_copy(*((b, a) if out else (a, b)), sems.at[i]) for i, (a, b) in enumerate(pairs)
        ]

    def start(self):
        if self.out and self.whole < self.length:
            self.tail[...] = self.buf[self.whole : self.length, 0 : self.tail.shape[-1]]
        for c in self.copies:
            c.start()

    def wait(self):
        for c in self.copies:
            c.wait()
        if not self.out:
            rest = self.buf.shape[0] - self.length
            zeros = jnp.zeros((rest, self.buf.shape[1]), f32)
            if self.whole < self.length:
                zeros = jnp.concatenate([self.tail[...], zeros])
            self.buf[self.whole :, :] = zeros


def tail_shape(length, width):
    return pltpu.VMEM((max(length % 8, 1), width), f32)


def unit_of(v, width):
    mean = row_sums(v) * (1.0 / width)
    centred = v - mean
    inverse = lax.rsqrt(row_sums(centred * centred) * (1.0 / width) + norm_eps)
    return centred * inverse, inverse


def by_rows(n, step, body):
    def one(r, _):
        body(pl.ds(pl.multiple_of(r * step, step), step), r * step)
        return 0

    lax.fori_loop(0, n // step, one, 0)


def real(v, start, length):
    row = lax.broadcasted_iota(jnp.int32, v.shape, 0) + start
    return jnp.where(row < length, v, 0.0)


def normalize_into(dst, src, gain, bias, length):
    n, width = src.shape

    def body(rows, start):
        unit, _ = unit_of(src[rows, :], width)
        dst[rows, 0:width] = real(unit * gain[...] + bias[...], start, length).astype(bf16)

    by_rows(n, 32, body)


def norm_back(grad, v, gain, width):
    unit, inverse = unit_of(v, width)
    e = grad * gain
    return inverse * (e - row_sums(e) * (1.0 / width) - unit * (row_sums(e * unit) * (1.0 / width)))


LANES = 128
SCALE = HEAD_DIM**-0.5
LOG2E = 1.4426950408889634


def nn(a, b):
    return lax.dot_general(a, b, (((1,), (0,)), ((), ())), preferred_element_type=f32)


def nt(a, b):
    return lax.dot_general(a, b, (((1,), (1,)), ((), ())), preferred_element_type=f32)


def tn_(a, b):
    return lax.dot_general(a, b, (((0,), (0,)), ((), ())), preferred_element_type=f32)


def whole(shape):
    return pl.BlockSpec(shape, lambda *_: (0,) * len(shape))


def params(limit=60, **more):
    return pltpu.CompilerParams(vmem_limit_bytes=limit << 20, **more)


def head_window(head, width):
    tile = jnp.minimum(head * HEAD_DIM // LANES, width // LANES - 2)
    return pl.ds(pl.multiple_of(tile * LANES, LANES), 2 * LANES), head * HEAD_DIM - tile * LANES


def only_head(values, start):
    lane = lax.broadcasted_iota(jnp.int32, values.shape, 1)
    return jnp.where((lane >= start) & (lane < start + HEAD_DIM), values, jnp.zeros_like(values))


def own_rows(head):
    return pl.ds(pl.multiple_of(head * HEAD_DIM, 8), HEAD_DIM)


def attend_forward_head(length, head, q_ref, k_ref, vt_ref, sum_ref, log_ref):
    win, start = head_window(head, q_ref.shape[-1])
    q = only_head(q_ref[:, win], start)
    v = vt_ref[own_rows(head), :].astype(bf16)
    s = nt(k_ref[:, win], q)
    key = lax.broadcasted_iota(jnp.int32, s.shape, 0)
    s = jnp.where(key < length, s, -1e30)
    top = jnp.max(s, axis=0, keepdims=True)
    p = jnp.exp2((s - top) * (SCALE * LOG2E))
    total = jnp.sum(p, axis=0, keepdims=True)
    sum_ref[own_rows(head), :] = nn(v, p.astype(bf16)) * (1.0 / total)
    log_ref[pl.ds(head, 1), :] = top * (SCALE * LOG2E) + jnp.log(total) * LOG2E


def attend_back_head(length, head, q_ref, k_ref, v_ref, do_ref, log_ref, kt_ref, dq_ref, dk_ref, dv_ref):
    win, start = head_window(head, q_ref.shape[-1])
    q = only_head(q_ref[:, win], start)
    k = k_ref[:, win]
    do = only_head(do_ref[:, win], start)
    s = nt(k, q)
    key = lax.broadcasted_iota(jnp.int32, s.shape, 0)
    p = jnp.exp2(jnp.where(key < length, s * (SCALE * LOG2E), -1e30) - log_ref[pl.ds(head, 1), :])
    dp = nt(v_ref[:, win], do)
    pd = p * dp
    ds = (pd - p * jnp.sum(pd, axis=0, keepdims=True)).astype(bf16)
    dv_ref[:, win] += nn(p.astype(bf16), do)
    dk_ref[:, win] += nn(ds, q) * SCALE
    dq_ref[own_rows(head), :] = nn(kt_ref[own_rows(head), :].astype(bf16), ds) * SCALE


def transpose_into(dst, src):
    dst[...] = src[...].astype(f32).T.astype(dst.dtype)


def attend_forward_kernel(length, q_ref, k_ref, v_ref, mixed_ref, log_ref, vt_ref, sum_ref):
    head = pl.program_id(0)

    @pl.when(head == 0)
    def _():
        transpose_into(vt_ref, v_ref.at[0])

    attend_forward_head(length, head, q_ref.at[0], k_ref.at[0], vt_ref, sum_ref, log_ref)

    @pl.when(head == pl.num_programs(0) - 1)
    def _():
        transpose_into(mixed_ref, sum_ref)


def attend_forward(length, qkv):
    _, n, width = qkv.shape
    heads = width // HEAD_DIM
    one = lambda j: pl.BlockSpec((1, n, width), lambda h: (j, 0, 0), pipeline_mode=pl.Buffered(1))
    return pl.pallas_call(
        functools.partial(attend_forward_kernel, length),
        grid=(heads,),
        in_specs=[one(0), one(1), one(2)],
        out_specs=(whole((n, width)), whole((heads, n))),
        out_shape=(jax.ShapeDtypeStruct((n, width), bf16), jax.ShapeDtypeStruct((heads, n), f32)),
        scratch_shapes=[pltpu.VMEM((width, n), f32)] * 2,
        compiler_params=params(),
        name="attend_forward",
    )(qkv, qkv, qkv)


def bits_of(n):
    return n.bit_length() - 1


class Comm:
    def __init__(self, send, recv):
        self.send, self.recv, self.n = send, recv, 0

    def new(self):
        self.n += 1
        return self.n - 1

    def copy(self, i, src, dst, **where):
        return pltpu.make_async_remote_copy(
            src_ref=src,
            dst_ref=dst,
            send_sem=self.send.at[i],
            recv_sem=self.recv.at[i],
            device_id=where,
            device_id_type=MESH,
        )


def enter(axes_sizes, f, h, z):
    fn, hn, tn = axes_sizes
    barrier = pltpu.get_barrier_semaphore()
    count = 0
    for b in range(bits_of(fn)):
        pl.semaphore_signal(
            barrier, 1, device_id={"fsdp": f ^ (1 << b)}, device_id_type=MESH
        )
        count += 1
    pl.semaphore_signal(barrier, 1, device_id={"heads": 1 - h}, device_id_type=MESH)
    count += 1
    for d in range(1, tn):
        pl.semaphore_signal(
            barrier, 1, device_id={"tensor": lax.rem(z + d, tn)}, device_id_type=MESH
        )
        count += 1
    pl.semaphore_wait(barrier, count)


class Rows:
    def __init__(self, comm, fn, f, slot, rows, own, align=8):
        self.comm, self.fn, self.f, self.slot, self.own = comm, fn, f, slot, own
        self.nb = bits_of(fn)
        half = rows // 2 // align * align
        self.parts = ((0, half, list(range(self.nb))), (half, rows - half, list(range(self.nb))[::-1]))
        self.first = [comm.new() for _ in range(self.nb)]
        self.later = {}
        for p, (_, _, order) in enumerate(self.parts):
            for m in range(1, fn):
                last = max(order.index(b) for b in range(self.nb) if m >> b & 1)
                for b in order[last + 1 :]:
                    self.later[p, m, b] = comm.new()
        self.sent = []

    def part(self, origin, p):
        start, size, _ = self.parts[p]
        return self.slot(origin, (start, size))

    def begin(self):
        for b in range(self.nb):
            self.send(
                lambda b=b: self.comm.copy(
                    self.first[b], self.own(), self.slot(self.f, None), fsdp=self.f ^ (1 << b)
                )
            )

    def _arrived(self, m, p):
        order = self.parts[p][2]
        last = max(order.index(b) for b in range(self.nb) if m >> b & 1)
        b = order[last]
        src = m ^ (1 << b)
        if src == 0:
            return None
        where = self.part(self.f ^ m, p)
        return self.comm.copy(self.later[p, src, b], where, where, fsdp=self.f ^ (1 << b))

    def forward(self, m):
        if m & (m - 1) == 0:
            b = bits_of(m)
            where = self.slot(self.f ^ m, None)
            self.comm.copy(self.first[b], where, where, fsdp=self.f ^ m).wait_recv()
        for p, (_, _, order) in enumerate(self.parts):
            if m & (m - 1):
                self._arrived(m, p).wait_recv()
            last = max(order.index(b) for b in range(self.nb) if m >> b & 1)
            for b in order[last + 1 :]:

                def onward(p=p, b=b):
                    where = self.part(self.f ^ m, p)
                    return self.comm.copy(self.later[p, m, b], where, where, fsdp=self.f ^ (1 << b))

                self.send(onward)

    def masks(self):
        return sorted(range(1, self.fn), key=lambda m: (bin(m).count("1"), m))

    def leaf(self, m):
        return not any(key[1] == m for key in self.later)

    def forward_all(self):
        for m in self.masks():
            if not self.leaf(m):
                self.forward(m)

    def settle(self):
        for m in self.masks():
            if self.leaf(m):
                self.forward(m)

    def send(self, make):
        make().start()
        self.sent.append(make)

    def drain(self):
        for make in self.sent:
            make().wait_send()


def tree_sems(fn):
    nb = bits_of(fn)
    return nb + 2 * (fn - 1 - nb)


class Bounce:
    def __init__(self, src, buf, dst, sem):
        self.load = pltpu.make_async_copy(src, buf, sem)
        self.save = pltpu.make_async_copy(buf, dst, sem)

    def start(self):
        self.load.start()

    def turn(self):
        self.load.wait()
        self.save.start()

    def wait(self):
        self.save.wait()


class Block:
    def __init__(self, comm, sizes, zw, dst, s, buf, own=None):
        fn, hn, tn = sizes
        f, h, z = lax.axis_index("fsdp"), lax.axis_index("heads"), lax.axis_index("tensor")
        rows = zw.shape[1]
        self.comm, self.dst, self.h, self.buf = comm, dst, h, buf
        t = lax.rem(z + s, tn)

        def slot(o, r):
            start, size = (0, rows) if r is None else r
            return dst.at[h, pl.ds(pl.multiple_of(o * rows + start, 8), size)]

        self.own = lambda: zw.at[t] if own is None else own
        self.slot = lambda: slot(f, None)
        self.job = Rows(comm, fn, f, slot, rows, self.own)
        self.local = comm.new()
        self.core = comm.new()

    def mine(self):
        return Bounce(self.own(), self.buf, self.slot(), self.comm.send.at[self.local])

    def to_core(self, which):
        b = self.dst.at[which]
        return self.comm.copy(self.core, b, b, heads=1 - self.h)

    def begin(self):
        self.job.begin()
        self.mine().start()

    def forward(self):
        self.mine().turn()
        self.job.forward_all()

    def exchange(self):
        self.job.settle()
        self.mine().wait()
        self.to_core(self.h).start()

    def arrive(self):
        self.to_core(1 - self.h).wait_recv()

    def drain(self):
        self.job.drain()
        self.to_core(self.h).wait_send()


def block_sems(fn):
    return tree_sems(fn) + 2


class Weight:
    def __init__(self, comm, fn, f, h, rows, own, dst, extra, own_sem, buf):
        self.comm, self.h, self.dst, self.extra = comm, h, dst, extra
        width = fn * rows
        self.main, self.more = pl.ds(0, width), pl.ds(width, RANK)

        def slot(o, r):
            start, size = (0, rows) if r is None else r
            return dst.at[h, pl.ds(pl.multiple_of(o * rows + start, 8), size)]

        self.job = Rows(comm, fn, f, slot, rows, lambda: own)
        self.core, self.core_extra = comm.new(), comm.new()
        self.mine = lambda: Bounce(own, buf, slot(f, None), own_sem.at[0])
        self.mine_extra = lambda: pltpu.make_async_copy(
            extra.at[h], dst.at[h, self.more], own_sem.at[1]
        )

    def start_extra(self):
        self.mine_extra().start()
        self.to_core_extra().start()

    def to_core_extra(self):
        return self.comm.copy(
            self.core_extra, self.extra.at[1 - self.h], self.dst.at[self.h, self.more], heads=1 - self.h
        )

    def to_core(self, which):
        b = self.dst.at[which, self.main]
        return self.comm.copy(self.core, b, b, heads=1 - self.h)

    def exchange(self):
        self.job.settle()
        self.mine().wait()
        self.to_core(self.h).start()

    def arrive(self):
        self.mine_extra().wait()
        where = self.dst.at[1 - self.h, self.more]
        self.comm.copy(self.core_extra, where, where, heads=1 - self.h).wait_recv()
        self.to_core(1 - self.h).wait_recv()

    def drain(self):
        self.job.drain()
        self.to_core(self.h).wait_send()
        self.to_core_extra().wait_send()


def attention_kernel(
    sizes,
    wq,
    wo,
    w2,
    aq,
    ap,
    a2,
    first_ref,
    out_ref,
    x_ref,
    gain1,
    bias1,
    gain,
    bias,
    up_ref,
    oq,
    oo,
    zw,
    ax,
    ln_out,
    qkv_out,
    qmid_ref,
    mixed_ref,
    log_ref,
    hidden_ref,
    ln2_ref,
    mid_ref,
    got,
    send,
    recv,
    wq_buf,
    wo_buf,
    w_sems,
    own_sems,
    own_q,
    own_o,
    own_z,
    own_b,
    qkv_ref,
    lnx_ref,
    vt_ref,
    sum_ref,
    x_buf,
    x_tail,
    x_sems,
):
    i = pl.program_id(0)
    fn, hn, tn = sizes
    f, h, z = lax.axis_index("fsdp"), lax.axis_index("heads"), lax.axis_index("tensor")
    rows, half = wo.shape
    length = x_ref.shape[0]
    n, width = mixed_ref.shape
    heads = width // HEAD_DIM
    comm = Comm(send, recv)
    qs = [
        Weight(comm, fn, f, h, rows, wq.at[j], oq.at[j], aq.at[j], own_sems.at[j], own_q.at[j])
        for j in range(3)
    ]
    o = Weight(comm, fn, f, h, rows, wo, oo, ap, own_sems.at[3], own_o)
    line = ([comm.new() for _ in range(tn - 1)], [comm.new() for _ in range(tn - 1)])
    small = [comm.new() for _ in range(tn - 1)]
    blocks = [
        Block(comm, sizes, zw, got.at[b], b, own_b.at[b], w2.at[h] if b == 0 else None)
        for b in range(got.shape[0])
    ]
    begin_z, step_z, drain_z = line_copies(comm, tn, z, lambda t: zw.at[t], line, w2.at[h])
    mine_z = lambda: Bounce(w2.at[h], own_z, zw.at[z], own_sems.at[4, 0])
    mine_a = lambda: pltpu.make_async_copy(a2.at[z], ax.at[:, z], own_sems.at[4, 1])
    to_line = lambda d: comm.copy(
        small[d - 1], a2.at[lax.rem(z + d, tn)], ax.at[:, z], tensor=lax.rem(z + d, tn)
    )
    load_x = Tokens(x_ref, x_buf, x_tail, x_sems)
    load_q = lambda j: pltpu.make_async_copy(oq.at[j], wq_buf.at[j], w_sems.at[j])
    load_o = lambda: pltpu.make_async_copy(oo, wo_buf, w_sems.at[3])
    save_ln = lambda: pltpu.make_async_copy(lnx_ref.at[:, pl.ds(0, width)], ln_out, w_sems.at[4])
    save_qkv = lambda: pltpu.make_async_copy(qkv_ref, qkv_out, w_sems.at[5])

    @pl.when(i == 0)
    def _():
        load_x.start()
        for w in qs + [o]:
            w.mine().start()
        mine_z().start()
        enter(sizes, f, h, z)
        qs[0].job.begin()
        qs[1].job.begin()
        begin_z()
        for w in qs + [o]:
            w.start_extra()
        mine_a().start()
        for d in range(1, tn):
            to_line(d).start()
        for w in qs + [o]:
            w.mine().turn()
        mine_z().turn()
        load_x.wait()
        normalize_into(lnx_ref, x_buf, gain1, bias1, length)
        save_ln().start()

    @pl.when(i == 1)
    def _():
        qs[0].job.forward_all()
        qs[2].job.begin()
        qs[1].job.forward_all()
        qs[0].exchange()
        step_z(0, lambda t: None)
        qs[0].arrive()
        load_q(0).start()

    @pl.when(i == 2)
    def _():
        qs[2].job.forward_all()
        o.job.begin()
        qs[1].exchange()
        if tn > 2:
            step_z(1, lambda t: None)
        qs[1].arrive()
        load_q(1).start()
        qs[2].exchange()

    @pl.when(i == 3)
    def _():
        qs[2].arrive()
        load_q(2).start()

    @pl.when((i >= 1) & (i < 4))
    def _():
        j = i - 1
        mid = nt(lnx_ref[:, 0:width], first_ref[j]).astype(bf16)
        qmid_ref[j] = mid
        load_q(j).wait()

        @pl.when(i == 1)
        def _():
            save_ln().wait()

        lnx_ref[:, width:] = mid
        for p in range(hn):
            qkv_ref[j, :, p * half : (p + 1) * half] = nn(lnx_ref[...], wq_buf[j, p]).astype(bf16)

    @pl.when(i == 4)
    def _():
        save_qkv().start()
        o.job.forward_all()
        blocks[0].begin()
        for k in range(2, tn - 1):
            step_z(k, lambda t: None)
        for b in blocks[1:]:
            b.begin()
        transpose_into(vt_ref, qkv_ref.at[2])

    @pl.when(i == 8)
    def _():
        o.exchange()

    @pl.when(i == 11)
    def _():
        o.arrive()
        load_o().start()

    for b in range(got.shape[0]):

        @pl.when(i == 16 + 3 * b)
        def _():
            blocks[b].forward()

    @pl.when((i >= 4) & (i < 4 + heads))
    def _():
        attend_forward_head(length, i - 4, qkv_ref.at[0], qkv_ref.at[1], vt_ref, sum_ref, log_ref)

    @pl.when(i == 4 + heads)
    def _():
        blocks[0].exchange()
        transpose_into(mixed_ref, sum_ref)
        load_o().wait()
        br = sum(nt(mixed_ref[:, p * half : (p + 1) * half], wo_buf[p]) for p in range(hn))
        mid = br[:, width:].astype(bf16)
        mid_ref[...] = mid
        hidden_ref[...] = br[:, :width] + nn(mid, out_ref[...])

    @pl.when(i == 5 + heads)
    def _():
        for b in blocks[1:]:
            b.exchange()

        def body(rows, start):
            v = real(x_buf[rows, :] + hidden_ref[rows, :], start, length)
            hidden_ref[rows, :] = v
            unit, _ = unit_of(v, width)
            ln2_ref[rows, 0:width] = real(unit * gain[...] + bias[...], start, length).astype(bf16)

        by_rows(n, 32, body)
        up_mid = nt(ln2_ref[:, 0:width], up_ref[...])
        lane = lax.broadcasted_iota(jnp.int32, (n, EXTRA - RANK), 1)
        ln2_ref[:, width : width + RANK] = up_mid.astype(bf16)
        ln2_ref[:, width + RANK :] = (lane == 0).astype(bf16)
        save_qkv().wait()
        mine_z().wait()
        mine_a().wait()
        for d in range(1, tn):
            to_line(d).wait_send()
            p = lax.rem(z + tn - d, tn)
            comm.copy(small[d - 1], a2.at[p], ax.at[:, p], tensor=p).wait_recv()
        drain_z()
        for b in blocks:
            b.arrive()
        for w in qs + [o] + blocks:
            w.drain()


def attention(sizes, wq, wo, w2, aq, ap, a2, first, out, x, gain1, bias1, gain, bias, up):
    fn, hn, tn = sizes
    rows, half = wo.shape
    units = w2.shape[-1]
    width = fn * rows
    length = x.shape[0]
    n = padded(length)
    heads = width // HEAD_DIM
    early = min(2, tn)
    any_ = pl.BlockSpec(memory_space=pl.ANY)
    one = lambda s: pl.BlockSpec(s, lambda i: (0,) * len(s), pipeline_mode=pl.Buffered(1))
    shape = jax.ShapeDtypeStruct
    nsem = 4 * (tree_sems(fn) + 2) + 3 * (tn - 1) + early * block_sems(fn)
    hbm = [
        ((3, hn, width + RANK, half), bf16),
        ((hn, width + RANK, half), bf16),
        ((tn, rows, units), bf16),
        ((2, tn, EXTRA, units), bf16),
        ((n, width), bf16),
        ((3, n, width), bf16),
    ]
    outs = [
        ((3, n, RANK), bf16),
        ((n, width), bf16),
        ((heads, n), f32),
        ((n, width), f32),
        ((n, width + EXTRA), bf16),
        ((n, RANK), bf16),
    ]
    vec = one((1, width))
    return pl.pallas_call(
        functools.partial(attention_kernel, sizes),
        grid=(6 + heads,),
        in_specs=[any_] * 6
        + [one(first.shape), one(out.shape), any_, vec, vec, vec, vec, one(up.shape)],
        out_specs=(any_,) * len(hbm) + tuple(one(s) for s, _ in outs) + (any_,),
        out_shape=tuple(shape(*o) for o in hbm + outs) + (shape((early, 2, width, units), bf16),),
        scratch_shapes=[
            pltpu.SemaphoreType.DMA((nsem,)),
            pltpu.SemaphoreType.DMA((nsem,)),
            pltpu.VMEM((3, hn, width + RANK, half), bf16),
            pltpu.VMEM((hn, width + RANK, half), bf16),
            pltpu.SemaphoreType.DMA((6,)),
            pltpu.SemaphoreType.DMA((5, 2)),
            pltpu.VMEM((3, rows, half), bf16),
            pltpu.VMEM((rows, half), bf16),
            pltpu.VMEM((rows, units), bf16),
            pltpu.VMEM((early, rows, units), bf16),
            pltpu.VMEM((3, n, width), bf16),
            pltpu.VMEM((n, width + RANK), bf16),
            pltpu.VMEM((width, n), f32),
            pltpu.VMEM((width, n), f32),
            pltpu.VMEM((n, width), f32),
            tail_shape(length, width),
            pltpu.SemaphoreType.DMA((2,)),
        ],
        compiler_params=params(collective_id=3, has_side_effects=True),
        name="attention",
    )(wq, wo, w2, aq, ap, a2, first, out, x, gain1, bias1, gain, bias, up)


def gelu_both(v, g):
    c, a = 0.7978845608028654, 0.044715
    sq = v * v
    t = jnp.tanh(v * (c + (c * a) * sq))
    half = 0.5 * (1.0 + t)
    slope = half + (0.5 * v) * ((1.0 - t * t) * (c + (3.0 * c * a) * sq))
    return v * half, g * slope


def mlp_half(ln_ref, g_ref, wu_ref, wd_ref, act_ref, gb_ref, out_acc, g_acc, rows, first, between):
    before = nn(ln_ref[rows, :], wu_ref[...])
    g_act = nn(g_ref[rows, :], wd_ref[...])
    act, gb = gelu_both(before, g_act)
    act, gb = act.astype(bf16), gb.astype(bf16)
    act_ref[rows, :] = act
    gb_ref[rows, :] = gb
    between()
    o, g = nt(act, wd_ref[...]), nt(gb, wu_ref[...])

    @pl.when(first)
    def _():
        out_acc[rows, :] = o
        g_acc[rows, :] = g

    @pl.when(jnp.logical_not(first))
    def _():
        out_acc[rows, :] += o
        g_acc[rows, :] += g


def mlp_kernel(
    sizes,
    length,
    plan,
    ln_ref,
    cot_ref,
    hidden_ref,
    early,
    zw,
    ax,
    up_ref,
    down_ref,
    dbias,
    gain,
    y_ref,
    gh_ref,
    g_up_in,
    g_down_out,
    g_units,
    late,
    send,
    recv,
    w_buf,
    w_sems,
    g_buf,
    tail,
    gx,
    act,
    gb,
    out_acc,
    g_acc,
    sem,
    own_buf,
):
    i = pl.program_id(0)
    fn, hn, tn = sizes
    f, h, z = lax.axis_index("fsdp"), lax.axis_index("heads"), lax.axis_index("tensor")
    n, width = hidden_ref.shape
    main = slice(0, width)
    s, half = i // 2, lax.rem(i, 2)
    comm = Comm(send, recv)
    done = early.shape[0]
    blocks = {b: Block(comm, sizes, zw, late.at[b - done], b, own_buf.at[b - done]) for b in range(done, tn)}

    def loads(b):
        slot = b % 2
        src = early.at[b] if b < done else late.at[b - done]
        return [
            pltpu.make_async_copy(src, w_buf.at[slot, :, pl.ds(0, width)], w_sems.at[slot, 0]),
            pltpu.make_async_copy(
                ax.at[:, lax.rem(z + b, tn)], w_buf.at[slot, :, pl.ds(width, EXTRA)], w_sems.at[slot, 1]
            ),
        ]

    @pl.when(i == 0)
    def _():
        c = Tokens(cot_ref, g_buf, tail, sem)
        c.start()
        for b in range(done):
            for w in loads(b):
                w.start()
        enter(sizes, f, h, z)
        if done in blocks:
            blocks[done].begin()
        c.wait()

        def body(rows, start):
            gx[rows, main] = g_buf[rows, :].astype(bf16)

        by_rows(n, 32, body)
        gx[:, width : width + RANK] = nt(gx[:, main], down_ref[...]).astype(bf16)
        gx[:, width + RANK :] = jnp.zeros((n, EXTRA - RANK), bf16)

    def events(steps):
        for at, what in steps:

            @pl.when(i == at)
            def _():
                for b, name in what:
                    if name == "load":
                        if b < tn:
                            if b in blocks:
                                blocks[b].arrive()
                            for w in loads(b):
                                w.start()
                    elif b in blocks:
                        getattr(blocks[b], name)()

    events(plan[0])

    for b in range(tn):

        @pl.when(i == 2 * b)
        def _():
            for w in loads(b):
                w.wait()

    slot = lax.rem(s, 2)
    rows = pl.ds(pl.multiple_of(half * (n // 2), n // 2), n // 2)
    mlp_half(ln_ref, gx, w_buf.at[slot, 0], w_buf.at[slot, 1], act, gb, out_acc, g_acc, rows, s == 0, lambda: events(plan[1]))

    @pl.when(half == 1)
    def _():
        g_units[0, s] = tn_(ln_ref[:, width : width + RANK], gb[...]).astype(bf16)
        g_units[1, s] = tn_(gx[:, width : width + RANK], act[...]).astype(bf16)

    @pl.when(i == pl.num_programs(0) - 1)
    def _():
        down_mid = out_acc[:, width : width + RANK].astype(bf16)
        g_up_mid = g_acc[:, width : width + RANK].astype(bf16)
        g_up_in[...] = tn_(g_up_mid, ln_ref[:, main]).astype(bf16)
        g_down_out[...] = tn_(down_mid, gx[:, main]).astype(bf16)
        out_acc[:, main] += nn(down_mid, down_ref[...])
        g_acc[:, main] += nn(g_up_mid, up_ref[...])

        def body(rows, start):
            v = hidden_ref[rows, :]
            out_acc[rows, main] += v + dbias[...]
            gh_ref[rows, :] = g_buf[rows, :] + real(
                norm_back(g_acc[rows, main], v, gain[...], width), start, length
            )

        by_rows(n, 32, body)
        c = Tokens(y_ref, out_acc, tail, sem, out=True)
        c.start()
        for b in blocks.values():
            b.drain()
        c.wait()


def mlp(sizes, ln, cot, hidden, early, zw, ax, up, down, dbias, gain):
    fn, hn, tn = sizes
    n, width = hidden.shape
    depth = ln.shape[1]
    done, _, _, units = early.shape
    length = cot.shape[0]
    late = max(tn - done, 1)
    plan = (
        (
            (2, ((2, "forward"), (3, "begin"))),
            (3, ((2, "exchange"),)),
            (6, ((3, "load"),)),
        ),
        (
            (3, ((2, "load"),)),
            (4, ((3, "forward"),)),
            (5, ((3, "exchange"),)),
        ),
    )
    any_ = pl.BlockSpec(memory_space=pl.ANY)
    one = lambda s: pl.BlockSpec(s, lambda t: (0,) * len(s), pipeline_mode=pl.Buffered(1))
    shape = jax.ShapeDtypeStruct
    nsem = late * block_sems(fn)
    return pl.pallas_call(
        functools.partial(mlp_kernel, sizes, length, plan),
        grid=(2 * tn,),
        in_specs=[
            one((n, depth)),
            any_,
            one((n, width)),
            any_,
            any_,
            any_,
            one((RANK, width)),
            one((RANK, width)),
            one((1, width)),
            one((1, width)),
        ],
        out_specs=(
            any_,
            one((n, width)),
            one((RANK, width)),
            one((RANK, width)),
            one((2, tn, RANK, units)),
            any_,
        ),
        out_shape=(
            shape((length, 1, width), f32),
            shape((n, width), f32),
            shape((RANK, width), bf16),
            shape((RANK, width), bf16),
            shape((2, tn, RANK, units), bf16),
            shape((late, 2, width, units), bf16),
        ),
        scratch_shapes=[
            pltpu.SemaphoreType.DMA((nsem,)),
            pltpu.SemaphoreType.DMA((nsem,)),
            pltpu.VMEM((2, 2, depth, units), bf16),
            pltpu.SemaphoreType.DMA((2, 2)),
            pltpu.VMEM((n, width), f32),
            tail_shape(length, width),
            pltpu.VMEM((n, depth), bf16),
            pltpu.VMEM((n, units), bf16),
            pltpu.VMEM((n, units), bf16),
            pltpu.VMEM((n, depth), f32),
            pltpu.VMEM((n, depth), f32),
            pltpu.SemaphoreType.DMA((2,)),
            pltpu.VMEM((late,) + zw.shape[1:], bf16),
        ],
        compiler_params=params(collective_id=4, has_side_effects=True),
        name="mlp",
    )(ln, cot, hidden, early, zw, ax, up, down, dbias, gain)


def branch_back_kernel(gh_ref, w_ref, out_ref, mixed_ref, mid_ref, g_up_in, g_down_out, gm_ref, grads, gx):
    n, width = gh_ref.shape
    half = w_ref.shape[-1]

    def body(rows, start):
        gx[rows, 0:width] = gh_ref[rows, :].astype(bf16)

    by_rows(n, 32, body)
    g_mid = nt(gx[:, 0:width], out_ref[...]).astype(bf16)
    gx[:, width:] = g_mid
    grads[...] = jnp.zeros_like(grads)
    grads[0:RANK, :] = tn_(mid_ref[...], gx[:, 0:width]).astype(bf16)
    grads[RANK : 2 * RANK, :] = g_up_in[...]
    grads[2 * RANK : 3 * RANK, :] = g_down_out[...]
    grads[3 * RANK : 4 * RANK, :] = tn_(g_mid, mixed_ref[...]).astype(bf16)
    for p in range(w_ref.shape[0]):
        gm_ref[:, p * half : (p + 1) * half] = nn(gx[...], w_ref[p]).astype(bf16)


def branch_back(rows, gh, w, out, mixed, mid, g_up_in, g_down_out):
    n, width = gh.shape
    return pl.pallas_call(
        branch_back_kernel,
        out_shape=(
            jax.ShapeDtypeStruct((n, width), bf16),
            jax.ShapeDtypeStruct((rows, width), bf16),
        ),
        scratch_shapes=[pltpu.VMEM((n, width + RANK), bf16)],
        compiler_params=params(),
        name="branch_back",
    )(gh, w, out, mixed, mid, g_up_in, g_down_out)


def add_by_adapter(pick, parts):
    width = parts.shape[-1]
    return nn(pick[...], parts.astype(f32).reshape(-1, width).astype(bf16))


def picks(adapters, count, rows):
    hot = adapters[None, :] == jnp.arange(count)[:, None]
    same = jnp.eye(rows, dtype=bool)
    return (hot[:, None, :, None] & same[None, :, None, :]).reshape(count * rows, -1).astype(bf16)


def line_copies(comm, tn, z, here, sems, own=None):
    up, down = sems

    def send(sem, block, to, src=None):
        return comm.copy(sem, here(block) if src is None else src, here(block), tensor=to)

    def begin():
        @pl.when(z < tn - 1)
        def _():
            send(up[0], z, z + 1, own).start()

        @pl.when(z > 0)
        def _():
            send(down[0], z, z - 1, own).start()

    def step(k, then):
        @pl.when(z - 1 - k >= 0)
        def _():
            b = z - 1 - k
            comm.copy(up[k], here(b), here(b), tensor=z - 1).wait_recv()
            if k + 1 < tn - 1:

                @pl.when(z < tn - 1)
                def _():
                    send(up[k + 1], b, z + 1).start()

            then(b)

        @pl.when(z + 1 + k < tn)
        def _():
            b = z + 1 + k
            comm.copy(down[k], here(b), here(b), tensor=z + 1).wait_recv()
            if k + 1 < tn - 1:

                @pl.when(z > 0)
                def _():
                    send(down[k + 1], b, z - 1).start()

            then(b)

    def drain():
        for k in range(tn - 1):

            @pl.when((z < tn - 1) & (z - k >= 0))
            def _():
                send(up[k], z, z + 1).wait_send()

            @pl.when((z > 0) & (z + k < tn))
            def _():
                send(down[k], z, z - 1).wait_send()

    return begin, step, drain


class Reduce:
    def __init__(self, sizes, count, comm, hot, local, a, out, ra, dense, b=None, out_b=None, rb=None, hot_b=None):
        fn, hn, tn = sizes
        f, h, z = lax.axis_index("fsdp"), lax.axis_index("heads"), lax.axis_index("tensor")
        self.fn, self.hn, self.tn, self.f, self.h, self.z = fn, hn, tn, f, h, z
        self.count, self.comm, self.hot, self.hot_b, self.local = count, comm, hot, hot_b, local
        self.a, self.out, self.ra, self.dense, self.b, self.out_b, self.rb = a, out, ra, dense, b, out_b, rb
        self.piece = ra.shape[1]
        self.s_first = [comm.new() for _ in range(fn - 1)]
        s_line = ([comm.new() for _ in range(tn - 1)], [comm.new() for _ in range(tn - 1)])
        self.s_core = [comm.new() for _ in range(tn)]
        self.s_last = comm.new()
        self.sent = []
        per = count // hn
        self.mine, self.theirs = pl.ds(h * per, per), pl.ds((1 - h) * per, per)

        def slot(o, r):
            start, size = (0, per) if r is None else r
            return out.at[o, pl.ds(h * per + start, size)]

        self.spread = Rows(comm, fn, f, slot, per, lambda: dense.at[self.mine], align=1)
        self.begin, self.line, self.drain_line = line_copies(
            comm, tn, z, lambda t: self.group(t, h), s_line
        )
        if b is not None:
            self.s_first_b = [comm.new() for _ in range(tn - 1)]
            self.s_core_b = comm.new()

            def slot_b(o, r):
                start, size = (0, tn) if r is None else r
                return rb.at[h, o, pl.ds(start, size)]

            self.spread_b = Rows(comm, fn, f, slot_b, tn, lambda: rb.at[h, f], align=1)

    def group(self, z, h):
        return self.ra.at[pl.ds((z * self.hn + h) * self.fn, self.fn)]

    def one(self, z, h, f):
        return self.ra.at[(z * self.hn + h) * self.fn + f]

    def rows(self, f):
        return self.a.at[pl.ds(pl.multiple_of(f * self.piece, 8), self.piece)]

    def send(self, make):
        make().start()
        self.sent.append(make)

    def own(self):
        copies = [pltpu.make_async_copy(self.rows(self.f), self.one(self.z, self.h, self.f), self.local.at[0])]
        if self.b is not None:
            copies.append(
                pltpu.make_async_copy(self.b.at[:, 0], self.rb.at[self.h, self.f, self.z], self.local.at[1])
            )
        return copies

    def start(self):
        f, h, z, comm = self.f, self.h, self.z, self.comm
        for m in range(1, self.fn):
            self.send(
                lambda m=m: comm.copy(
                    self.s_first[m - 1], self.rows(f ^ m), self.one(z, h, f), fsdp=f ^ m
                )
            )
        if self.b is not None:
            for d in range(1, self.tn):
                self.send(
                    lambda d=d: comm.copy(
                        self.s_first_b[d - 1],
                        self.b.at[:, d],
                        self.rb.at[h, f, z],
                        tensor=lax.rem(z + d, self.tn),
                    )
                )
        for c in self.own():
            c.start()

    def second(self):
        f, h, z, comm = self.f, self.h, self.z, self.comm
        for c in self.own():
            c.wait()
        for m in range(1, self.fn):
            b = self.one(z, h, f ^ m)
            comm.copy(self.s_first[m - 1], b, b, fsdp=f ^ m).wait_recv()
        self.begin()
        self.to_core(z).start()
        if self.b is not None:
            for d in range(1, self.tn):
                p = lax.rem(z + self.tn - d, self.tn)
                b = self.rb.at[h, f, p]
                comm.copy(self.s_first_b[d - 1], b, b, tensor=p).wait_recv()
            self.spread_b.begin()

    def to_core(self, block):
        b = self.group(block, self.h)
        return pltpu.make_async_remote_copy(
            src_ref=b,
            dst_ref=b,
            send_sem=self.comm.send.at[self.s_core[0] + block],
            recv_sem=self.comm.recv.at[self.s_core[0] + block],
            device_id={"heads": 1 - self.h},
            device_id_type=MESH,
        )

    def line_step(self, k):
        if k < self.tn - 1:
            self.line(k, lambda b: self.to_core(b).start())

    def forward_b(self):
        self.spread_b.forward_all()

    def exchange_b(self):
        self.spread_b.settle()
        b = self.rb.at[self.h]
        self.send(lambda: self.comm.copy(self.s_core_b, b, b, heads=1 - self.h))

    def fourth(self):
        h = self.h
        for k in range(self.tn):
            b = self.group(k, 1 - h)
            self.comm.copy(self.s_core[k], b, b, heads=1 - h).wait_recv()
        total = add_by_adapter(self.hot, self.ra[...])
        self.dense[...] = total.reshape(self.dense.shape).astype(bf16)
        self.spread.begin()
        self.last().start()

    def last(self):
        return pltpu.make_async_copy(
            self.dense.at[self.mine], self.out.at[self.f, self.mine], self.local.at[0]
        )

    def fifth(self):
        b = self.rb.at[1 - self.h]
        self.comm.copy(self.s_core_b, b, b, heads=1 - self.h).wait_recv()
        for k in range(2):
            total = add_by_adapter(self.hot_b, self.rb[:, :, :, k, :, :])
            self.out_b[k] = total.reshape(self.out_b.shape[1:])

    def sixth(self):
        self.spread.forward_all()

    def seventh(self):
        self.last().wait()
        self.spread.settle()
        b = self.out.at[:, self.mine]
        self.send(lambda: self.comm.copy(self.s_last, b, b, heads=1 - self.h))

    def finish(self):
        h = self.h
        b = self.out.at[:, self.theirs]
        self.comm.copy(self.s_last, b, b, heads=1 - h).wait_recv()
        for make in self.sent:
            make().wait_send()
        self.drain_line()
        self.spread.drain()
        if self.b is not None:
            self.spread_b.drain()
        for k in range(self.tn):
            self.to_core(k).wait_send()


def reduce_sems(sizes, both):
    fn, hn, tn = sizes
    nb = bits_of(fn)
    tree = nb + 2 * (fn - 1 - nb)
    n = fn - 1 + 2 * (tn - 1) + tn + 1 + tree
    return n + (tn - 1 + 1 + tree if both else 0)


def enter_reduce(sizes, f, h, z):
    fn, hn, tn = sizes
    barrier = pltpu.get_barrier_semaphore()
    for m in range(1, fn):
        pl.semaphore_signal(barrier, 1, device_id={"fsdp": f ^ m}, device_id_type=MESH)
    pl.semaphore_signal(barrier, 1, device_id={"heads": 1 - h}, device_id_type=MESH)
    for d in range(1, tn):
        pl.semaphore_signal(barrier, 1, device_id={"tensor": lax.rem(z + d, tn)}, device_id_type=MESH)
    pl.semaphore_wait(barrier, fn - 1 + 1 + tn - 1)


def piece_rows(rows, fn):
    return -(-rows // (8 * fn)) * 8


def reduce_shapes(sizes, count, width, piece, units, both):
    fn, hn, tn = sizes
    n = fn * hn * tn
    shapes = [
        pltpu.SemaphoreType.DMA((reduce_sems(sizes, both),)),
        pltpu.SemaphoreType.DMA((reduce_sems(sizes, both),)),
        pltpu.SemaphoreType.DMA((2,)),
        pltpu.VMEM((n, piece, width), bf16),
        pltpu.VMEM((count, piece, width), bf16),
    ]
    if both:
        shapes.append(pltpu.VMEM((hn, fn, tn, 2, RANK, units), bf16))
    return shapes


def attend_back_kernel(
    sizes, length, count, plan, hot, hot_b, q_ref, k_ref, v_ref, do_ref, log_ref, a, b, out_ref, sums, sums_b, send, recv, local, ra, dense, rb, kt_ref, dq_ref, dk_ref, dv_ref
):
    head = pl.program_id(0)
    job = Reduce(sizes, count, Comm(send, recv), hot, local, a, sums, ra, dense, b, sums_b, rb, hot_b)

    @pl.when(head == 0)
    def _():
        enter_reduce(sizes, job.f, job.h, job.z)
        job.start()
        transpose_into(kt_ref, k_ref.at[0])
        for r in (dk_ref, dv_ref):
            r[...] = jnp.zeros_like(r)

    for at, what in plan:

        @pl.when(head == at)
        def _():
            for name, *more in what:
                getattr(job, name)(*more)

    attend_back_head(
        length, head, q_ref.at[0], k_ref.at[0], v_ref.at[0], do_ref, log_ref, kt_ref, dq_ref, dk_ref, dv_ref
    )

    @pl.when(head == pl.num_programs(0) - 1)
    def _():
        transpose_into(out_ref.at[0], dq_ref)
        out_ref[1] = dk_ref[...].astype(bf16)
        out_ref[2] = dv_ref[...].astype(bf16)
        job.finish()


def attend_back(sizes, length, count, hot, hot_b, qkv, do, log, a, b):
    fn, hn, tn = sizes
    _, n, width = qkv.shape
    heads = width // HEAD_DIM
    units = b.shape[-1]
    piece = a.shape[0] // fn
    plan = (
        (2, (("second",),)),
        (5, (("line_step", 0),)),
        (7, (("line_step", 1), ("forward_b",))),
        (9, (("line_step", 2), ("exchange_b",))),
        (11, (("fourth",),)),
        (12, (("fifth",),)),
        (13, (("sixth",),)),
        (15, (("seventh",),)),
    )
    any_ = pl.BlockSpec(memory_space=pl.ANY)
    one = lambda j: pl.BlockSpec((1, n, width), lambda h: (j, 0, 0), pipeline_mode=pl.Buffered(1))
    return pl.pallas_call(
        functools.partial(attend_back_kernel, sizes, length, count, plan),
        grid=(heads,),
        in_specs=[
            whole(hot.shape),
            whole(hot_b.shape),
            one(0),
            one(1),
            one(2),
            whole((n, width)),
            whole((heads, n)),
            any_,
            any_,
        ],
        out_specs=(whole((3, n, width)), any_, whole((2, count, RANK, units))),
        out_shape=(
            jax.ShapeDtypeStruct((3, n, width), bf16),
            jax.ShapeDtypeStruct((fn, count, piece, width), bf16),
            jax.ShapeDtypeStruct((2, count, RANK, units), f32),
        ),
        scratch_shapes=reduce_shapes(sizes, count, width, piece, units, True)
        + [pltpu.VMEM((width, n), f32)] * 2
        + [pltpu.VMEM((n, width), f32)] * 2,
        compiler_params=params(collective_id=1, has_side_effects=True),
        name="attend_back",
    )(hot, hot_b, qkv, qkv, qkv, do, log, a, b)


def project_back_kernel(
    sizes,
    count,
    hot,
    g_ref,
    w_any,
    first_ref,
    mid_ref,
    ln_ref,
    gh_any,
    x_ref,
    gain,
    gi_ref,
    sums,
    a,
    send,
    recv,
    local,
    ra,
    dense,
    w_buf,
    gh_buf,
    w_sems,
    x_buf,
    tail,
    acc,
    grads,
    g_mid,
    sem,
):
    i = pl.program_id(0)
    length = x_ref.shape[0]
    n, width = ln_ref.shape
    half = w_buf.shape[-1]
    parts = w_buf.shape[1]
    load = Tokens(x_ref, x_buf, tail, sem)
    job = Reduce(sizes, count, Comm(send, recv), hot, local, a, sums, ra, dense)

    def load_w(j):
        return pltpu.make_async_copy(w_any.at[j], w_buf.at[j], w_sems.at[j])

    load_gh = pltpu.make_async_copy(gh_any, gh_buf, w_sems.at[3])
    save = pltpu.make_async_copy(grads, a, w_sems.at[4])

    @pl.when(i == 0)
    def _():
        for j in range(3):
            load_w(j).start()
        load.start()
        load_gh.start()
        enter_reduce(sizes, job.f, job.h, job.z)
        if grads.shape[0] > 6 * RANK:
            grads[6 * RANK :, :] = jnp.zeros((grads.shape[0] - 6 * RANK, width), bf16)
        for j in range(3):
            load_w(j).wait()
            m = sum(
                nt(g_ref[j, :, p * half : (p + 1) * half], w_buf[j, p, pl.ds(width, RANK), :])
                for p in range(parts)
            ).astype(bf16)
            g_mid[j] = m
            grads[(3 + j) * RANK : (4 + j) * RANK, :] = tn_(mid_ref[j], g_ref[j]).astype(bf16)
        mids = jnp.concatenate([g_mid[j].astype(f32).T for j in range(3)]).astype(bf16)
        grads[0 : 3 * RANK, :] = nn(mids, ln_ref[...]).astype(bf16)
        save.start()
        save.wait()
        job.start()

    @pl.when(i == 2)
    def _():
        job.second()

    @pl.when(i == 3)
    def _():
        job.line_step(0)

    @pl.when((i > 0) & (i < 4))
    def _():
        j = i - 1
        r = nn(g_mid[j], first_ref[j])
        for p in range(parts):
            r = r + nt(g_ref[j, :, p * half : (p + 1) * half], w_buf[j, p, pl.ds(0, width), :])

        @pl.when(i == 1)
        def _():
            acc[...] = r

        @pl.when(i > 1)
        def _():
            acc[...] += r

    @pl.when(i == 4)
    def _():
        job.line_step(1)
        load.wait()
        load_gh.wait()

        def body(rows, start):
            v = x_buf[rows, :]
            acc[rows, :] = gh_buf[rows, :] + norm_back(acc[rows, :], v, gain[...], width)

        by_rows(n, 32, body)
        c = Tokens(gi_ref, acc, tail, sem, out=True)
        c.start()
        for k in range(2, sizes[2] - 1):
            job.line_step(k)
        job.fourth()
        job.sixth()
        job.seventh()
        job.finish()
        c.wait()


def project_back(sizes, count, hot, g, w, first, mid, ln, gh, x, gain):
    fn, hn, tn = sizes
    n, width = ln.shape
    length = x.shape[0]
    piece = piece_rows(6 * RANK, fn)
    any_ = pl.BlockSpec(memory_space=pl.ANY)
    one = lambda s: pl.BlockSpec(s, lambda t: (0,) * len(s), pipeline_mode=pl.Buffered(1))
    shape = jax.ShapeDtypeStruct
    return pl.pallas_call(
        functools.partial(project_back_kernel, sizes, count),
        grid=(5,),
        in_specs=[
            one(hot.shape),
            one(g.shape),
            any_,
            one(first.shape),
            one(mid.shape),
            one((n, width)),
            any_,
            any_,
            one((1, width)),
        ],
        out_specs=(any_, any_, any_),
        out_shape=(
            shape((length, 1, width), f32),
            shape((fn, count, piece, width), bf16),
            shape((fn * piece, width), bf16),
        ),
        scratch_shapes=reduce_shapes(sizes, count, width, piece, 0, False)
        + [
            pltpu.VMEM(w.shape, bf16),
            pltpu.VMEM((n, width), f32),
            pltpu.SemaphoreType.DMA((5,)),
            pltpu.VMEM((n, width), f32),
            tail_shape(length, width),
            pltpu.VMEM((n, width), f32),
            pltpu.VMEM((fn * piece, width), bf16),
            pltpu.VMEM(mid.shape, bf16),
            pltpu.SemaphoreType.DMA((2,)),
        ],
        compiler_params=params(collective_id=2, has_side_effects=True),
        name="qkv_back",
    )(hot, g, w, first, mid, ln, gh, x, gain)


def per_device(
    inputs,
    cotangent,
    image_adapter_index,
    first_norm_gain,
    first_norm_bias,
    second_norm_gain,
    second_norm_bias,
    query_key_value_weight,
    attention_output_weight,
    up_weight,
    down_weight,
    up_projection_bias,
    down_projection_bias,
    query_key_value_adapter_first,
    query_key_value_adapter_second,
    projection_adapter_first,
    projection_adapter_second,
    up_adapter_first,
    up_adapter_second,
    down_adapter_first,
    down_adapter_second,
):
    sizes = tuple(lax.axis_size(a) for a in ("fsdp", "heads", "tensor"))
    fn, hn, tn = sizes
    f, h, z = (lax.axis_index(a) for a in ("fsdp", "heads", "tensor"))
    images, length, width = inputs.shape
    assert images == 1
    count = query_key_value_adapter_first.shape[1]
    units = up_weight.shape[-1]
    number = image_adapter_index[(f * hn + h) * tn + z]
    pair = image_adapter_index[(f * hn + jnp.arange(hn)) * tn + z]
    line = image_adapter_index[(f * hn + h) * tn + jnp.arange(tn)]
    aq = query_key_value_adapter_second[:, pair]
    ap = jnp.swapaxes(projection_adapter_first, 1, 2)[pair]
    more = jnp.zeros((tn, EXTRA - RANK, units), bf16)
    au = jnp.concatenate([up_adapter_second[line], more.at[:, 0].set(up_projection_bias)], 1)
    ad = jnp.concatenate([down_adapter_first[line], more], 1)
    x, cot = jnp.swapaxes(inputs, 0, 1), jnp.swapaxes(cotangent, 0, 1)
    row = lambda v: v.astype(f32)[None]
    gain1, gain2 = row(first_norm_gain), row(second_norm_gain)
    qkv_in = jnp.swapaxes(query_key_value_adapter_first, 2, 3)[:, number]
    u_in = jnp.swapaxes(up_adapter_first, 1, 2)[number]
    p_out, d_out = projection_adapter_second[number], down_adapter_second[number]
    wq, wo, zw, ax, ln1, qkv, qkv_mid, mixed, log, hidden, ln2, proj_mid, early = attention(
        sizes,
        jnp.swapaxes(query_key_value_weight, 0, 1),
        attention_output_weight,
        jnp.stack([up_weight, down_weight]),
        aq,
        ap,
        jnp.stack([au, ad], 1),
        qkv_in,
        p_out,
        x,
        gain1,
        row(first_norm_bias),
        gain2,
        row(second_norm_bias),
        u_in,
    )
    y, g_hidden, g_up_in, g_down_out, g_units, _ = mlp(
        sizes, ln2, cot, hidden, early, zw, ax, u_in, d_out, row(down_projection_bias), gain2
    )
    g_mixed, grads = branch_back(
        piece_rows(4 * RANK, fn) * fn, g_hidden, wo, p_out, mixed, proj_mid, g_up_in, g_down_out
    )
    by_place = image_adapter_index.reshape(fn, hn, tn)
    order = jnp.transpose(by_place, (2, 1, 0)).reshape(-1)
    order_b = jnp.transpose(by_place, (1, 0, 2)).reshape(-1)
    pick = picks(order, count, piece_rows(4 * RANK, fn))
    pick_b = picks(order_b, count, RANK)
    g_qkv, first, second = attend_back(sizes, length, count, pick, pick_b, qkv, g_mixed, log, grads, g_units)
    g_x, last, _ = project_back(sizes, count, picks(order, count, piece_rows(6 * RANK, fn)), g_qkv, wq, qkv_in, qkv_mid, ln1, g_hidden, x, gain1)

    def whole_rows(v, rows):
        return jnp.moveaxis(v, 0, 1).reshape(count, -1, width)[:, :rows]

    first, last = whole_rows(first, 4 * RANK), whole_rows(last, 6 * RANK)

    def rows(v, i, k=1):
        return v[:, i * RANK : (i + k) * RANK].astype(f32)

    def own_half(v):
        return lax.dynamic_slice_in_dim(v, h * (width // hn), width // hn, axis=-1)

    def three(v):
        return jnp.swapaxes(v.reshape(count, 3, RANK, -1), 0, 1)

    return (
        jnp.swapaxes(y, 0, 1),
        jnp.swapaxes(g_x, 0, 1),
        jnp.swapaxes(three(rows(last, 0, 3)), 2, 3),
        own_half(three(rows(last, 3, 3))),
        jnp.swapaxes(own_half(rows(first, 3)), 1, 2),
        rows(first, 0),
        jnp.swapaxes(rows(first, 1), 1, 2),
        second[0],
        second[1],
        rows(first, 2),
    )


def solution(mesh):
    in_specs = (
        P(("fsdp", "heads", "tensor"), None, None),
        P(("fsdp", "heads", "tensor"), None, None),
        P(),
        P(),
        P(),
        P(),
        P(),
        P("fsdp", None, "heads"),
        P("fsdp", "heads"),
        P("fsdp", "tensor"),
        P("fsdp", "tensor"),
        P("tensor"),
        P(),
        P(),
        P(None, None, None, "heads"),
        P(None, "heads", None),
        P(),
        P(),
        P(None, None, "tensor"),
        P(None, None, "tensor"),
        P(),
    )
    out_specs = (
        P(("fsdp", "heads", "tensor"), None, None),
        P(("fsdp", "heads", "tensor"), None, None),
        P(),
        P(None, None, None, "heads"),
        P(None, "heads", None),
        P(),
        P(),
        P(None, None, "tensor"),
        P(None, None, "tensor"),
        P(),
    )
    return jax.shard_map(
        per_device, mesh=mesh, in_specs=in_specs, out_specs=out_specs, check_vma=False
    )
```

```python
import functools
import jax
import jax.numpy as jnp
from jax import lax
from jax.experimental import pallas as pl
from jax.experimental.pallas import tpu as pltpu
from jax.sharding import PartitionSpec as P

HEAD_DIM = 72
norm_eps = 1e-06
f32 = jnp.float32
bf16 = jnp.bfloat16
MESH = pl.DeviceIdType.MESH


RANK = 16
EXTRA = 32


def padded(n):
    return -(-n // 16) * 16


def row_sums(v):
    return jnp.sum(v, axis=-1, keepdims=True)


class Tokens:
    def __init__(self, hbm, buf, tail, sems, out=False):
        self.length = hbm.shape[0]
        self.buf, self.tail, self.out = buf, tail, out
        self.whole = self.length // 8 * 8
        pairs = [(hbm.at[0 : self.whole, 0, :], buf.at[0 : self.whole, 0 : hbm.shape[-1]])]
        if self.whole < self.length:
            pairs.append((hbm.at[self.whole : self.length, 0, :], tail))
        self.copies = [
            pltpu.make_async_copy(*((b, a) if out else (a, b)), sems.at[i]) for i, (a, b) in enumerate(pairs)
        ]

    def start(self):
        if self.out and self.whole < self.length:
            self.tail[...] = self.buf[self.whole : self.length, 0 : self.tail.shape[-1]]
        for c in self.copies:
            c.start()

    def wait(self):
        for c in self.copies:
            c.wait()
        if not self.out:
            rest = self.buf.shape[0] - self.length
            zeros = jnp.zeros((rest, self.buf.shape[1]), f32)
            if self.whole < self.length:
                zeros = jnp.concatenate([self.tail[...], zeros])
            self.buf[self.whole :, :] = zeros


def tail_shape(length, width):
    return pltpu.VMEM((max(length % 8, 1), width), f32)


def unit_of(v, width):
    mean = row_sums(v) * (1.0 / width)
    centred = v - mean
    inverse = lax.rsqrt(row_sums(centred * centred) * (1.0 / width) + norm_eps)
    return centred * inverse, inverse


def by_rows(n, step, body):
    def one(r, _):
        body(pl.ds(pl.multiple_of(r * step, step), step), r * step)
        return 0

    lax.fori_loop(0, n // step, one, 0)


def real(v, start, length):
    row = lax.broadcasted_iota(jnp.int32, v.shape, 0) + start
    return jnp.where(row < length, v, 0.0)


def normalize_into(dst, src, gain, bias, length):
    n, width = src.shape

    def body(rows, start):
        unit, _ = unit_of(src[rows, :], width)
        dst[rows, 0:width] = real(unit * gain[...] + bias[...], start, length).astype(bf16)

    by_rows(n, 32, body)


def norm_back(grad, v, gain, width):
    unit, inverse = unit_of(v, width)
    e = grad * gain
    return inverse * (e - row_sums(e) * (1.0 / width) - unit * (row_sums(e * unit) * (1.0 / width)))


LANES = 128
SCALE = HEAD_DIM**-0.5
LOG2E = 1.4426950408889634


def nn(a, b):
    return lax.dot_general(a, b, (((1,), (0,)), ((), ())), preferred_element_type=f32)


def nt(a, b):
    return lax.dot_general(a, b, (((1,), (1,)), ((), ())), preferred_element_type=f32)


def tn_(a, b):
    return lax.dot_general(a, b, (((0,), (0,)), ((), ())), preferred_element_type=f32)


def whole(shape):
    return pl.BlockSpec(shape, lambda *_: (0,) * len(shape))


def params(limit=60, **more):
    return pltpu.CompilerParams(vmem_limit_bytes=limit << 20, **more)


def head_window(head, width):
    tile = jnp.minimum(head * HEAD_DIM // LANES, width // LANES - 2)
    return pl.ds(pl.multiple_of(tile * LANES, LANES), 2 * LANES), head * HEAD_DIM - tile * LANES


def only_head(values, start):
    lane = lax.broadcasted_iota(jnp.int32, values.shape, 1)
    return jnp.where((lane >= start) & (lane < start + HEAD_DIM), values, jnp.zeros_like(values))


def own_rows(head):
    return pl.ds(pl.multiple_of(head * HEAD_DIM, 8), HEAD_DIM)


def attend_forward_head(length, head, q_ref, k_ref, vt_ref, sum_ref, log_ref):
    win, start = head_window(head, q_ref.shape[-1])
    q = only_head(q_ref[:, win], start)
    v = vt_ref[own_rows(head), :].astype(bf16)
    s = nt(k_ref[:, win], q)
    key = lax.broadcasted_iota(jnp.int32, s.shape, 0)
    s = jnp.where(key < length, s, -1e30)
    top = jnp.max(s, axis=0, keepdims=True)
    p = jnp.exp2((s - top) * (SCALE * LOG2E))
    total = jnp.sum(p, axis=0, keepdims=True)
    sum_ref[own_rows(head), :] = nn(v, p.astype(bf16)) * (1.0 / total)
    log_ref[pl.ds(head, 1), :] = top * (SCALE * LOG2E) + jnp.log(total) * LOG2E


def attend_back_head(length, head, q_ref, k_ref, v_ref, do_ref, log_ref, kt_ref, dq_ref, dk_ref, dv_ref):
    win, start = head_window(head, q_ref.shape[-1])
    q = only_head(q_ref[:, win], start)
    k = k_ref[:, win]
    do = only_head(do_ref[:, win], start)
    s = nt(k, q)
    key = lax.broadcasted_iota(jnp.int32, s.shape, 0)
    p = jnp.exp2(jnp.where(key < length, s * (SCALE * LOG2E), -1e30) - log_ref[pl.ds(head, 1), :])
    dp = nt(v_ref[:, win], do)
    pd = p * dp
    ds = (pd - p * jnp.sum(pd, axis=0, keepdims=True)).astype(bf16)
    dv_ref[:, win] += nn(p.astype(bf16), do)
    dk_ref[:, win] += nn(ds, q) * SCALE
    dq_ref[own_rows(head), :] = nn(kt_ref[own_rows(head), :].astype(bf16), ds) * SCALE


def columns(width, body):
    def one(c, _):
        body(pl.ds(pl.multiple_of(c * LANES, LANES), LANES))
        return 0

    lax.fori_loop(0, width // LANES, one, 0)


def to_rows(dst, src):
    def body(at):
        dst[at, :] = src[:, at].astype(f32).T.astype(dst.dtype)

    columns(src.shape[1], body)


def to_lanes(dst, src):
    def body(at):
        dst[:, at] = src[at, :].T.astype(dst.dtype)

    columns(src.shape[0], body)


def bits_of(n):
    return n.bit_length() - 1


class Comm:
    def __init__(self, send, recv):
        self.send, self.recv, self.n = send, recv, 0

    def new(self):
        self.n += 1
        return self.n - 1

    def copy(self, i, src, dst, **where):
        return pltpu.make_async_remote_copy(
            src_ref=src,
            dst_ref=dst,
            send_sem=self.send.at[i],
            recv_sem=self.recv.at[i],
            device_id=where,
            device_id_type=MESH,
        )


def enter(axes_sizes, f, h, z):
    fn, hn, tn = axes_sizes
    barrier = pltpu.get_barrier_semaphore()
    count = 0
    for b in range(bits_of(fn)):
        pl.semaphore_signal(
            barrier, 1, device_id={"fsdp": f ^ (1 << b)}, device_id_type=MESH
        )
        count += 1
    pl.semaphore_signal(barrier, 1, device_id={"heads": 1 - h}, device_id_type=MESH)
    count += 1
    for d in range(1, tn):
        pl.semaphore_signal(
            barrier, 1, device_id={"tensor": lax.rem(z + d, tn)}, device_id_type=MESH
        )
        count += 1
    pl.semaphore_wait(barrier, count)


class Rows:
    def __init__(self, comm, fn, f, slot, rows, own, align=8):
        self.comm, self.fn, self.f, self.slot, self.own = comm, fn, f, slot, own
        self.nb = bits_of(fn)
        half = rows // 2 // align * align
        self.parts = ((0, half, list(range(self.nb))), (half, rows - half, list(range(self.nb))[::-1]))
        self.first = [comm.new() for _ in range(self.nb)]
        self.later = {}
        for p, (_, _, order) in enumerate(self.parts):
            for m in range(1, fn):
                last = max(order.index(b) for b in range(self.nb) if m >> b & 1)
                for b in order[last + 1 :]:
                    self.later[p, m, b] = comm.new()
        self.sent = []

    def part(self, origin, p):
        start, size, _ = self.parts[p]
        return self.slot(origin, (start, size))

    def begin(self):
        for b in range(self.nb):
            self.send(
                lambda b=b: self.comm.copy(
                    self.first[b], self.own(), self.slot(self.f, None), fsdp=self.f ^ (1 << b)
                )
            )

    def _arrived(self, m, p):
        order = self.parts[p][2]
        last = max(order.index(b) for b in range(self.nb) if m >> b & 1)
        b = order[last]
        src = m ^ (1 << b)
        if src == 0:
            return None
        where = self.part(self.f ^ m, p)
        return self.comm.copy(self.later[p, src, b], where, where, fsdp=self.f ^ (1 << b))

    def forward(self, m):
        if m & (m - 1) == 0:
            b = bits_of(m)
            where = self.slot(self.f ^ m, None)
            self.comm.copy(self.first[b], where, where, fsdp=self.f ^ m).wait_recv()
        for p, (_, _, order) in enumerate(self.parts):
            if m & (m - 1):
                self._arrived(m, p).wait_recv()
            last = max(order.index(b) for b in range(self.nb) if m >> b & 1)
            for b in order[last + 1 :]:

                def onward(p=p, b=b):
                    where = self.part(self.f ^ m, p)
                    return self.comm.copy(self.later[p, m, b], where, where, fsdp=self.f ^ (1 << b))

                self.send(onward)

    def masks(self):
        return sorted(range(1, self.fn), key=lambda m: (bin(m).count("1"), m))

    def leaf(self, m):
        return not any(key[1] == m for key in self.later)

    def forward_all(self):
        for m in self.masks():
            if not self.leaf(m):
                self.forward(m)

    def settle(self):
        for m in self.masks():
            if self.leaf(m):
                self.forward(m)

    def send(self, make):
        make().start()
        self.sent.append(make)

    def drain(self):
        for make in self.sent:
            make().wait_send()


def tree_sems(fn):
    nb = bits_of(fn)
    return nb + 2 * (fn - 1 - nb)


class Bounce:
    def __init__(self, src, buf, dst, sem):
        self.load = pltpu.make_async_copy(src, buf, sem)
        self.save = pltpu.make_async_copy(buf, dst, sem)

    def start(self):
        self.load.start()

    def turn(self):
        self.load.wait()
        self.save.start()

    def wait(self):
        self.save.wait()


class Block:
    def __init__(self, comm, sizes, zw, dst, s, buf, own=None):
        fn, hn, tn = sizes
        f, h, z = lax.axis_index("fsdp"), lax.axis_index("heads"), lax.axis_index("tensor")
        rows = zw.shape[1]
        self.comm, self.dst, self.h, self.buf = comm, dst, h, buf
        t = lax.rem(z + s, tn)

        def slot(o, r):
            start, size = (0, rows) if r is None else r
            return dst.at[h, pl.ds(pl.multiple_of(o * rows + start, 8), size)]

        self.own = lambda: zw.at[t] if own is None else own
        self.slot = lambda: slot(f, None)
        self.job = Rows(comm, fn, f, slot, rows, self.own)
        self.local = comm.new()
        self.core = comm.new()

    def mine(self):
        return Bounce(self.own(), self.buf, self.slot(), self.comm.send.at[self.local])

    def to_core(self, which):
        b = self.dst.at[which]
        return self.comm.copy(self.core, b, b, heads=1 - self.h)

    def begin(self):
        self.job.begin()
        self.mine().start()

    def forward(self):
        self.mine().turn()
        self.job.forward_all()

    def exchange(self):
        self.job.settle()
        self.mine().wait()
        self.to_core(self.h).start()

    def arrive(self):
        self.to_core(1 - self.h).wait_recv()

    def drain(self):
        self.job.drain()
        self.to_core(self.h).wait_send()


def block_sems(fn):
    return tree_sems(fn) + 2


class Weight:
    def __init__(self, comm, fn, f, h, rows, own, dst, extra, own_sem, buf):
        self.comm, self.h, self.dst, self.extra = comm, h, dst, extra
        width = fn * rows
        self.main, self.more = pl.ds(0, width), pl.ds(width, RANK)

        def slot(o, r):
            start, size = (0, rows) if r is None else r
            return dst.at[h, pl.ds(pl.multiple_of(o * rows + start, 8), size)]

        self.job = Rows(comm, fn, f, slot, rows, lambda: own)
        self.core, self.core_extra = comm.new(), comm.new()
        self.mine = lambda: Bounce(own, buf, slot(f, None), own_sem.at[0])
        self.mine_extra = lambda: pltpu.make_async_copy(
            extra.at[h], dst.at[h, self.more], own_sem.at[1]
        )

    def start_extra(self):
        self.mine_extra().start()
        self.to_core_extra().start()

    def to_core_extra(self):
        return self.comm.copy(
            self.core_extra, self.extra.at[1 - self.h], self.dst.at[self.h, self.more], heads=1 - self.h
        )

    def to_core(self, which):
        b = self.dst.at[which, self.main]
        return self.comm.copy(self.core, b, b, heads=1 - self.h)

    def exchange(self):
        self.job.settle()
        self.mine().wait()
        self.to_core(self.h).start()

    def arrive(self):
        self.mine_extra().wait()
        where = self.dst.at[1 - self.h, self.more]
        self.comm.copy(self.core_extra, where, where, heads=1 - self.h).wait_recv()
        self.to_core(1 - self.h).wait_recv()

    def drain(self):
        self.job.drain()
        self.to_core(self.h).wait_send()
        self.to_core_extra().wait_send()


def attention_kernel(
    sizes,
    wq,
    wo,
    wu,
    wd,
    bq,
    bp,
    bu,
    bd,
    ub,
    index,
    first_ref,
    out_ref,
    x_ref,
    vectors,
    up_ref,
    oq,
    oo,
    zw,
    ax,
    ln_out,
    qkv_out,
    qmid_ref,
    mixed_ref,
    log_ref,
    hidden_ref,
    ln2_ref,
    mid_ref,
    got,
    send,
    recv,
    wq_buf,
    wo_buf,
    w_sems,
    own_sems,
    own_q,
    own_o,
    own_z,
    own_b,
    aq,
    ap,
    a2,
    qkv_ref,
    lnx_ref,
    vt_ref,
    sum_ref,
    x_buf,
    x_tail,
    x_sems,
):
    i = pl.program_id(0)
    fn, hn, tn = sizes
    f, h, z = lax.axis_index("fsdp"), lax.axis_index("heads"), lax.axis_index("tensor")
    rows, half = wo.shape
    length = x_ref.shape[0]
    n, width = mixed_ref.shape
    number = index[(f * hn + h) * tn + z]
    gain1, bias1, gain, bias = (vectors.at[k : k + 1] for k in range(4))
    heads = width // HEAD_DIM
    comm = Comm(send, recv)
    qs = [
        Weight(comm, fn, f, h, rows, wq.at[j], oq.at[j], aq.at[j], own_sems.at[j], own_q.at[j])
        for j in range(3)
    ]
    o = Weight(comm, fn, f, h, rows, wo, oo, ap, own_sems.at[3], own_o)
    line = ([comm.new() for _ in range(tn - 1)], [comm.new() for _ in range(tn - 1)])
    small = [comm.new() for _ in range(tn - 1)]
    blocks = [
        Block(comm, sizes, zw, got.at[b], b, own_b.at[b], own_z if b == 0 else None)
        for b in range(got.shape[0])
    ]
    begin_z, step_z, drain_z = line_copies(comm, tn, z, lambda t: zw.at[t], line, own_z)
    mine_z = [Bounce(w, own_z, zw.at[z], own_sems.at[4, 0]) for w in (wu, wd)]
    mine_a = lambda: pltpu.make_async_copy(a2.at[z], ax.at[:, z], own_sems.at[4, 1])
    to_line = lambda d: comm.copy(
        small[d - 1], a2.at[lax.rem(z + d, tn)], ax.at[:, z], tensor=lax.rem(z + d, tn)
    )
    load_x = Tokens(x_ref, x_buf, x_tail, x_sems)
    load_q = lambda j: pltpu.make_async_copy(oq.at[j], wq_buf.at[j], w_sems.at[j])
    load_o = lambda: pltpu.make_async_copy(oo, wo_buf, w_sems.at[3])
    save_ln = lambda: pltpu.make_async_copy(lnx_ref.at[:, pl.ds(0, width)], ln_out, w_sems.at[4])
    save_qkv = lambda: pltpu.make_async_copy(qkv_ref, qkv_out, w_sems.at[5])

    @pl.when(i == 0)
    def _():
        load_x.start()
        for w in qs + [o]:
            w.mine().start()
        for p in range(2):

            @pl.when(h == p)
            def _():
                mine_z[p].start()

        for p in range(hn):
            k = index[(f * hn + p) * tn + z]
            for j in range(3):
                aq[j, p] = bq[j, k]
            ap[p] = bp[k]
        for t in range(tn):
            k = index[(f * hn + h) * tn + t]
            a2[t, 0, 0:RANK] = bu[k]
            a2[t, 1, 0:RANK] = bd[k]
            a2[t, 0, RANK:] = ub[...]
            a2[t, 1, RANK:] = jnp.zeros_like(ub)
        enter(sizes, f, h, z)
        qs[0].job.begin()
        qs[1].job.begin()
        mine_z[0].turn()
        begin_z()
        for w in qs + [o]:
            w.start_extra()
        mine_a().start()
        for d in range(1, tn):
            to_line(d).start()
        for w in qs + [o]:
            w.mine().turn()
        load_x.wait()
        normalize_into(lnx_ref, x_buf, gain1, bias1, length)
        save_ln().start()

    @pl.when(i == 1)
    def _():
        qs[0].job.forward_all()
        qs[2].job.begin()
        qs[1].job.forward_all()
        qs[0].exchange()
        step_z(0, lambda t: None)
        qs[0].arrive()
        load_q(0).start()

    @pl.when(i == 2)
    def _():
        qs[2].job.forward_all()
        o.job.begin()
        qs[1].exchange()
        if tn > 2:
            step_z(1, lambda t: None)
        qs[1].arrive()
        load_q(1).start()
        qs[2].exchange()

    @pl.when(i == 3)
    def _():
        qs[2].arrive()
        load_q(2).start()

    @pl.when((i >= 1) & (i < 4))
    def _():
        j = i - 1
        mid = nt(lnx_ref[:, 0:width], first_ref[j, number]).astype(bf16)
        qmid_ref[j] = mid
        load_q(j).wait()

        @pl.when(i == 1)
        def _():
            save_ln().wait()

        lnx_ref[:, width:] = mid
        for p in range(hn):
            qkv_ref[j, :, p * half : (p + 1) * half] = nn(lnx_ref[...], wq_buf[j, p]).astype(bf16)

    @pl.when(i == 4)
    def _():
        save_qkv().start()
        o.job.forward_all()
        blocks[0].begin()
        for k in range(2, tn - 1):
            step_z(k, lambda t: None)
        for b in blocks[1:]:
            b.begin()
        to_rows(vt_ref, qkv_ref.at[2])

    @pl.when(i == 8)
    def _():
        o.exchange()

    @pl.when(i == 11)
    def _():
        o.arrive()
        load_o().start()

    for b in range(got.shape[0]):

        @pl.when(i == 16 + 3 * b)
        def _():
            blocks[b].forward()

    @pl.when((i >= 4) & (i < 4 + heads))
    def _():
        attend_forward_head(length, i - 4, qkv_ref.at[0], qkv_ref.at[1], vt_ref, sum_ref, log_ref)

    @pl.when(i == 4 + heads)
    def _():
        blocks[0].exchange()
        to_lanes(mixed_ref, sum_ref)
        load_o().wait()
        br = sum(nt(mixed_ref[:, p * half : (p + 1) * half], wo_buf[p]) for p in range(hn))
        mid = br[:, width:].astype(bf16)
        mid_ref[...] = mid
        hidden_ref[...] = br[:, :width] + nn(mid, out_ref[number])

    @pl.when(i == 5 + heads)
    def _():
        for b in blocks[1:]:
            b.exchange()

        def body(rows, start):
            v = real(x_buf[rows, :] + hidden_ref[rows, :], start, length)
            hidden_ref[rows, :] = v
            unit, _ = unit_of(v, width)
            ln2_ref[rows, 0:width] = real(unit * gain[...] + bias[...], start, length).astype(bf16)

        by_rows(n, 32, body)
        up_mid = nt(ln2_ref[:, 0:width], up_ref[number])
        lane = lax.broadcasted_iota(jnp.int32, (n, EXTRA - RANK), 1)
        ln2_ref[:, width : width + RANK] = up_mid.astype(bf16)
        ln2_ref[:, width + RANK :] = (lane == 0).astype(bf16)
        save_qkv().wait()
        mine_z[0].wait()
        mine_a().wait()
        for d in range(1, tn):
            to_line(d).wait_send()
            p = lax.rem(z + tn - d, tn)
            comm.copy(small[d - 1], a2.at[p], ax.at[:, p], tensor=p).wait_recv()
        drain_z()
        for b in blocks:
            b.arrive()
        for w in qs + [o] + blocks:
            w.drain()


def attention(sizes, wq, wo, wu, wd, bq, bp, bu, bd, ub, index, first, out, x, vectors, up):
    fn, hn, tn = sizes
    rows, half = wo.shape
    units = wu.shape[-1]
    width = fn * rows
    length = x.shape[0]
    n = padded(length)
    heads = width // HEAD_DIM
    early = min(2, tn)
    any_ = pl.BlockSpec(memory_space=pl.ANY)
    one = lambda s: pl.BlockSpec(s, lambda i: (0,) * len(s), pipeline_mode=pl.Buffered(1))
    shape = jax.ShapeDtypeStruct
    nsem = 4 * (tree_sems(fn) + 2) + 3 * (tn - 1) + early * block_sems(fn)
    hbm = [
        ((3, hn, width + RANK, half), bf16),
        ((hn, width + RANK, half), bf16),
        ((tn, rows, units), bf16),
        ((2, tn, EXTRA, units), bf16),
        ((n, width), bf16),
        ((3, n, width), bf16),
    ]
    outs = [
        ((3, n, RANK), bf16),
        ((n, width), bf16),
        ((heads, n), f32),
        ((n, width), f32),
        ((n, width + EXTRA), bf16),
        ((n, RANK), bf16),
    ]
    return pl.pallas_call(
        functools.partial(attention_kernel, sizes),
        grid=(6 + heads,),
        in_specs=[any_] * 4
        + [one(v.shape) for v in (bq, bp, bu, bd, ub)]
        + [pl.BlockSpec(memory_space=pltpu.SMEM)]
        + [one(first.shape), one(out.shape), any_, one(vectors.shape), one(up.shape)],
        out_specs=(any_,) * len(hbm) + tuple(one(s) for s, _ in outs) + (any_,),
        out_shape=tuple(shape(*o) for o in hbm + outs) + (shape((early, 2, width, units), bf16),),
        scratch_shapes=[
            pltpu.SemaphoreType.DMA((nsem,)),
            pltpu.SemaphoreType.DMA((nsem,)),
            pltpu.VMEM((3, hn, width + RANK, half), bf16),
            pltpu.VMEM((hn, width + RANK, half), bf16),
            pltpu.SemaphoreType.DMA((6,)),
            pltpu.SemaphoreType.DMA((5, 2)),
            pltpu.VMEM((3, rows, half), bf16),
            pltpu.VMEM((rows, half), bf16),
            pltpu.VMEM((rows, units), bf16),
            pltpu.VMEM((early, rows, units), bf16),
            pltpu.VMEM((3, hn, RANK, half), bf16),
            pltpu.VMEM((hn, RANK, half), bf16),
            pltpu.VMEM((tn, 2, EXTRA, units), bf16),
            pltpu.VMEM((3, n, width), bf16),
            pltpu.VMEM((n, width + RANK), bf16),
            pltpu.VMEM((width, n), f32),
            pltpu.VMEM((width, n), f32),
            pltpu.VMEM((n, width), f32),
            tail_shape(length, width),
            pltpu.SemaphoreType.DMA((2,)),
        ],
        compiler_params=params(collective_id=3, has_side_effects=True),
        name="attention",
    )(wq, wo, wu, wd, bq, bp, bu, bd, ub, index, first, out, x, vectors, up)


def gelu_both(v, g):
    c, a = 0.7978845608028654, 0.044715
    sq = v * v
    t = jnp.tanh(v * (c + (c * a) * sq))
    half = 0.5 * (1.0 + t)
    slope = half + (0.5 * v) * ((1.0 - t * t) * (c + (3.0 * c * a) * sq))
    return v * half, g * slope


def mlp_half(ln_ref, g_ref, wu_ref, wd_ref, act_ref, gb_ref, out_acc, g_acc, rows, first, between):
    before = nn(ln_ref[rows, :], wu_ref[...])
    g_act = nn(g_ref[rows, :], wd_ref[...])
    act, gb = gelu_both(before, g_act)
    act, gb = act.astype(bf16), gb.astype(bf16)
    act_ref[rows, :] = act
    gb_ref[rows, :] = gb
    between()
    o, g = nt(act, wd_ref[...]), nt(gb, wu_ref[...])

    @pl.when(first)
    def _():
        out_acc[rows, :] = o
        g_acc[rows, :] = g

    @pl.when(jnp.logical_not(first))
    def _():
        out_acc[rows, :] += o
        g_acc[rows, :] += g


def mlp_kernel(
    sizes,
    length,
    plan,
    ln_ref,
    cot_ref,
    hidden_ref,
    early,
    zw,
    ax,
    index,
    up_bank,
    down_bank,
    vectors,
    y_ref,
    gh_ref,
    g_up_in,
    g_down_out,
    g_units,
    late,
    send,
    recv,
    w_buf,
    w_sems,
    g_buf,
    tail,
    gx,
    act,
    gb,
    out_acc,
    g_acc,
    sem,
    own_buf,
):
    i = pl.program_id(0)
    fn, hn, tn = sizes
    f, h, z = lax.axis_index("fsdp"), lax.axis_index("heads"), lax.axis_index("tensor")
    n, width = hidden_ref.shape
    number = index[(f * hn + h) * tn + z]
    gain, dbias = vectors.at[2:3], vectors.at[4:5]
    main = slice(0, width)
    s, half = i // 2, lax.rem(i, 2)
    comm = Comm(send, recv)
    done = early.shape[0]
    blocks = {b: Block(comm, sizes, zw, late.at[b - done], b, own_buf.at[b - done]) for b in range(done, tn)}

    def loads(b):
        slot = b % 2
        src = early.at[b] if b < done else late.at[b - done]
        return [
            pltpu.make_async_copy(src, w_buf.at[slot, :, pl.ds(0, width)], w_sems.at[slot, 0]),
            pltpu.make_async_copy(
                ax.at[:, lax.rem(z + b, tn)], w_buf.at[slot, :, pl.ds(width, EXTRA)], w_sems.at[slot, 1]
            ),
        ]

    @pl.when(i == 0)
    def _():
        c = Tokens(cot_ref, g_buf, tail, sem)
        c.start()
        for b in range(done):
            for w in loads(b):
                w.start()
        enter(sizes, f, h, z)
        if done in blocks:
            blocks[done].begin()
        c.wait()

        def body(rows, start):
            gx[rows, main] = g_buf[rows, :].astype(bf16)

        by_rows(n, 32, body)
        gx[:, width : width + RANK] = nt(gx[:, main], down_bank[number]).astype(bf16)
        gx[:, width + RANK :] = jnp.zeros((n, EXTRA - RANK), bf16)

    def events(steps):
        for at, what in steps:

            @pl.when(i == at)
            def _():
                for b, name in what:
                    if name == "load":
                        if b < tn:
                            if b in blocks:
                                blocks[b].arrive()
                            for w in loads(b):
                                w.start()
                    elif b in blocks:
                        getattr(blocks[b], name)()

    events(plan[0])

    for b in range(tn):

        @pl.when(i == 2 * b)
        def _():
            for w in loads(b):
                w.wait()

    slot = lax.rem(s, 2)
    rows = pl.ds(pl.multiple_of(half * (n // 2), n // 2), n // 2)
    mlp_half(ln_ref, gx, w_buf.at[slot, 0], w_buf.at[slot, 1], act, gb, out_acc, g_acc, rows, s == 0, lambda: events(plan[1]))

    @pl.when(half == 1)
    def _():
        g_units[0, s] = tn_(ln_ref[:, width : width + RANK], gb[...]).astype(bf16)
        g_units[1, s] = tn_(gx[:, width : width + RANK], act[...]).astype(bf16)

    @pl.when(i == pl.num_programs(0) - 1)
    def _():
        down_mid = out_acc[:, width : width + RANK].astype(bf16)
        g_up_mid = g_acc[:, width : width + RANK].astype(bf16)
        g_up_in[...] = tn_(g_up_mid, ln_ref[:, main]).astype(bf16)
        g_down_out[...] = tn_(down_mid, gx[:, main]).astype(bf16)
        out_acc[:, main] += nn(down_mid, down_bank[number])
        g_acc[:, main] += nn(g_up_mid, up_bank[number])

        def body(rows, start):
            v = hidden_ref[rows, :]
            out_acc[rows, main] += v + dbias[...]
            gh_ref[rows, :] = g_buf[rows, :] + real(
                norm_back(g_acc[rows, main], v, gain[...], width), start, length
            )

        by_rows(n, 32, body)
        c = Tokens(y_ref, out_acc, tail, sem, out=True)
        c.start()
        for b in blocks.values():
            b.drain()
        c.wait()


def mlp(sizes, ln, cot, hidden, early, zw, ax, index, up, down, vectors):
    fn, hn, tn = sizes
    n, width = hidden.shape
    depth = ln.shape[1]
    done, _, _, units = early.shape
    length = cot.shape[0]
    late = max(tn - done, 1)
    plan = (
        (
            (2, ((2, "forward"), (3, "begin"))),
            (3, ((2, "exchange"),)),
            (6, ((3, "load"),)),
        ),
        (
            (3, ((2, "load"),)),
            (4, ((3, "forward"),)),
            (5, ((3, "exchange"),)),
        ),
    )
    any_ = pl.BlockSpec(memory_space=pl.ANY)
    one = lambda s: pl.BlockSpec(s, lambda t: (0,) * len(s), pipeline_mode=pl.Buffered(1))
    shape = jax.ShapeDtypeStruct
    nsem = late * block_sems(fn)
    return pl.pallas_call(
        functools.partial(mlp_kernel, sizes, length, plan),
        grid=(2 * tn,),
        in_specs=[
            one((n, depth)),
            any_,
            one((n, width)),
            any_,
            any_,
            any_,
            pl.BlockSpec(memory_space=pltpu.SMEM),
            one(up.shape),
            one(down.shape),
            one(vectors.shape),
        ],
        out_specs=(
            any_,
            one((n, width)),
            one((RANK, width)),
            one((RANK, width)),
            one((2, tn, RANK, units)),
            any_,
        ),
        out_shape=(
            shape((length, 1, width), f32),
            shape((n, width), f32),
            shape((RANK, width), bf16),
            shape((RANK, width), bf16),
            shape((2, tn, RANK, units), bf16),
            shape((late, 2, width, units), bf16),
        ),
        scratch_shapes=[
            pltpu.SemaphoreType.DMA((nsem,)),
            pltpu.SemaphoreType.DMA((nsem,)),
            pltpu.VMEM((2, 2, depth, units), bf16),
            pltpu.SemaphoreType.DMA((2, 2)),
            pltpu.VMEM((n, width), f32),
            tail_shape(length, width),
            pltpu.VMEM((n, depth), bf16),
            pltpu.VMEM((n, units), bf16),
            pltpu.VMEM((n, units), bf16),
            pltpu.VMEM((n, depth), f32),
            pltpu.VMEM((n, depth), f32),
            pltpu.SemaphoreType.DMA((2,)),
            pltpu.VMEM((late,) + zw.shape[1:], bf16),
        ],
        compiler_params=params(collective_id=4, has_side_effects=True),
        name="mlp",
    )(ln, cot, hidden, early, zw, ax, index, up, down, vectors)


def branch_back_kernel(place, index, gh_ref, w_ref, out_bank, mixed_ref, mid_ref, g_up_in, g_down_out, gm_ref, grads, gx):
    n, width = gh_ref.shape
    half = w_ref.shape[-1]

    def body(rows, start):
        gx[rows, 0:width] = gh_ref[rows, :].astype(bf16)

    by_rows(n, 32, body)
    g_mid = nt(gx[:, 0:width], out_bank[index[place()]]).astype(bf16)
    gx[:, width:] = g_mid
    grads[...] = jnp.zeros_like(grads)
    grads[0:RANK, :] = tn_(mid_ref[...], gx[:, 0:width]).astype(bf16)
    grads[RANK : 2 * RANK, :] = g_up_in[...]
    grads[2 * RANK : 3 * RANK, :] = g_down_out[...]
    grads[3 * RANK : 4 * RANK, :] = tn_(g_mid, mixed_ref[...]).astype(bf16)
    for p in range(w_ref.shape[0]):
        gm_ref[:, p * half : (p + 1) * half] = nn(gx[...], w_ref[p]).astype(bf16)


def branch_back(rows, place, index, gh, w, out, mixed, mid, g_up_in, g_down_out):
    n, width = gh.shape
    return pl.pallas_call(
        functools.partial(branch_back_kernel, place),
        in_specs=[pl.BlockSpec(memory_space=pltpu.SMEM)] + [pl.BlockSpec(memory_space=pltpu.VMEM)] * 7,
        out_shape=(
            jax.ShapeDtypeStruct((n, width), bf16),
            jax.ShapeDtypeStruct((rows, width), bf16),
        ),
        scratch_shapes=[pltpu.VMEM((n, width + RANK), bf16)],
        compiler_params=params(),
        name="branch_back",
    )(index, gh, w, out, mixed, mid, g_up_in, g_down_out)


def add_by_adapter(pick, parts):
    width = parts.shape[-1]
    if parts.shape[-2] % 16:
        parts = parts.astype(f32)
    return nn(pick[...], parts.reshape(-1, width).astype(bf16))


def picks(adapters, count, rows):
    shape = (count * rows, adapters.shape[0] * rows)
    place = jnp.repeat(adapters * rows, rows) + jnp.tile(jnp.arange(rows), adapters.shape[0])
    return (lax.broadcasted_iota(jnp.int32, shape, 0) == place[None, :]).astype(bf16)


def line_copies(comm, tn, z, here, sems, own=None):
    up, down = sems

    def send(sem, block, to, src=None):
        return comm.copy(sem, here(block) if src is None else src, here(block), tensor=to)

    def begin():
        @pl.when(z < tn - 1)
        def _():
            send(up[0], z, z + 1, own).start()

        @pl.when(z > 0)
        def _():
            send(down[0], z, z - 1, own).start()

    def step(k, then):
        @pl.when(z - 1 - k >= 0)
        def _():
            b = z - 1 - k
            comm.copy(up[k], here(b), here(b), tensor=z - 1).wait_recv()
            if k + 1 < tn - 1:

                @pl.when(z < tn - 1)
                def _():
                    send(up[k + 1], b, z + 1).start()

            then(b)

        @pl.when(z + 1 + k < tn)
        def _():
            b = z + 1 + k
            comm.copy(down[k], here(b), here(b), tensor=z + 1).wait_recv()
            if k + 1 < tn - 1:

                @pl.when(z > 0)
                def _():
                    send(down[k + 1], b, z - 1).start()

            then(b)

    def drain():
        for k in range(tn - 1):

            @pl.when((z < tn - 1) & (z - k >= 0))
            def _():
                send(up[k], z, z + 1).wait_send()

            @pl.when((z > 0) & (z + k < tn))
            def _():
                send(down[k], z, z - 1).wait_send()

    return begin, step, drain


class Reduce:
    def __init__(self, sizes, count, comm, hot, local, a, out, ra, dense, b=None, out_b=None, rb=None, hot_b=None):
        fn, hn, tn = sizes
        f, h, z = lax.axis_index("fsdp"), lax.axis_index("heads"), lax.axis_index("tensor")
        self.fn, self.hn, self.tn, self.f, self.h, self.z = fn, hn, tn, f, h, z
        self.count, self.comm, self.hot, self.hot_b, self.local = count, comm, hot, hot_b, local
        self.a, self.out, self.ra, self.dense, self.b, self.out_b, self.rb = a, out, ra, dense, b, out_b, rb
        self.piece = ra.shape[1]
        self.s_first = [comm.new() for _ in range(fn - 1)]
        s_line = ([comm.new() for _ in range(tn - 1)], [comm.new() for _ in range(tn - 1)])
        self.s_core = [comm.new() for _ in range(tn)]
        self.s_last = comm.new()
        self.sent = []
        per = count // hn
        self.mine, self.theirs = pl.ds(h * per, per), pl.ds((1 - h) * per, per)

        def slot(o, r):
            start, size = (0, per) if r is None else r
            return out.at[o, pl.ds(h * per + start, size)]

        self.spread = Rows(comm, fn, f, slot, per, lambda: dense.at[self.mine], align=1)
        self.begin, self.line, self.drain_line = line_copies(
            comm, tn, z, lambda t: self.group(t, h), s_line
        )
        if b is not None:
            self.s_first_b = [comm.new() for _ in range(tn - 1)]
            self.s_core_b = comm.new()

            def slot_b(o, r):
                start, size = (0, tn) if r is None else r
                return rb.at[h, o, pl.ds(start, size)]

            self.spread_b = Rows(comm, fn, f, slot_b, tn, lambda: rb.at[h, f], align=1)

    def group(self, z, h):
        return self.ra.at[pl.ds((z * self.hn + h) * self.fn, self.fn)]

    def one(self, z, h, f):
        return self.ra.at[(z * self.hn + h) * self.fn + f]

    def rows(self, f):
        return self.a.at[pl.ds(pl.multiple_of(f * self.piece, 8), self.piece)]

    def send(self, make):
        make().start()
        self.sent.append(make)

    def own(self):
        copies = [pltpu.make_async_copy(self.rows(self.f), self.one(self.z, self.h, self.f), self.local.at[0])]
        if self.b is not None:
            copies.append(
                pltpu.make_async_copy(self.b.at[:, 0], self.rb.at[self.h, self.f, self.z], self.local.at[1])
            )
        return copies

    def start(self):
        f, h, z, comm = self.f, self.h, self.z, self.comm
        for m in range(1, self.fn):
            self.send(
                lambda m=m: comm.copy(
                    self.s_first[m - 1], self.rows(f ^ m), self.one(z, h, f), fsdp=f ^ m
                )
            )
        if self.b is not None:
            for d in range(1, self.tn):
                self.send(
                    lambda d=d: comm.copy(
                        self.s_first_b[d - 1],
                        self.b.at[:, d],
                        self.rb.at[h, f, z],
                        tensor=lax.rem(z + d, self.tn),
                    )
                )
        for c in self.own():
            c.start()

    def second(self):
        f, h, z, comm = self.f, self.h, self.z, self.comm
        for c in self.own():
            c.wait()
        for m in range(1, self.fn):
            b = self.one(z, h, f ^ m)
            comm.copy(self.s_first[m - 1], b, b, fsdp=f ^ m).wait_recv()
        self.begin()
        self.to_core(z).start()
        if self.b is not None:
            for d in range(1, self.tn):
                p = lax.rem(z + self.tn - d, self.tn)
                b = self.rb.at[h, f, p]
                comm.copy(self.s_first_b[d - 1], b, b, tensor=p).wait_recv()
            self.spread_b.begin()

    def to_core(self, block):
        b = self.group(block, self.h)
        return pltpu.make_async_remote_copy(
            src_ref=b,
            dst_ref=b,
            send_sem=self.comm.send.at[self.s_core[0] + block],
            recv_sem=self.comm.recv.at[self.s_core[0] + block],
            device_id={"heads": 1 - self.h},
            device_id_type=MESH,
        )

    def line_step(self, k):
        if k < self.tn - 1:
            self.line(k, lambda b: self.to_core(b).start())

    def forward_b(self):
        self.spread_b.forward_all()

    def exchange_b(self):
        self.spread_b.settle()
        b = self.rb.at[self.h]
        self.send(lambda: self.comm.copy(self.s_core_b, b, b, heads=1 - self.h))

    def fourth(self):
        h = self.h
        for k in range(self.tn):
            b = self.group(k, 1 - h)
            self.comm.copy(self.s_core[k], b, b, heads=1 - h).wait_recv()
        total = add_by_adapter(self.hot, self.ra[...])
        self.dense[...] = total.reshape(self.dense.shape).astype(bf16)
        self.spread.begin()
        self.last().start()

    def last(self):
        return pltpu.make_async_copy(
            self.dense.at[self.mine], self.out.at[self.f, self.mine], self.local.at[0]
        )

    def fifth(self):
        b = self.rb.at[1 - self.h]
        self.comm.copy(self.s_core_b, b, b, heads=1 - self.h).wait_recv()
        for k in range(2):
            total = add_by_adapter(self.hot_b, self.rb[:, :, :, k, :, :])
            self.out_b[k][...] = total.reshape(self.out_b[k].shape)

    def sixth(self):
        self.spread.forward_all()

    def seventh(self):
        self.last().wait()
        self.spread.settle()
        b = self.out.at[:, self.mine]
        self.send(lambda: self.comm.copy(self.s_last, b, b, heads=1 - self.h))

    def finish(self):
        h = self.h
        b = self.out.at[:, self.theirs]
        self.comm.copy(self.s_last, b, b, heads=1 - h).wait_recv()
        for make in self.sent:
            make().wait_send()
        self.drain_line()
        self.spread.drain()
        if self.b is not None:
            self.spread_b.drain()
        for k in range(self.tn):
            self.to_core(k).wait_send()


def reduce_sems(sizes, both):
    fn, hn, tn = sizes
    nb = bits_of(fn)
    tree = nb + 2 * (fn - 1 - nb)
    n = fn - 1 + 2 * (tn - 1) + tn + 1 + tree
    return n + (tn - 1 + 1 + tree if both else 0)


def enter_reduce(sizes, f, h, z):
    fn, hn, tn = sizes
    barrier = pltpu.get_barrier_semaphore()
    for m in range(1, fn):
        pl.semaphore_signal(barrier, 1, device_id={"fsdp": f ^ m}, device_id_type=MESH)
    pl.semaphore_signal(barrier, 1, device_id={"heads": 1 - h}, device_id_type=MESH)
    for d in range(1, tn):
        pl.semaphore_signal(barrier, 1, device_id={"tensor": lax.rem(z + d, tn)}, device_id_type=MESH)
    pl.semaphore_wait(barrier, fn - 1 + 1 + tn - 1)


def piece_rows(rows, fn):
    return -(-rows // (8 * fn)) * 8


def reduce_shapes(sizes, count, width, piece, units, both):
    fn, hn, tn = sizes
    n = fn * hn * tn
    shapes = [
        pltpu.SemaphoreType.DMA((reduce_sems(sizes, both),)),
        pltpu.SemaphoreType.DMA((reduce_sems(sizes, both),)),
        pltpu.SemaphoreType.DMA((2,)),
        pltpu.VMEM((n, piece, width), bf16),
        pltpu.VMEM((count, piece, width), bf16),
    ]
    if both:
        shapes.append(pltpu.VMEM((hn, fn, tn, 2, RANK, units), bf16))
    return shapes


def attend_back_kernel(
    sizes, length, count, plan, hot, hot_b, q_ref, k_ref, v_ref, do_ref, log_ref, a, b, out_ref, sums, sums_u, sums_d, send, recv, local, ra, dense, rb, kt_ref, dq_ref, dk_ref, dv_ref
):
    head = pl.program_id(0)
    job = Reduce(sizes, count, Comm(send, recv), hot, local, a, sums, ra, dense, b, (sums_u, sums_d), rb, hot_b)

    @pl.when(head == 0)
    def _():
        enter_reduce(sizes, job.f, job.h, job.z)
        job.start()
        to_rows(kt_ref, k_ref.at[0])

        def clear(at):
            for r in (dk_ref, dv_ref):
                r[:, at] = jnp.zeros((r.shape[0], LANES), f32)

        columns(dk_ref.shape[1], clear)

    for at, what in plan:

        @pl.when(head == at)
        def _():
            for name, *more in what:
                getattr(job, name)(*more)

    attend_back_head(
        length, head, q_ref.at[0], k_ref.at[0], v_ref.at[0], do_ref, log_ref, kt_ref, dq_ref, dk_ref, dv_ref
    )

    @pl.when(head == pl.num_programs(0) - 1)
    def _():
        to_lanes(out_ref.at[0], dq_ref)

        def cast(at):
            out_ref[1, :, at] = dk_ref[:, at].astype(bf16)
            out_ref[2, :, at] = dv_ref[:, at].astype(bf16)

        columns(dk_ref.shape[1], cast)
        job.finish()


def attend_back(sizes, length, count, hot, hot_b, qkv, do, log, a, b):
    fn, hn, tn = sizes
    _, n, width = qkv.shape
    heads = width // HEAD_DIM
    units = b.shape[-1]
    piece = a.shape[0] // fn
    plan = (
        (2, (("second",),)),
        (5, (("line_step", 0),)),
        (7, (("line_step", 1), ("forward_b",))),
        (9, (("line_step", 2), ("exchange_b",))),
        (11, (("fourth",),)),
        (12, (("fifth",),)),
        (13, (("sixth",),)),
        (15, (("seventh",),)),
    )
    any_ = pl.BlockSpec(memory_space=pl.ANY)
    one = lambda j: pl.BlockSpec((1, n, width), lambda h: (j, 0, 0), pipeline_mode=pl.Buffered(1))
    return pl.pallas_call(
        functools.partial(attend_back_kernel, sizes, length, count, plan),
        grid=(heads,),
        in_specs=[
            whole(hot.shape),
            whole(hot_b.shape),
            one(0),
            one(1),
            one(2),
            whole((n, width)),
            whole((heads, n)),
            any_,
            any_,
        ],
        out_specs=(whole((3, n, width)), any_) + (whole((count, RANK, units)),) * 2,
        out_shape=(
            jax.ShapeDtypeStruct((3, n, width), bf16),
            jax.ShapeDtypeStruct((fn, count, piece, width), bf16),
        )
        + (jax.ShapeDtypeStruct((count, RANK, units), f32),) * 2,
        scratch_shapes=reduce_shapes(sizes, count, width, piece, units, True)
        + [pltpu.VMEM((width, n), f32)] * 2
        + [pltpu.VMEM((n, width), f32)] * 2,
        compiler_params=params(collective_id=1, has_side_effects=True),
        name="attend_back",
    )(hot, hot_b, qkv, qkv, qkv, do, log, a, b)


def project_back_kernel(
    sizes,
    count,
    hot,
    index,
    before,
    g_ref,
    w_any,
    first_ref,
    mid_ref,
    ln_ref,
    gh_any,
    x_ref,
    vectors,
    gi_ref,
    sums,
    a,
    g_proj_out,
    g_up_in,
    g_down_out,
    g_proj_in,
    send,
    recv,
    local,
    ra,
    dense,
    w_buf,
    gh_buf,
    w_sems,
    x_buf,
    tail,
    acc,
    grads,
    g_mid,
    sem,
    before_buf,
):
    i = pl.program_id(0)
    length = x_ref.shape[0]
    n, width = ln_ref.shape
    half = w_buf.shape[-1]
    gain = vectors.at[0:1]
    parts = w_buf.shape[1]
    load = Tokens(x_ref, x_buf, tail, sem)
    job = Reduce(sizes, count, Comm(send, recv), hot, local, a, sums, ra, dense)
    number = index[(job.f * job.hn + job.h) * job.tn + job.z]

    def load_w(j):
        return pltpu.make_async_copy(w_any.at[j], w_buf.at[j], w_sems.at[j])

    load_gh = pltpu.make_async_copy(gh_any, gh_buf, w_sems.at[3])
    load_before = pltpu.make_async_copy(before, before_buf, w_sems.at[5])
    save = pltpu.make_async_copy(grads, a, w_sems.at[4])

    @pl.when(i == 0)
    def _():
        for j in range(3):
            load_w(j).start()
        load.start()
        load_gh.start()
        load_before.start()
        enter_reduce(sizes, job.f, job.h, job.z)
        if grads.shape[0] > 6 * RANK:
            grads[6 * RANK :, :] = jnp.zeros((grads.shape[0] - 6 * RANK, width), bf16)
        for j in range(3):
            load_w(j).wait()

        def small(j, _):
            m = sum(
                nt(g_ref[j, :, p * half : (p + 1) * half], w_buf[j, p, pl.ds(width, RANK), :])
                for p in range(parts)
            ).astype(bf16)
            g_mid[j] = m
            at = pl.ds(pl.multiple_of((3 + j) * RANK, RANK), RANK)
            grads[at, :] = tn_(mid_ref[j], g_ref[j]).astype(bf16)
            return 0

        lax.fori_loop(0, 3, small, 0)
        mids = jnp.concatenate([g_mid[j].astype(f32).T for j in range(3)]).astype(bf16)
        grads[0 : 3 * RANK, :] = nn(mids, ln_ref[...]).astype(bf16)
        save.start()
        save.wait()
        job.start()

    @pl.when(i == 2)
    def _():
        job.second()

    @pl.when(i == 3)
    def _():
        job.line_step(0)

    @pl.when((i > 0) & (i < 4))
    def _():
        j = i - 1
        r = nn(g_mid[j], first_ref[j, number])
        for p in range(parts):
            r = r + nt(g_ref[j, :, p * half : (p + 1) * half], w_buf[j, p, pl.ds(0, width), :])

        @pl.when(i == 1)
        def _():
            acc[...] = r

        @pl.when(i > 1)
        def _():
            acc[...] += r

    @pl.when(i == 4)
    def _():
        job.line_step(1)
        load.wait()
        load_gh.wait()

        def body(rows, start):
            v = x_buf[rows, :]
            acc[rows, :] = gh_buf[rows, :] + norm_back(acc[rows, :], v, gain[...], width)

        by_rows(n, 32, body)
        c = Tokens(gi_ref, acc, tail, sem, out=True)
        c.start()
        for k in range(2, sizes[2] - 1):
            job.line_step(k)
        job.fourth()
        load_before.wait()
        piece = before_buf.shape[2]

        def rows_of(k, r):
            k = k * RANK + r * 8
            return before_buf[k // piece, :, k % piece : k % piece + 8, :].astype(f32)

        for k, dst in enumerate((g_proj_out, g_up_in, g_down_out)):
            for r in range(2):
                dst[:, r * 8 : r * 8 + 8, :] = rows_of(k, r)

        for p in range(parts):

            @pl.when(job.h == p)
            def _():
                for r in range(2):
                    g_proj_in[:, r * 8 : r * 8 + 8, :] = rows_of(3, r)[:, :, p * half : (p + 1) * half]

        job.sixth()
        job.seventh()
        job.finish()
        c.wait()


def project_back(sizes, count, hot, index, before, g, w, first, mid, ln, gh, x, vectors):
    fn, hn, tn = sizes
    n, width = ln.shape
    half = w.shape[-1]
    length = x.shape[0]
    piece = piece_rows(6 * RANK, fn)
    any_ = pl.BlockSpec(memory_space=pl.ANY)
    one = lambda s: pl.BlockSpec(s, lambda t: (0,) * len(s), pipeline_mode=pl.Buffered(1))
    shape = jax.ShapeDtypeStruct
    return pl.pallas_call(
        functools.partial(project_back_kernel, sizes, count),
        grid=(5,),
        in_specs=[
            one(hot.shape),
            pl.BlockSpec(memory_space=pltpu.SMEM),
            any_,
            one(g.shape),
            any_,
            one(first.shape),
            one(mid.shape),
            one((n, width)),
            any_,
            any_,
            one(vectors.shape),
        ],
        out_specs=(any_, any_, any_) + (one((count, RANK, width)),) * 3 + (one((count, RANK, half)),),
        out_shape=(
            shape((length, 1, width), f32),
            shape((fn, count, piece, width), bf16),
            shape((fn * piece, width), bf16),
        )
        + (shape((count, RANK, width), f32),) * 3
        + (shape((count, RANK, half), f32),),
        scratch_shapes=reduce_shapes(sizes, count, width, piece, 0, False)
        + [
            pltpu.VMEM(w.shape, bf16),
            pltpu.VMEM((n, width), f32),
            pltpu.SemaphoreType.DMA((6,)),
            pltpu.VMEM((n, width), f32),
            tail_shape(length, width),
            pltpu.VMEM((n, width), f32),
            pltpu.VMEM((fn * piece, width), bf16),
            pltpu.VMEM(mid.shape, bf16),
            pltpu.SemaphoreType.DMA((2,)),
            pltpu.VMEM(before.shape, bf16),
        ],
        compiler_params=params(collective_id=2, has_side_effects=True),
        name="qkv_back",
    )(hot, index, before, g, w, first, mid, ln, gh, x, vectors)


def per_device(
    inputs,
    cotangent,
    image_adapter_index,
    first_norm_gain,
    first_norm_bias,
    second_norm_gain,
    second_norm_bias,
    query_key_value_weight,
    attention_output_weight,
    up_weight,
    down_weight,
    up_projection_bias,
    down_projection_bias,
    query_key_value_adapter_first,
    query_key_value_adapter_second,
    projection_adapter_first,
    projection_adapter_second,
    up_adapter_first,
    up_adapter_second,
    down_adapter_first,
    down_adapter_second,
):
    sizes = tuple(lax.axis_size(a) for a in ("fsdp", "heads", "tensor"))
    fn, hn, tn = sizes
    f, h, z = (lax.axis_index(a) for a in ("fsdp", "heads", "tensor"))
    images, length, width = inputs.shape
    assert images == 1 and hn == 2
    count = query_key_value_adapter_first.shape[1]
    units = up_weight.shape[-1]
    x, cot = jnp.swapaxes(inputs, 0, 1), jnp.swapaxes(cotangent, 0, 1)
    vectors = jnp.concatenate(
        [
            first_norm_gain,
            first_norm_bias,
            second_norm_gain,
            second_norm_bias,
            down_projection_bias.astype(f32),
        ]
    ).reshape(5, width)
    index = image_adapter_index
    qkv_in = jnp.swapaxes(query_key_value_adapter_first, 2, 3)
    u_in = jnp.swapaxes(up_adapter_first, 1, 2)
    wq, wo, zw, ax, ln1, qkv, qkv_mid, mixed, log, hidden, ln2, proj_mid, early = attention(
        sizes,
        jnp.swapaxes(query_key_value_weight, 0, 1),
        attention_output_weight,
        up_weight,
        down_weight,
        query_key_value_adapter_second,
        jnp.swapaxes(projection_adapter_first, 1, 2),
        up_adapter_second,
        down_adapter_first,
        jnp.pad(up_projection_bias[None], ((0, EXTRA - RANK - 1), (0, 0))),
        index,
        qkv_in,
        projection_adapter_second,
        x,
        vectors,
        u_in,
    )
    y, g_hidden, g_up_in, g_down_out, g_units, _ = mlp(
        sizes, ln2, cot, hidden, early, zw, ax, index, u_in, down_adapter_second, vectors
    )
    g_mixed, grads = branch_back(
        piece_rows(4 * RANK, fn) * fn,
        lambda: (lax.axis_index("fsdp") * hn + lax.axis_index("heads")) * tn + lax.axis_index("tensor"),
        index,
        g_hidden,
        wo,
        projection_adapter_second,
        mixed,
        proj_mid,
        g_up_in,
        g_down_out,
    )
    by_place = image_adapter_index.reshape(fn, hn, tn)
    order = jnp.transpose(by_place, (2, 1, 0)).reshape(-1)
    order_b = jnp.transpose(by_place, (1, 0, 2)).reshape(-1)
    pick = picks(order, count, piece_rows(4 * RANK, fn))
    pick_b = picks(order_b, count, RANK)
    g_qkv, sums, g_up_out, g_down_in = attend_back(
        sizes, length, count, pick, pick_b, qkv, g_mixed, log, grads, g_units
    )
    g_x, last, _, g_proj_out, g_up_in, g_down_out, g_proj_in = project_back(
        sizes,
        count,
        picks(order, count, piece_rows(6 * RANK, fn)),
        index,
        sums,
        g_qkv,
        wq,
        qkv_in,
        qkv_mid,
        ln1,
        g_hidden,
        x,
        vectors,
    )
    last = jnp.moveaxis(last, 0, 1).reshape(count, -1, width)
    last = jnp.moveaxis(last[:, : 6 * RANK].reshape(count, 6, RANK, width), 0, 1).astype(f32)
    half = width // hn
    return (
        jnp.swapaxes(y, 0, 1),
        jnp.swapaxes(g_x, 0, 1),
        jnp.swapaxes(last[:3], 2, 3),
        lax.dynamic_slice_in_dim(last[3:], h * half, half, axis=-1),
        jnp.swapaxes(g_proj_in, 1, 2),
        g_proj_out,
        jnp.swapaxes(g_up_in, 1, 2),
        g_up_out,
        g_down_in,
        g_down_out,
    )


def solution(mesh):
    in_specs = (
        P(("fsdp", "heads", "tensor"), None, None),
        P(("fsdp", "heads", "tensor"), None, None),
        P(),
        P(),
        P(),
        P(),
        P(),
        P("fsdp", None, "heads"),
        P("fsdp", "heads"),
        P("fsdp", "tensor"),
        P("fsdp", "tensor"),
        P("tensor"),
        P(),
        P(),
        P(None, None, None, "heads"),
        P(None, "heads", None),
        P(),
        P(),
        P(None, None, "tensor"),
        P(None, None, "tensor"),
        P(),
    )
    out_specs = (
        P(("fsdp", "heads", "tensor"), None, None),
        P(("fsdp", "heads", "tensor"), None, None),
        P(),
        P(None, None, None, "heads"),
        P(None, "heads", None),
        P(),
        P(),
        P(None, None, "tensor"),
        P(None, None, "tensor"),
        P(),
    )
    return jax.shard_map(
        per_device, mesh=mesh, in_specs=in_specs, out_specs=out_specs, check_vma=False
    )
```

```python
import functools
import jax
import jax.numpy as jnp
from jax import lax
from jax.experimental import pallas as pl
from jax.experimental.pallas import tpu as pltpu
from jax.sharding import PartitionSpec as P

HEAD_DIM = 72
norm_eps = 1e-06
f32 = jnp.float32
bf16 = jnp.bfloat16
MESH = pl.DeviceIdType.MESH


RANK = 16
EXTRA = 32


def padded(n):
    return -(-n // 16) * 16


def row_sums(v):
    return jnp.sum(v, axis=-1, keepdims=True)


class Tokens:
    def __init__(self, hbm, buf, tail, sems, out=False):
        self.length = hbm.shape[0]
        self.buf, self.tail, self.out = buf, tail, out
        self.whole = self.length // 8 * 8
        pairs = [(hbm.at[0 : self.whole, 0, :], buf.at[0 : self.whole, 0 : hbm.shape[-1]])]
        if self.whole < self.length:
            pairs.append((hbm.at[self.whole : self.length, 0, :], tail))
        self.copies = [
            pltpu.make_async_copy(*((b, a) if out else (a, b)), sems.at[i]) for i, (a, b) in enumerate(pairs)
        ]

    def start(self):
        if self.out and self.whole < self.length:
            self.tail[...] = self.buf[self.whole : self.length, 0 : self.tail.shape[-1]]
        for c in self.copies:
            c.start()

    def wait(self):
        for c in self.copies:
            c.wait()
        if not self.out:
            rest = self.buf.shape[0] - self.length
            zeros = jnp.zeros((rest, self.buf.shape[1]), f32)
            if self.whole < self.length:
                zeros = jnp.concatenate([self.tail[...], zeros])
            self.buf[self.whole :, :] = zeros


def tail_shape(length, width):
    return pltpu.VMEM((max(length % 8, 1), width), f32)


def unit_of(v, width):
    mean = row_sums(v) * (1.0 / width)
    centred = v - mean
    inverse = lax.rsqrt(row_sums(centred * centred) * (1.0 / width) + norm_eps)
    return centred * inverse, inverse


def by_rows(n, step, body):
    def one(r, _):
        body(pl.ds(pl.multiple_of(r * step, step), step), r * step)
        return 0

    lax.fori_loop(0, n // step, one, 0)


def real(v, start, length):
    row = lax.broadcasted_iota(jnp.int32, v.shape, 0) + start
    return jnp.where(row < length, v, 0.0)


def normalize_into(dst, src, gain, bias, length):
    n, width = src.shape

    def body(rows, start):
        unit, _ = unit_of(src[rows, :], width)
        dst[rows, 0:width] = real(unit * gain[...] + bias[...], start, length).astype(bf16)

    by_rows(n, 32, body)


def norm_back(grad, v, gain, width):
    unit, inverse = unit_of(v, width)
    e = grad * gain
    return inverse * (e - row_sums(e) * (1.0 / width) - unit * (row_sums(e * unit) * (1.0 / width)))


LANES = 128
SCALE = HEAD_DIM**-0.5
LOG2E = 1.4426950408889634


def nn(a, b):
    return lax.dot_general(a, b, (((1,), (0,)), ((), ())), preferred_element_type=f32)


def nt(a, b):
    return lax.dot_general(a, b, (((1,), (1,)), ((), ())), preferred_element_type=f32)


def tn_(a, b):
    return lax.dot_general(a, b, (((0,), (0,)), ((), ())), preferred_element_type=f32)


def whole(shape):
    return pl.BlockSpec(shape, lambda *_: (0,) * len(shape))


def params(limit=60, **more):
    return pltpu.CompilerParams(vmem_limit_bytes=limit << 20, **more)


def head_window(head, width):
    tile = jnp.minimum(head * HEAD_DIM // LANES, width // LANES - 2)
    return pl.ds(pl.multiple_of(tile * LANES, LANES), 2 * LANES), head * HEAD_DIM - tile * LANES


def only_head(values, start):
    lane = lax.broadcasted_iota(jnp.int32, values.shape, 1)
    return jnp.where((lane >= start) & (lane < start + HEAD_DIM), values, jnp.zeros_like(values))


def own_rows(head):
    return pl.ds(pl.multiple_of(head * HEAD_DIM, 8), HEAD_DIM)


def attend_forward_head(length, head, q_ref, k_ref, vt_ref, sum_ref, log_ref):
    win, start = head_window(head, q_ref.shape[-1])
    q = only_head(q_ref[:, win], start)
    v = vt_ref[own_rows(head), :].astype(bf16)
    s = nt(k_ref[:, win], q)
    key = lax.broadcasted_iota(jnp.int32, s.shape, 0)
    s = jnp.where(key < length, s, -1e30)
    top = jnp.max(s, axis=0, keepdims=True)
    p = jnp.exp2((s - top) * (SCALE * LOG2E))
    total = jnp.sum(p, axis=0, keepdims=True)
    sum_ref[own_rows(head), :] = nn(v, p.astype(bf16)) * (1.0 / total)
    log_ref[pl.ds(head, 1), :] = top * (SCALE * LOG2E) + jnp.log(total) * LOG2E


def attend_back_head(length, head, q_ref, k_ref, v_ref, do_ref, log_ref, kt_ref, dq_ref, dk_ref, dv_ref):
    win, start = head_window(head, q_ref.shape[-1])
    q = only_head(q_ref[:, win], start)
    k = k_ref[:, win]
    do = only_head(do_ref[:, win], start)
    s = nt(k, q)
    key = lax.broadcasted_iota(jnp.int32, s.shape, 0)
    p = jnp.exp2(jnp.where(key < length, s * (SCALE * LOG2E), -1e30) - log_ref[pl.ds(head, 1), :])
    dp = nt(v_ref[:, win], do)
    pd = p * dp
    ds = (pd - p * jnp.sum(pd, axis=0, keepdims=True)).astype(bf16)
    dv_ref[:, win] += nn(p.astype(bf16), do)
    dk_ref[:, win] += nn(ds, q) * SCALE
    dq_ref[own_rows(head), :] = nn(kt_ref[own_rows(head), :].astype(bf16), ds) * SCALE


def columns(width, body):
    def one(c, _):
        body(pl.ds(pl.multiple_of(c * LANES, LANES), LANES))
        return 0

    lax.fori_loop(0, width // LANES, one, 0)


def to_rows(dst, src):
    def body(at):
        dst[at, :] = src[:, at].astype(f32).T.astype(dst.dtype)

    columns(src.shape[1], body)


def to_lanes(dst, src):
    def body(at):
        dst[:, at] = src[at, :].T.astype(dst.dtype)

    columns(src.shape[0], body)


def bits_of(n):
    return n.bit_length() - 1


class Comm:
    def __init__(self, send, recv):
        self.send, self.recv, self.n = send, recv, 0

    def new(self):
        self.n += 1
        return self.n - 1

    def copy(self, i, src, dst, **where):
        return pltpu.make_async_remote_copy(
            src_ref=src,
            dst_ref=dst,
            send_sem=self.send.at[i],
            recv_sem=self.recv.at[i],
            device_id=where,
            device_id_type=MESH,
        )


def enter(axes_sizes, f, h, z):
    fn, hn, tn = axes_sizes
    barrier = pltpu.get_barrier_semaphore()
    count = 0
    for b in range(bits_of(fn)):
        pl.semaphore_signal(
            barrier, 1, device_id={"fsdp": f ^ (1 << b)}, device_id_type=MESH
        )
        count += 1
    pl.semaphore_signal(barrier, 1, device_id={"heads": 1 - h}, device_id_type=MESH)
    count += 1
    for d in range(1, tn):
        pl.semaphore_signal(
            barrier, 1, device_id={"tensor": lax.rem(z + d, tn)}, device_id_type=MESH
        )
        count += 1
    pl.semaphore_wait(barrier, count)


class Rows:
    def __init__(self, comm, fn, f, slot, rows, own, align=8):
        self.comm, self.fn, self.f, self.slot, self.own = comm, fn, f, slot, own
        self.nb = bits_of(fn)
        half = rows // 2 // align * align
        self.parts = ((0, half, list(range(self.nb))), (half, rows - half, list(range(self.nb))[::-1]))
        self.first = [comm.new() for _ in range(self.nb)]
        self.later = {}
        for p, (_, _, order) in enumerate(self.parts):
            for m in range(1, fn):
                last = max(order.index(b) for b in range(self.nb) if m >> b & 1)
                for b in order[last + 1 :]:
                    self.later[p, m, b] = comm.new()
        self.sent = []
        self.first_done = False

    def part(self, origin, p):
        start, size, _ = self.parts[p]
        return self.slot(origin, (start, size))

    def begin(self):
        for b in range(self.nb):
            self.send(
                lambda b=b: self.comm.copy(
                    self.first[b], self.own(), self.slot(self.f, None), fsdp=self.f ^ (1 << b)
                )
            )

    def _arrived(self, m, p):
        order = self.parts[p][2]
        last = max(order.index(b) for b in range(self.nb) if m >> b & 1)
        b = order[last]
        src = m ^ (1 << b)
        if src == 0:
            return None
        where = self.part(self.f ^ m, p)
        return self.comm.copy(self.later[p, src, b], where, where, fsdp=self.f ^ (1 << b))

    def forward(self, m):
        if m & (m - 1) == 0 and not self.first_done:
            b = bits_of(m)
            where = self.slot(self.f ^ m, None)
            self.comm.copy(self.first[b], where, where, fsdp=self.f ^ m).wait_recv()
        for p, (_, _, order) in enumerate(self.parts):
            if m & (m - 1):
                self._arrived(m, p).wait_recv()
            last = max(order.index(b) for b in range(self.nb) if m >> b & 1)
            for b in order[last + 1 :]:

                def onward(p=p, b=b):
                    where = self.part(self.f ^ m, p)
                    return self.comm.copy(self.later[p, m, b], where, where, fsdp=self.f ^ (1 << b))

                self.send(onward)

    def masks(self):
        return sorted(range(1, self.fn), key=lambda m: (bin(m).count("1"), m))

    def finish_first(self):
        for b in range(self.nb):
            where = self.slot(self.f ^ (1 << b), None)
            self.comm.copy(self.first[b], where, where, fsdp=self.f ^ (1 << b)).wait_recv()
        self.drain()

    def leaf(self, m):
        return not any(key[1] == m for key in self.later)

    def forward_all(self):
        for m in self.masks():
            if not self.leaf(m):
                self.forward(m)

    def settle(self):
        for m in self.masks():
            if self.leaf(m):
                self.forward(m)

    def send(self, make):
        make().start()
        self.sent.append(make)

    def drain(self):
        for make in self.sent:
            make().wait_send()


def tree_sems(fn):
    nb = bits_of(fn)
    return nb + 2 * (fn - 1 - nb)


class Bounce:
    def __init__(self, src, buf, dst, sem):
        self.load = pltpu.make_async_copy(src, buf, sem)
        self.save = pltpu.make_async_copy(buf, dst, sem)

    def start(self):
        self.load.start()

    def turn(self):
        self.load.wait()
        self.save.start()

    def wait(self):
        self.save.wait()


class Block:
    def __init__(self, comm, sizes, zw, dst, s, buf, own=None):
        fn, hn, tn = sizes
        f, h, z = lax.axis_index("fsdp"), lax.axis_index("heads"), lax.axis_index("tensor")
        rows = zw.shape[1]
        self.comm, self.dst, self.h, self.buf = comm, dst, h, buf
        t = lax.rem(z + s, tn)

        def slot(o, r):
            start, size = (0, rows) if r is None else r
            return dst.at[h, pl.ds(pl.multiple_of(o * rows + start, 8), size)]

        self.own = lambda: zw.at[t] if own is None else own
        self.slot = lambda: slot(f, None)
        self.job = Rows(comm, fn, f, slot, rows, self.own)
        self.local = comm.new()
        self.core = comm.new()

    def mine(self):
        return Bounce(self.own(), self.buf, self.slot(), self.comm.send.at[self.local])

    def to_core(self, which):
        b = self.dst.at[which]
        return self.comm.copy(self.core, b, b, heads=1 - self.h)

    def begin(self):
        self.job.begin()
        self.mine().start()

    def forward(self):
        self.mine().turn()
        self.job.forward_all()

    def exchange(self):
        self.job.settle()
        self.mine().wait()
        self.to_core(self.h).start()

    def arrive(self):
        self.to_core(1 - self.h).wait_recv()

    def drain(self):
        self.job.drain()
        self.to_core(self.h).wait_send()


def block_sems(fn):
    return tree_sems(fn) + 2


class Weight:
    def __init__(self, comm, fn, f, h, rows, own, dst, extra, own_sem, buf):
        self.comm, self.h, self.dst, self.extra = comm, h, dst, extra
        width = fn * rows
        self.main, self.more = pl.ds(0, width), pl.ds(width, RANK)

        def slot(o, r):
            start, size = (0, rows) if r is None else r
            return dst.at[h, pl.ds(pl.multiple_of(o * rows + start, 8), size)]

        self.job = Rows(comm, fn, f, slot, rows, lambda: own)
        self.core, self.core_extra = comm.new(), comm.new()
        self.mine = lambda: Bounce(own, buf, slot(f, None), own_sem.at[0])
        self.mine_extra = lambda: pltpu.make_async_copy(
            extra.at[h], dst.at[h, self.more], own_sem.at[1]
        )

    def start_extra(self):
        self.mine_extra().start()
        self.to_core_extra().start()

    def to_core_extra(self):
        return self.comm.copy(
            self.core_extra, self.extra.at[1 - self.h], self.dst.at[self.h, self.more], heads=1 - self.h
        )

    def to_core(self, which):
        b = self.dst.at[which, self.main]
        return self.comm.copy(self.core, b, b, heads=1 - self.h)

    def exchange(self):
        self.job.settle()
        self.mine().wait()
        self.to_core(self.h).start()

    def arrive(self):
        self.mine_extra().wait()
        where = self.dst.at[1 - self.h, self.more]
        self.comm.copy(self.core_extra, where, where, heads=1 - self.h).wait_recv()
        self.to_core(1 - self.h).wait_recv()

    def drain(self):
        self.job.drain()
        self.to_core(self.h).wait_send()
        self.to_core_extra().wait_send()


def attention_kernel(
    sizes,
    wq,
    wo,
    wu,
    wd,
    bq,
    bp,
    bu,
    bd,
    ub,
    index,
    first_ref,
    out_ref,
    x_ref,
    vectors,
    up_ref,
    oq,
    oo,
    zw,
    ax,
    ln_out,
    qkv_out,
    qmid_ref,
    mixed_ref,
    log_ref,
    hidden_ref,
    ln2_ref,
    mid_ref,
    got,
    send,
    recv,
    wq_buf,
    wo_buf,
    w_sems,
    own_sems,
    own_q,
    own_o,
    own_z,
    own_b,
    aq,
    ap,
    a2,
    qkv_ref,
    lnx_ref,
    vt_ref,
    sum_ref,
    x_buf,
    x_tail,
    x_sems,
):
    i = pl.program_id(0)
    fn, hn, tn = sizes
    f, h, z = lax.axis_index("fsdp"), lax.axis_index("heads"), lax.axis_index("tensor")
    rows, half = wo.shape
    length = x_ref.shape[0]
    n, width = mixed_ref.shape
    number = index[(f * hn + h) * tn + z]
    gain1, bias1, gain, bias = (vectors.at[k : k + 1] for k in range(4))
    heads = width // HEAD_DIM
    comm = Comm(send, recv)
    qs = [
        Weight(comm, fn, f, h, rows, wq.at[j], oq.at[j], aq.at[j], own_sems.at[j], own_q.at[j])
        for j in range(3)
    ]
    o = Weight(comm, fn, f, h, rows, wo, oo, ap, own_sems.at[3], own_o)
    line = ([comm.new() for _ in range(tn - 1)], [comm.new() for _ in range(tn - 1)])
    small = [comm.new() for _ in range(tn - 1)]
    blocks = [
        Block(comm, sizes, zw, got.at[b], b, own_b.at[b], own_z if b == 0 else None)
        for b in range(own_b.shape[0])
    ]
    nxt = [Block(comm, sizes, zw, got.at[b], b, own_z) for b in range(len(blocks), min(len(blocks) + 2, tn))]
    begin_z, step_z, drain_z = line_copies(comm, tn, z, lambda t: zw.at[t], line, own_z)
    mine_z = [Bounce(w, own_z, zw.at[z], own_sems.at[4, 0]) for w in (wu, wd)]
    mine_a = lambda: pltpu.make_async_copy(a2.at[z], ax.at[:, z], own_sems.at[4, 1])
    to_line = lambda d: comm.copy(
        small[d - 1], a2.at[lax.rem(z + d, tn)], ax.at[:, z], tensor=lax.rem(z + d, tn)
    )
    load_x = Tokens(x_ref, x_buf, x_tail, x_sems)
    load_q = lambda j: pltpu.make_async_copy(oq.at[j], wq_buf.at[j], w_sems.at[j])
    load_o = lambda: pltpu.make_async_copy(oo, wo_buf, w_sems.at[3])
    save_ln = lambda: pltpu.make_async_copy(lnx_ref.at[:, pl.ds(0, width)], ln_out, w_sems.at[4])
    save_qkv = lambda: pltpu.make_async_copy(qkv_ref, qkv_out, w_sems.at[5])

    @pl.when(i == 0)
    def _():
        load_x.start()
        for w in qs + [o]:
            w.mine().start()
        for p in range(2):

            @pl.when(h == p)
            def _():
                mine_z[p].start()

        for p in range(hn):
            k = index[(f * hn + p) * tn + z]
            for j in range(3):
                aq[j, p] = bq[j, k]
            ap[p] = bp[k]
        for t in range(tn):
            k = index[(f * hn + h) * tn + t]
            a2[t, 0, 0:RANK] = bu[k]
            a2[t, 1, 0:RANK] = bd[k]
            a2[t, 0, RANK:] = ub[...]
            a2[t, 1, RANK:] = jnp.zeros_like(ub)
        enter(sizes, f, h, z)
        qs[0].job.begin()
        qs[1].job.begin()
        mine_z[0].turn()
        begin_z()
        for w in qs + [o]:
            w.start_extra()
        mine_a().start()
        for d in range(1, tn):
            to_line(d).start()
        for w in qs + [o]:
            w.mine().turn()
        load_x.wait()
        normalize_into(lnx_ref, x_buf, gain1, bias1, length)
        save_ln().start()

    @pl.when(i == 1)
    def _():
        qs[0].job.forward_all()
        qs[2].job.begin()
        qs[1].job.forward_all()
        step_z(0, lambda t: None)
        qs[0].exchange()
        qs[0].arrive()
        load_q(0).start()

    @pl.when(i == 2)
    def _():
        qs[2].job.forward_all()
        o.job.begin()
        qs[1].exchange()
        qs[1].arrive()
        load_q(1).start()
        qs[2].exchange()

    @pl.when(i == 3)
    def _():
        if tn > 2:
            step_z(1, lambda t: None)
        qs[2].arrive()
        load_q(2).start()

    @pl.when((i >= 1) & (i < 4))
    def _():
        j = i - 1
        mid = nt(lnx_ref[:, 0:width], first_ref[j, number]).astype(bf16)
        qmid_ref[j] = mid
        load_q(j).wait()

        @pl.when(i == 1)
        def _():
            save_ln().wait()

        lnx_ref[:, width:] = mid
        for p in range(hn):
            qkv_ref[j, :, p * half : (p + 1) * half] = nn(lnx_ref[...], wq_buf[j, p]).astype(bf16)

    @pl.when(i == 4)
    def _():
        save_qkv().start()
        o.job.forward_all()
        blocks[0].begin()
        to_rows(vt_ref, qkv_ref.at[2])

    @pl.when(i == 8)
    def _():
        o.exchange()

    @pl.when(i == 11)
    def _():
        o.arrive()
        load_o().start()

    @pl.when(i == 9)
    def _():
        for k in range(2, tn - 1):
            step_z(k, lambda t: None)
        for b in nxt[:1]:
            b.job.begin()

    @pl.when(i == 14)
    def _():
        for b in blocks:
            b.forward()
        for b in nxt[1:]:
            b.job.begin()

    @pl.when((i >= 4) & (i < 4 + heads))
    def _():
        attend_forward_head(length, i - 4, qkv_ref.at[0], qkv_ref.at[1], vt_ref, sum_ref, log_ref)

    @pl.when(i == 4 + heads)
    def _():
        to_lanes(mixed_ref, sum_ref)
        load_o().wait()
        br = sum(nt(mixed_ref[:, p * half : (p + 1) * half], wo_buf[p]) for p in range(hn))
        mid = br[:, width:].astype(bf16)
        mid_ref[...] = mid
        hidden_ref[...] = br[:, :width] + nn(mid, out_ref[number])

    @pl.when(i == 5 + heads)
    def _():
        def body(rows, start):
            v = real(x_buf[rows, :] + hidden_ref[rows, :], start, length)
            hidden_ref[rows, :] = v
            unit, _ = unit_of(v, width)
            ln2_ref[rows, 0:width] = real(unit * gain[...] + bias[...], start, length).astype(bf16)

        by_rows(n, 32, body)
        up_mid = nt(ln2_ref[:, 0:width], up_ref[number])
        lane = lax.broadcasted_iota(jnp.int32, (n, EXTRA - RANK), 1)
        ln2_ref[:, width : width + RANK] = up_mid.astype(bf16)
        ln2_ref[:, width + RANK :] = (lane == 0).astype(bf16)
        for b in blocks:
            b.exchange()
        save_qkv().wait()
        mine_z[0].wait()
        mine_a().wait()
        for d in range(1, tn):
            to_line(d).wait_send()
            p = lax.rem(z + tn - d, tn)
            comm.copy(small[d - 1], a2.at[p], ax.at[:, p], tensor=p).wait_recv()
        drain_z()
        for b in blocks:
            b.arrive()
        for w in qs + [o] + blocks:
            w.drain()
        for b in nxt:
            b.job.finish_first()


def attention(sizes, wq, wo, wu, wd, bq, bp, bu, bd, ub, index, first, out, x, vectors, up):
    fn, hn, tn = sizes
    rows, half = wo.shape
    units = wu.shape[-1]
    width = fn * rows
    length = x.shape[0]
    n = padded(length)
    heads = width // HEAD_DIM
    early = 1
    any_ = pl.BlockSpec(memory_space=pl.ANY)
    one = lambda s: pl.BlockSpec(s, lambda i: (0,) * len(s), pipeline_mode=pl.Buffered(1))
    shape = jax.ShapeDtypeStruct
    nsem = 4 * (tree_sems(fn) + 2) + 3 * (tn - 1) + (early + 2) * block_sems(fn)
    hbm = [
        ((3, hn, width + RANK, half), bf16),
        ((hn, width + RANK, half), bf16),
        ((tn, rows, units), bf16),
        ((2, tn, EXTRA, units), bf16),
        ((n, width), bf16),
        ((3, n, width), bf16),
    ]
    outs = [
        ((3, n, RANK), bf16),
        ((n, width), bf16),
        ((heads, n), f32),
        ((n, width), f32),
        ((n, width + EXTRA), bf16),
        ((n, RANK), bf16),
    ]
    return pl.pallas_call(
        functools.partial(attention_kernel, sizes),
        grid=(6 + heads,),
        in_specs=[any_] * 4
        + [one(v.shape) for v in (bq, bp, bu, bd, ub)]
        + [pl.BlockSpec(memory_space=pltpu.SMEM)]
        + [one(first.shape), one(out.shape), any_, one(vectors.shape), one(up.shape)],
        out_specs=(any_,) * len(hbm) + tuple(one(s) for s, _ in outs) + (any_,),
        out_shape=tuple(shape(*o) for o in hbm + outs) + (shape((tn, 2, width, units), bf16),),
        scratch_shapes=[
            pltpu.SemaphoreType.DMA((nsem,)),
            pltpu.SemaphoreType.DMA((nsem,)),
            pltpu.VMEM((3, hn, width + RANK, half), bf16),
            pltpu.VMEM((hn, width + RANK, half), bf16),
            pltpu.SemaphoreType.DMA((6,)),
            pltpu.SemaphoreType.DMA((5, 2)),
            pltpu.VMEM((3, rows, half), bf16),
            pltpu.VMEM((rows, half), bf16),
            pltpu.VMEM((rows, units), bf16),
            pltpu.VMEM((early, rows, units), bf16),
            pltpu.VMEM((3, hn, RANK, half), bf16),
            pltpu.VMEM((hn, RANK, half), bf16),
            pltpu.VMEM((tn, 2, EXTRA, units), bf16),
            pltpu.VMEM((3, n, width), bf16),
            pltpu.VMEM((n, width + RANK), bf16),
            pltpu.VMEM((width, n), f32),
            pltpu.VMEM((width, n), f32),
            pltpu.VMEM((n, width), f32),
            tail_shape(length, width),
            pltpu.SemaphoreType.DMA((2,)),
        ],
        compiler_params=params(collective_id=3, has_side_effects=True),
        name="attention",
    )(wq, wo, wu, wd, bq, bp, bu, bd, ub, index, first, out, x, vectors, up)


def gelu_both(v, g):
    c, a = 0.7978845608028654, 0.044715
    sq = v * v
    t = jnp.tanh(v * (c + (c * a) * sq))
    half = 0.5 * (1.0 + t)
    slope = half + (0.5 * v) * ((1.0 - t * t) * (c + (3.0 * c * a) * sq))
    return v * half, g * slope


def mlp_half(ln_ref, g_ref, wu_ref, wd_ref, act_ref, gb_ref, out_acc, g_acc, rows, first, between):
    before = nn(ln_ref[rows, :], wu_ref[...])
    g_act = nn(g_ref[rows, :], wd_ref[...])
    act, gb = gelu_both(before, g_act)
    act, gb = act.astype(bf16), gb.astype(bf16)
    act_ref[rows, :] = act
    gb_ref[rows, :] = gb
    between()
    o, g = nt(act, wd_ref[...]), nt(gb, wu_ref[...])

    @pl.when(first)
    def _():
        out_acc[rows, :] = o
        g_acc[rows, :] = g

    @pl.when(jnp.logical_not(first))
    def _():
        out_acc[rows, :] += o
        g_acc[rows, :] += g


def mlp_kernel(
    sizes,
    length,
    done,
    plan,
    ln_ref,
    cot_ref,
    hidden_ref,
    early,
    zw,
    ax,
    index,
    up_bank,
    down_bank,
    vectors,
    y_ref,
    gh_ref,
    g_up_in,
    g_down_out,
    g_units,
    late,
    send,
    recv,
    w_buf,
    w_sems,
    g_buf,
    tail,
    gx,
    act,
    gb,
    out_acc,
    g_acc,
    sem,
    own_buf,
):
    i = pl.program_id(0)
    fn, hn, tn = sizes
    f, h, z = lax.axis_index("fsdp"), lax.axis_index("heads"), lax.axis_index("tensor")
    n, width = hidden_ref.shape
    number = index[(f * hn + h) * tn + z]
    gain, dbias = vectors.at[2:3], vectors.at[4:5]
    main = slice(0, width)
    s, half = i // 2, lax.rem(i, 2)
    comm = Comm(send, recv)
    blocks = {b: Block(comm, sizes, zw, late.at[b], b, own_buf.at[b - done]) for b in range(done, tn)}
    resumed = [blocks[b] for b in range(done, min(done + 2, tn))]
    for b in resumed:
        b.job.first_done = True

    def loads(b):
        slot = b % 2
        return [
            pltpu.make_async_copy(late.at[b], w_buf.at[slot, :, pl.ds(0, width)], w_sems.at[slot, 0]),
            pltpu.make_async_copy(
                ax.at[:, lax.rem(z + b, tn)], w_buf.at[slot, :, pl.ds(width, EXTRA)], w_sems.at[slot, 1]
            ),
        ]

    @pl.when(i == 0)
    def _():
        c = Tokens(cot_ref, g_buf, tail, sem)
        c.start()
        for b in range(done):
            for w in loads(b):
                w.start()
        for b in resumed:
            b.mine().start()
        enter(sizes, f, h, z)
        for b in resumed:
            b.forward()
        for b in range(done + 2, tn):
            blocks[b].begin()
        c.wait()

        def body(rows, start):
            gx[rows, main] = g_buf[rows, :].astype(bf16)

        by_rows(n, 32, body)
        gx[:, width : width + RANK] = nt(gx[:, main], down_bank[number]).astype(bf16)
        gx[:, width + RANK :] = jnp.zeros((n, EXTRA - RANK), bf16)

    def events(steps):
        for at, what in steps:

            @pl.when(i == at)
            def _():
                for b, name in what:
                    if name == "load":
                        if b < tn:
                            if b in blocks:
                                blocks[b].arrive()
                            for w in loads(b):
                                w.start()
                    elif b in blocks:
                        getattr(blocks[b], name)()

    events(plan[0])

    for b in range(tn):

        @pl.when(i == 2 * b)
        def _():
            for w in loads(b):
                w.wait()

    slot = lax.rem(s, 2)
    rows = pl.ds(pl.multiple_of(half * (n // 2), n // 2), n // 2)
    mlp_half(ln_ref, gx, w_buf.at[slot, 0], w_buf.at[slot, 1], act, gb, out_acc, g_acc, rows, s == 0, lambda: events(plan[1]))

    @pl.when(half == 1)
    def _():
        g_units[0, s] = tn_(ln_ref[:, width : width + RANK], gb[...]).astype(bf16)
        g_units[1, s] = tn_(gx[:, width : width + RANK], act[...]).astype(bf16)

    @pl.when(i == pl.num_programs(0) - 1)
    def _():
        down_mid = out_acc[:, width : width + RANK].astype(bf16)
        g_up_mid = g_acc[:, width : width + RANK].astype(bf16)
        g_up_in[...] = tn_(g_up_mid, ln_ref[:, main]).astype(bf16)
        g_down_out[...] = tn_(down_mid, gx[:, main]).astype(bf16)
        out_acc[:, main] += nn(down_mid, down_bank[number])
        g_acc[:, main] += nn(g_up_mid, up_bank[number])

        def body(rows, start):
            v = hidden_ref[rows, :]
            out_acc[rows, main] += v + dbias[...]
            gh_ref[rows, :] = g_buf[rows, :] + real(
                norm_back(g_acc[rows, main], v, gain[...], width), start, length
            )

        by_rows(n, 32, body)
        c = Tokens(y_ref, out_acc, tail, sem, out=True)
        c.start()
        for b in blocks.values():
            b.drain()
        c.wait()


def mlp(sizes, ln, cot, hidden, early, zw, ax, index, up, down, vectors):
    fn, hn, tn = sizes
    n, width = hidden.shape
    depth = ln.shape[1]
    units = early.shape[-1]
    done = 1
    length = cot.shape[0]
    late = max(tn - done, 1)
    plan = (
        (
            (2, ((2, "exchange"),)),
            (3, ((2, "load"),)),
            (4, ((3, "forward"),)),
            (5, ((3, "exchange"),)),
        ),
        (
            (0, ((1, "exchange"),)),
            (1, ((1, "load"),)),
            (5, ((3, "load"),)),
        ),
    )
    any_ = pl.BlockSpec(memory_space=pl.ANY)
    one = lambda s: pl.BlockSpec(s, lambda t: (0,) * len(s), pipeline_mode=pl.Buffered(1))
    shape = jax.ShapeDtypeStruct
    nsem = late * block_sems(fn)
    return pl.pallas_call(
        functools.partial(mlp_kernel, sizes, length, done, plan),
        grid=(2 * tn,),
        in_specs=[
            one((n, depth)),
            any_,
            one((n, width)),
            any_,
            any_,
            any_,
            pl.BlockSpec(memory_space=pltpu.SMEM),
            one(up.shape),
            one(down.shape),
            one(vectors.shape),
        ],
        out_specs=(
            any_,
            one((n, width)),
            one((RANK, width)),
            one((RANK, width)),
            one((2, tn, RANK, units)),
            any_,
        ),
        out_shape=(
            shape((length, 1, width), f32),
            shape((n, width), f32),
            shape((RANK, width), bf16),
            shape((RANK, width), bf16),
            shape((2, tn, RANK, units), bf16),
            shape(early.shape, bf16),
        ),
        input_output_aliases={3: 6 - 1},
        scratch_shapes=[
            pltpu.SemaphoreType.DMA((nsem,)),
            pltpu.SemaphoreType.DMA((nsem,)),
            pltpu.VMEM((2, 2, depth, units), bf16),
            pltpu.SemaphoreType.DMA((2, 2)),
            pltpu.VMEM((n, width), f32),
            tail_shape(length, width),
            pltpu.VMEM((n, depth), bf16),
            pltpu.VMEM((n, units), bf16),
            pltpu.VMEM((n, units), bf16),
            pltpu.VMEM((n, depth), f32),
            pltpu.VMEM((n, depth), f32),
            pltpu.SemaphoreType.DMA((2,)),
            pltpu.VMEM((late,) + zw.shape[1:], bf16),
        ],
        compiler_params=params(collective_id=4, has_side_effects=True),
        name="mlp",
    )(ln, cot, hidden, early, zw, ax, index, up, down, vectors)


def branch_back_kernel(place, index, gh_ref, w_ref, out_bank, mixed_ref, mid_ref, g_up_in, g_down_out, gm_ref, grads, gx):
    n, width = gh_ref.shape
    half = w_ref.shape[-1]

    def body(rows, start):
        gx[rows, 0:width] = gh_ref[rows, :].astype(bf16)

    by_rows(n, 32, body)
    g_mid = nt(gx[:, 0:width], out_bank[index[place()]]).astype(bf16)
    gx[:, width:] = g_mid
    grads[...] = jnp.zeros_like(grads)
    grads[0:RANK, :] = tn_(mid_ref[...], gx[:, 0:width]).astype(bf16)
    grads[RANK : 2 * RANK, :] = g_up_in[...]
    grads[2 * RANK : 3 * RANK, :] = g_down_out[...]
    grads[3 * RANK : 4 * RANK, :] = tn_(g_mid, mixed_ref[...]).astype(bf16)
    for p in range(w_ref.shape[0]):
        gm_ref[:, p * half : (p + 1) * half] = nn(gx[...], w_ref[p]).astype(bf16)


def branch_back(rows, place, index, gh, w, out, mixed, mid, g_up_in, g_down_out):
    n, width = gh.shape
    return pl.pallas_call(
        functools.partial(branch_back_kernel, place),
        in_specs=[pl.BlockSpec(memory_space=pltpu.SMEM)] + [pl.BlockSpec(memory_space=pltpu.VMEM)] * 7,
        out_shape=(
            jax.ShapeDtypeStruct((n, width), bf16),
            jax.ShapeDtypeStruct((rows, width), bf16),
        ),
        scratch_shapes=[pltpu.VMEM((n, width + RANK), bf16)],
        compiler_params=params(),
        name="branch_back",
    )(index, gh, w, out, mixed, mid, g_up_in, g_down_out)


def add_by_adapter(pick, parts):
    width = parts.shape[-1]
    if parts.shape[-2] % 16:
        parts = parts.astype(f32)
    return nn(pick[...], parts.reshape(-1, width).astype(bf16))


def picks(adapters, count, rows):
    shape = (count * rows, adapters.shape[0] * rows)
    place = jnp.repeat(adapters * rows, rows) + jnp.tile(jnp.arange(rows), adapters.shape[0])
    return (lax.broadcasted_iota(jnp.int32, shape, 0) == place[None, :]).astype(bf16)


def line_copies(comm, tn, z, here, sems, own=None):
    up, down = sems

    def send(sem, block, to, src=None):
        return comm.copy(sem, here(block) if src is None else src, here(block), tensor=to)

    def begin():
        @pl.when(z < tn - 1)
        def _():
            send(up[0], z, z + 1, own).start()

        @pl.when(z > 0)
        def _():
            send(down[0], z, z - 1, own).start()

    def step(k, then):
        @pl.when(z - 1 - k >= 0)
        def _():
            b = z - 1 - k
            comm.copy(up[k], here(b), here(b), tensor=z - 1).wait_recv()
            if k + 1 < tn - 1:

                @pl.when(z < tn - 1)
                def _():
                    send(up[k + 1], b, z + 1).start()

            then(b)

        @pl.when(z + 1 + k < tn)
        def _():
            b = z + 1 + k
            comm.copy(down[k], here(b), here(b), tensor=z + 1).wait_recv()
            if k + 1 < tn - 1:

                @pl.when(z > 0)
                def _():
                    send(down[k + 1], b, z - 1).start()

            then(b)

    def drain():
        for k in range(tn - 1):

            @pl.when((z < tn - 1) & (z - k >= 0))
            def _():
                send(up[k], z, z + 1).wait_send()

            @pl.when((z > 0) & (z + k < tn))
            def _():
                send(down[k], z, z - 1).wait_send()

    return begin, step, drain


class Reduce:
    def __init__(self, sizes, count, comm, hot, local, a, out, ra, dense, b=None, out_b=None, rb=None, hot_b=None):
        fn, hn, tn = sizes
        f, h, z = lax.axis_index("fsdp"), lax.axis_index("heads"), lax.axis_index("tensor")
        self.fn, self.hn, self.tn, self.f, self.h, self.z = fn, hn, tn, f, h, z
        self.count, self.comm, self.hot, self.hot_b, self.local = count, comm, hot, hot_b, local
        self.a, self.out, self.ra, self.dense, self.b, self.out_b, self.rb = a, out, ra, dense, b, out_b, rb
        self.piece = ra.shape[1]
        self.s_first = [comm.new() for _ in range(fn - 1)]
        s_line = ([comm.new() for _ in range(tn - 1)], [comm.new() for _ in range(tn - 1)])
        self.s_core = [comm.new() for _ in range(tn)]
        self.s_last = comm.new()
        self.sent = []
        per = count // hn
        self.mine, self.theirs = pl.ds(h * per, per), pl.ds((1 - h) * per, per)

        def slot(o, r):
            start, size = (0, per) if r is None else r
            return out.at[o, pl.ds(h * per + start, size)]

        self.spread = Rows(comm, fn, f, slot, per, lambda: dense.at[self.mine], align=1)
        self.begin, self.line, self.drain_line = line_copies(
            comm, tn, z, lambda t: self.group(t, h), s_line
        )
        if b is not None:
            self.s_first_b = [comm.new() for _ in range(tn - 1)]
            self.s_core_b = comm.new()

            def slot_b(o, r):
                start, size = (0, tn) if r is None else r
                return rb.at[h, o, pl.ds(start, size)]

            self.spread_b = Rows(comm, fn, f, slot_b, tn, lambda: rb.at[h, f], align=1)

    def group(self, z, h):
        return self.ra.at[pl.ds((z * self.hn + h) * self.fn, self.fn)]

    def one(self, z, h, f):
        return self.ra.at[(z * self.hn + h) * self.fn + f]

    def rows(self, f):
        return self.a.at[pl.ds(pl.multiple_of(f * self.piece, 8), self.piece)]

    def send(self, make):
        make().start()
        self.sent.append(make)

    def own(self):
        copies = [pltpu.make_async_copy(self.rows(self.f), self.one(self.z, self.h, self.f), self.local.at[0])]
        if self.b is not None:
            copies.append(
                pltpu.make_async_copy(self.b.at[:, 0], self.rb.at[self.h, self.f, self.z], self.local.at[1])
            )
        return copies

    def start(self):
        f, h, z, comm = self.f, self.h, self.z, self.comm
        for m in range(1, self.fn):
            self.send(
                lambda m=m: comm.copy(
                    self.s_first[m - 1], self.rows(f ^ m), self.one(z, h, f), fsdp=f ^ m
                )
            )
        if self.b is not None:
            for d in range(1, self.tn):
                self.send(
                    lambda d=d: comm.copy(
                        self.s_first_b[d - 1],
                        self.b.at[:, d],
                        self.rb.at[h, f, z],
                        tensor=lax.rem(z + d, self.tn),
                    )
                )
        for c in self.own():
            c.start()

    def second(self):
        f, h, z, comm = self.f, self.h, self.z, self.comm
        for c in self.own():
            c.wait()
        for m in range(1, self.fn):
            b = self.one(z, h, f ^ m)
            comm.copy(self.s_first[m - 1], b, b, fsdp=f ^ m).wait_recv()
        self.begin()
        self.to_core(z).start()
        if self.b is not None:
            for d in range(1, self.tn):
                p = lax.rem(z + self.tn - d, self.tn)
                b = self.rb.at[h, f, p]
                comm.copy(self.s_first_b[d - 1], b, b, tensor=p).wait_recv()
            self.spread_b.begin()

    def to_core(self, block):
        b = self.group(block, self.h)
        return pltpu.make_async_remote_copy(
            src_ref=b,
            dst_ref=b,
            send_sem=self.comm.send.at[self.s_core[0] + block],
            recv_sem=self.comm.recv.at[self.s_core[0] + block],
            device_id={"heads": 1 - self.h},
            device_id_type=MESH,
        )

    def line_step(self, k):
        if k < self.tn - 1:
            self.line(k, lambda b: self.to_core(b).start())

    def forward_b(self):
        self.spread_b.forward_all()

    def exchange_b(self):
        self.spread_b.settle()
        b = self.rb.at[self.h]
        self.send(lambda: self.comm.copy(self.s_core_b, b, b, heads=1 - self.h))

    def fourth(self):
        h = self.h
        for k in range(self.tn):
            b = self.group(k, 1 - h)
            self.comm.copy(self.s_core[k], b, b, heads=1 - h).wait_recv()
        total = add_by_adapter(self.hot, self.ra[...])
        self.dense[...] = total.reshape(self.dense.shape).astype(bf16)
        self.spread.begin()
        self.last().start()

    def last(self):
        return pltpu.make_async_copy(
            self.dense.at[self.mine], self.out.at[self.f, self.mine], self.local.at[0]
        )

    def fifth(self):
        b = self.rb.at[1 - self.h]
        self.comm.copy(self.s_core_b, b, b, heads=1 - self.h).wait_recv()
        for k in range(2):
            total = add_by_adapter(self.hot_b, self.rb[:, :, :, k, :, :])
            self.out_b[k][...] = total.reshape(self.out_b[k].shape)

    def sixth(self):
        self.spread.forward_all()

    def seventh(self):
        self.last().wait()
        self.spread.settle()
        b = self.out.at[:, self.mine]
        self.send(lambda: self.comm.copy(self.s_last, b, b, heads=1 - self.h))

    def finish(self):
        h = self.h
        b = self.out.at[:, self.theirs]
        self.comm.copy(self.s_last, b, b, heads=1 - h).wait_recv()
        for make in self.sent:
            make().wait_send()
        self.drain_line()
        self.spread.drain()
        if self.b is not None:
            self.spread_b.drain()
        for k in range(self.tn):
            self.to_core(k).wait_send()


def reduce_sems(sizes, both):
    fn, hn, tn = sizes
    nb = bits_of(fn)
    tree = nb + 2 * (fn - 1 - nb)
    n = fn - 1 + 2 * (tn - 1) + tn + 1 + tree
    return n + (tn - 1 + 1 + tree if both else 0)


def enter_reduce(sizes, f, h, z):
    fn, hn, tn = sizes
    barrier = pltpu.get_barrier_semaphore()
    for m in range(1, fn):
        pl.semaphore_signal(barrier, 1, device_id={"fsdp": f ^ m}, device_id_type=MESH)
    pl.semaphore_signal(barrier, 1, device_id={"heads": 1 - h}, device_id_type=MESH)
    for d in range(1, tn):
        pl.semaphore_signal(barrier, 1, device_id={"tensor": lax.rem(z + d, tn)}, device_id_type=MESH)
    pl.semaphore_wait(barrier, fn - 1 + 1 + tn - 1)


def piece_rows(rows, fn):
    return -(-rows // (8 * fn)) * 8


def reduce_shapes(sizes, count, width, piece, units, both):
    fn, hn, tn = sizes
    n = fn * hn * tn
    shapes = [
        pltpu.SemaphoreType.DMA((reduce_sems(sizes, both),)),
        pltpu.SemaphoreType.DMA((reduce_sems(sizes, both),)),
        pltpu.SemaphoreType.DMA((2,)),
        pltpu.VMEM((n, piece, width), bf16),
        pltpu.VMEM((count, piece, width), bf16),
    ]
    if both:
        shapes.append(pltpu.VMEM((hn, fn, tn, 2, RANK, units), bf16))
    return shapes


def attend_back_kernel(
    sizes, length, count, plan, hot, hot_b, q_ref, k_ref, v_ref, do_ref, log_ref, a, b, out_ref, sums, sums_u, sums_d, send, recv, local, ra, dense, rb, kt_ref, dq_ref, dk_ref, dv_ref
):
    head = pl.program_id(0)
    job = Reduce(sizes, count, Comm(send, recv), hot, local, a, sums, ra, dense, b, (sums_u, sums_d), rb, hot_b)

    @pl.when(head == 0)
    def _():
        enter_reduce(sizes, job.f, job.h, job.z)
        job.start()
        to_rows(kt_ref, k_ref.at[0])

        def clear(at):
            for r in (dk_ref, dv_ref):
                r[:, at] = jnp.zeros((r.shape[0], LANES), f32)

        columns(dk_ref.shape[1], clear)

    for at, what in plan:

        @pl.when(head == at)
        def _():
            for name, *more in what:
                getattr(job, name)(*more)

    attend_back_head(
        length, head, q_ref.at[0], k_ref.at[0], v_ref.at[0], do_ref, log_ref, kt_ref, dq_ref, dk_ref, dv_ref
    )

    @pl.when(head == pl.num_programs(0) - 1)
    def _():
        to_lanes(out_ref.at[0], dq_ref)

        def cast(at):
            out_ref[1, :, at] = dk_ref[:, at].astype(bf16)
            out_ref[2, :, at] = dv_ref[:, at].astype(bf16)

        columns(dk_ref.shape[1], cast)
        job.finish()


def attend_back(sizes, length, count, hot, hot_b, qkv, do, log, a, b):
    fn, hn, tn = sizes
    _, n, width = qkv.shape
    heads = width // HEAD_DIM
    units = b.shape[-1]
    piece = a.shape[0] // fn
    plan = (
        (2, (("second",),)),
        (5, (("line_step", 0),)),
        (7, (("line_step", 1), ("forward_b",))),
        (9, (("line_step", 2), ("exchange_b",))),
        (11, (("fourth",),)),
        (12, (("fifth",),)),
        (13, (("sixth",),)),
        (15, (("seventh",),)),
    )
    any_ = pl.BlockSpec(memory_space=pl.ANY)
    one = lambda j: pl.BlockSpec((1, n, width), lambda h: (j, 0, 0), pipeline_mode=pl.Buffered(1))
    return pl.pallas_call(
        functools.partial(attend_back_kernel, sizes, length, count, plan),
        grid=(heads,),
        in_specs=[
            whole(hot.shape),
            whole(hot_b.shape),
            one(0),
            one(1),
            one(2),
            whole((n, width)),
            whole((heads, n)),
            any_,
            any_,
        ],
        out_specs=(whole((3, n, width)), any_) + (whole((count, RANK, units)),) * 2,
        out_shape=(
            jax.ShapeDtypeStruct((3, n, width), bf16),
            jax.ShapeDtypeStruct((fn, count, piece, width), bf16),
        )
        + (jax.ShapeDtypeStruct((count, RANK, units), f32),) * 2,
        scratch_shapes=reduce_shapes(sizes, count, width, piece, units, True)
        + [pltpu.VMEM((width, n), f32)] * 2
        + [pltpu.VMEM((n, width), f32)] * 2,
        compiler_params=params(collective_id=1, has_side_effects=True),
        name="attend_back",
    )(hot, hot_b, qkv, qkv, qkv, do, log, a, b)


def project_back_kernel(
    sizes,
    count,
    hot,
    index,
    before,
    g_ref,
    w_any,
    first_ref,
    mid_ref,
    ln_ref,
    gh_any,
    x_ref,
    vectors,
    gi_ref,
    sums,
    a,
    g_proj_out,
    g_up_in,
    g_down_out,
    g_proj_in,
    send,
    recv,
    local,
    ra,
    dense,
    w_buf,
    gh_buf,
    w_sems,
    x_buf,
    tail,
    acc,
    grads,
    g_mid,
    sem,
    before_buf,
):
    i = pl.program_id(0)
    length = x_ref.shape[0]
    n, width = ln_ref.shape
    half = w_buf.shape[-1]
    gain = vectors.at[0:1]
    parts = w_buf.shape[1]
    load = Tokens(x_ref, x_buf, tail, sem)
    job = Reduce(sizes, count, Comm(send, recv), hot, local, a, sums, ra, dense)
    number = index[(job.f * job.hn + job.h) * job.tn + job.z]

    def load_w(j):
        return pltpu.make_async_copy(w_any.at[j], w_buf.at[j], w_sems.at[j])

    load_gh = pltpu.make_async_copy(gh_any, gh_buf, w_sems.at[3])
    load_before = pltpu.make_async_copy(before, before_buf, w_sems.at[5])
    save = pltpu.make_async_copy(grads, a, w_sems.at[4])

    @pl.when(i == 0)
    def _():
        for j in range(3):
            load_w(j).start()
        load.start()
        load_gh.start()
        load_before.start()
        enter_reduce(sizes, job.f, job.h, job.z)
        if grads.shape[0] > 6 * RANK:
            grads[6 * RANK :, :] = jnp.zeros((grads.shape[0] - 6 * RANK, width), bf16)
        for j in range(3):
            load_w(j).wait()

        def small(j, _):
            m = sum(
                nt(g_ref[j, :, p * half : (p + 1) * half], w_buf[j, p, pl.ds(width, RANK), :])
                for p in range(parts)
            ).astype(bf16)
            g_mid[j] = m
            at = pl.ds(pl.multiple_of((3 + j) * RANK, RANK), RANK)
            grads[at, :] = tn_(mid_ref[j], g_ref[j]).astype(bf16)
            return 0

        lax.fori_loop(0, 3, small, 0)
        mids = jnp.concatenate([g_mid[j].astype(f32).T for j in range(3)]).astype(bf16)
        grads[0 : 3 * RANK, :] = nn(mids, ln_ref[...]).astype(bf16)
        save.start()
        save.wait()
        job.start()

    @pl.when(i == 2)
    def _():
        job.second()

    @pl.when(i == 3)
    def _():
        job.line_step(0)

    @pl.when((i > 0) & (i < 4))
    def _():
        j = i - 1
        r = nn(g_mid[j], first_ref[j, number])
        for p in range(parts):
            r = r + nt(g_ref[j, :, p * half : (p + 1) * half], w_buf[j, p, pl.ds(0, width), :])

        @pl.when(i == 1)
        def _():
            acc[...] = r

        @pl.when(i > 1)
        def _():
            acc[...] += r

    @pl.when(i == 4)
    def _():
        job.line_step(1)
        load.wait()
        load_gh.wait()

        def body(rows, start):
            v = x_buf[rows, :]
            acc[rows, :] = gh_buf[rows, :] + norm_back(acc[rows, :], v, gain[...], width)

        by_rows(n, 32, body)
        c = Tokens(gi_ref, acc, tail, sem, out=True)
        c.start()
        for k in range(2, sizes[2] - 1):
            job.line_step(k)
        job.fourth()
        load_before.wait()
        piece = before_buf.shape[2]

        def rows_of(k, r):
            k = k * RANK + r * 8
            return before_buf[k // piece, :, k % piece : k % piece + 8, :].astype(f32)

        for k, dst in enumerate((g_proj_out, g_up_in, g_down_out)):
            for r in range(2):
                dst[:, r * 8 : r * 8 + 8, :] = rows_of(k, r)

        for p in range(parts):

            @pl.when(job.h == p)
            def _():
                for r in range(2):
                    g_proj_in[:, r * 8 : r * 8 + 8, :] = rows_of(3, r)[:, :, p * half : (p + 1) * half]

        job.sixth()
        job.seventh()
        job.finish()
        c.wait()


def project_back(sizes, count, hot, index, before, g, w, first, mid, ln, gh, x, vectors):
    fn, hn, tn = sizes
    n, width = ln.shape
    half = w.shape[-1]
    length = x.shape[0]
    piece = piece_rows(6 * RANK, fn)
    any_ = pl.BlockSpec(memory_space=pl.ANY)
    one = lambda s: pl.BlockSpec(s, lambda t: (0,) * len(s), pipeline_mode=pl.Buffered(1))
    shape = jax.ShapeDtypeStruct
    return pl.pallas_call(
        functools.partial(project_back_kernel, sizes, count),
        grid=(5,),
        in_specs=[
            one(hot.shape),
            pl.BlockSpec(memory_space=pltpu.SMEM),
            any_,
            one(g.shape),
            any_,
            one(first.shape),
            one(mid.shape),
            one((n, width)),
            any_,
            any_,
            one(vectors.shape),
        ],
        out_specs=(any_, any_, any_) + (one((count, RANK, width)),) * 3 + (one((count, RANK, half)),),
        out_shape=(
            shape((length, 1, width), f32),
            shape((fn, count, piece, width), bf16),
            shape((fn * piece, width), bf16),
        )
        + (shape((count, RANK, width), f32),) * 3
        + (shape((count, RANK, half), f32),),
        scratch_shapes=reduce_shapes(sizes, count, width, piece, 0, False)
        + [
            pltpu.VMEM(w.shape, bf16),
            pltpu.VMEM((n, width), f32),
            pltpu.SemaphoreType.DMA((6,)),
            pltpu.VMEM((n, width), f32),
            tail_shape(length, width),
            pltpu.VMEM((n, width), f32),
            pltpu.VMEM((fn * piece, width), bf16),
            pltpu.VMEM(mid.shape, bf16),
            pltpu.SemaphoreType.DMA((2,)),
            pltpu.VMEM(before.shape, bf16),
        ],
        compiler_params=params(collective_id=2, has_side_effects=True),
        name="qkv_back",
    )(hot, index, before, g, w, first, mid, ln, gh, x, vectors)


def per_device(
    inputs,
    cotangent,
    image_adapter_index,
    first_norm_gain,
    first_norm_bias,
    second_norm_gain,
    second_norm_bias,
    query_key_value_weight,
    attention_output_weight,
    up_weight,
    down_weight,
    up_projection_bias,
    down_projection_bias,
    query_key_value_adapter_first,
    query_key_value_adapter_second,
    projection_adapter_first,
    projection_adapter_second,
    up_adapter_first,
    up_adapter_second,
    down_adapter_first,
    down_adapter_second,
):
    sizes = tuple(lax.axis_size(a) for a in ("fsdp", "heads", "tensor"))
    fn, hn, tn = sizes
    f, h, z = (lax.axis_index(a) for a in ("fsdp", "heads", "tensor"))
    images, length, width = inputs.shape
    assert images == 1 and hn == 2
    count = query_key_value_adapter_first.shape[1]
    units = up_weight.shape[-1]
    x, cot = jnp.swapaxes(inputs, 0, 1), jnp.swapaxes(cotangent, 0, 1)
    vectors = jnp.concatenate(
        [
            first_norm_gain,
            first_norm_bias,
            second_norm_gain,
            second_norm_bias,
            down_projection_bias.astype(f32),
        ]
    ).reshape(5, width)
    index = image_adapter_index
    qkv_in = jnp.swapaxes(query_key_value_adapter_first, 2, 3)
    u_in = jnp.swapaxes(up_adapter_first, 1, 2)
    wq, wo, zw, ax, ln1, qkv, qkv_mid, mixed, log, hidden, ln2, proj_mid, early = attention(
        sizes,
        jnp.swapaxes(query_key_value_weight, 0, 1),
        attention_output_weight,
        up_weight,
        down_weight,
        query_key_value_adapter_second,
        jnp.swapaxes(projection_adapter_first, 1, 2),
        up_adapter_second,
        down_adapter_first,
        jnp.pad(up_projection_bias[None], ((0, EXTRA - RANK - 1), (0, 0))),
        index,
        qkv_in,
        projection_adapter_second,
        x,
        vectors,
        u_in,
    )
    y, g_hidden, g_up_in, g_down_out, g_units, _ = mlp(
        sizes, ln2, cot, hidden, early, zw, ax, index, u_in, down_adapter_second, vectors
    )
    g_mixed, grads = branch_back(
        piece_rows(4 * RANK, fn) * fn,
        lambda: (lax.axis_index("fsdp") * hn + lax.axis_index("heads")) * tn + lax.axis_index("tensor"),
        index,
        g_hidden,
        wo,
        projection_adapter_second,
        mixed,
        proj_mid,
        g_up_in,
        g_down_out,
    )
    by_place = image_adapter_index.reshape(fn, hn, tn)
    order = jnp.transpose(by_place, (2, 1, 0)).reshape(-1)
    order_b = jnp.transpose(by_place, (1, 0, 2)).reshape(-1)
    pick = picks(order, count, piece_rows(4 * RANK, fn))
    pick_b = picks(order_b, count, RANK)
    g_qkv, sums, g_up_out, g_down_in = attend_back(
        sizes, length, count, pick, pick_b, qkv, g_mixed, log, grads, g_units
    )
    g_x, last, _, g_proj_out, g_up_in, g_down_out, g_proj_in = project_back(
        sizes,
        count,
        picks(order, count, piece_rows(6 * RANK, fn)),
        index,
        sums,
        g_qkv,
        wq,
        qkv_in,
        qkv_mid,
        ln1,
        g_hidden,
        x,
        vectors,
    )
    last = jnp.moveaxis(last, 0, 1).reshape(count, -1, width)
    last = jnp.moveaxis(last[:, : 6 * RANK].reshape(count, 6, RANK, width), 0, 1).astype(f32)
    half = width // hn
    return (
        jnp.swapaxes(y, 0, 1),
        jnp.swapaxes(g_x, 0, 1),
        jnp.swapaxes(last[:3], 2, 3),
        lax.dynamic_slice_in_dim(last[3:], h * half, half, axis=-1),
        jnp.swapaxes(g_proj_in, 1, 2),
        g_proj_out,
        jnp.swapaxes(g_up_in, 1, 2),
        g_up_out,
        g_down_in,
        g_down_out,
    )


def solution(mesh):
    in_specs = (
        P(("fsdp", "heads", "tensor"), None, None),
        P(("fsdp", "heads", "tensor"), None, None),
        P(),
        P(),
        P(),
        P(),
        P(),
        P("fsdp", None, "heads"),
        P("fsdp", "heads"),
        P("fsdp", "tensor"),
        P("fsdp", "tensor"),
        P("tensor"),
        P(),
        P(),
        P(None, None, None, "heads"),
        P(None, "heads", None),
        P(),
        P(),
        P(None, None, "tensor"),
        P(None, None, "tensor"),
        P(),
    )
    out_specs = (
        P(("fsdp", "heads", "tensor"), None, None),
        P(("fsdp", "heads", "tensor"), None, None),
        P(),
        P(None, None, None, "heads"),
        P(None, "heads", None),
        P(),
        P(),
        P(None, None, "tensor"),
        P(None, None, "tensor"),
        P(),
    )
    return jax.shard_map(
        per_device, mesh=mesh, in_specs=in_specs, out_specs=out_specs, check_vma=False
    )
```

```python
import functools
import jax
import jax.numpy as jnp
from jax import lax
from jax.experimental import pallas as pl
from jax.experimental.pallas import tpu as pltpu
from jax.sharding import PartitionSpec as P

HEAD_DIM = 72
norm_eps = 1e-06
f32 = jnp.float32
bf16 = jnp.bfloat16
MESH = pl.DeviceIdType.MESH


RANK = 16
EXTRA = 32


def padded(n):
    return -(-n // 16) * 16


def row_sums(v):
    return jnp.sum(v, axis=-1, keepdims=True)


class Tokens:
    def __init__(self, hbm, buf, tail, sems, out=False):
        self.length = hbm.shape[0]
        self.buf, self.tail, self.out = buf, tail, out
        self.whole = self.length // 8 * 8
        pairs = [(hbm.at[0 : self.whole, 0, :], buf.at[0 : self.whole, 0 : hbm.shape[-1]])]
        if self.whole < self.length:
            pairs.append((hbm.at[self.whole : self.length, 0, :], tail))
        self.copies = [
            pltpu.make_async_copy(*((b, a) if out else (a, b)), sems.at[i]) for i, (a, b) in enumerate(pairs)
        ]

    def start(self):
        if self.out and self.whole < self.length:
            self.tail[...] = self.buf[self.whole : self.length, 0 : self.tail.shape[-1]]
        for c in self.copies:
            c.start()

    def wait(self):
        for c in self.copies:
            c.wait()
        if not self.out:
            rest = self.buf.shape[0] - self.length
            zeros = jnp.zeros((rest, self.buf.shape[1]), f32)
            if self.whole < self.length:
                zeros = jnp.concatenate([self.tail[...], zeros])
            self.buf[self.whole :, :] = zeros


def tail_shape(length, width):
    return pltpu.VMEM((max(length % 8, 1), width), f32)


def unit_of(v, width):
    mean = row_sums(v) * (1.0 / width)
    centred = v - mean
    inverse = lax.rsqrt(row_sums(centred * centred) * (1.0 / width) + norm_eps)
    return centred * inverse, inverse


def by_rows(n, step, body):
    def one(r, _):
        body(pl.ds(pl.multiple_of(r * step, step), step), r * step)
        return 0

    lax.fori_loop(0, n // step, one, 0)


def real(v, start, length):
    row = lax.broadcasted_iota(jnp.int32, v.shape, 0) + start
    return jnp.where(row < length, v, 0.0)


def normalize_into(dst, src, gain, bias, length):
    n, width = src.shape

    def body(rows, start):
        unit, _ = unit_of(src[rows, :], width)
        dst[rows, 0:width] = real(unit * gain[...] + bias[...], start, length).astype(bf16)

    by_rows(n, 32, body)


def norm_back(grad, v, gain, width):
    unit, inverse = unit_of(v, width)
    e = grad * gain
    return inverse * (e - row_sums(e) * (1.0 / width) - unit * (row_sums(e * unit) * (1.0 / width)))


LANES = 128
SCALE = HEAD_DIM**-0.5
LOG2E = 1.4426950408889634


def nn(a, b):
    return lax.dot_general(a, b, (((1,), (0,)), ((), ())), preferred_element_type=f32)


def nt(a, b):
    return lax.dot_general(a, b, (((1,), (1,)), ((), ())), preferred_element_type=f32)


def tn_(a, b):
    return lax.dot_general(a, b, (((0,), (0,)), ((), ())), preferred_element_type=f32)


def whole(shape):
    return pl.BlockSpec(shape, lambda *_: (0,) * len(shape))


def params(limit=60, **more):
    return pltpu.CompilerParams(vmem_limit_bytes=limit << 20, **more)


def head_window(head, width):
    tile = jnp.minimum(head * HEAD_DIM // LANES, width // LANES - 2)
    return pl.ds(pl.multiple_of(tile * LANES, LANES), 2 * LANES), head * HEAD_DIM - tile * LANES


def only_head(values, start):
    lane = lax.broadcasted_iota(jnp.int32, values.shape, 1)
    return jnp.where((lane >= start) & (lane < start + HEAD_DIM), values, jnp.zeros_like(values))


def own_rows(head):
    return pl.ds(pl.multiple_of(head * HEAD_DIM, 8), HEAD_DIM)


def attend_forward_head(length, head, q_ref, k_ref, vt_ref, sum_ref, log_ref):
    win, start = head_window(head, q_ref.shape[-1])
    q = only_head(q_ref[:, win], start)
    v = vt_ref[own_rows(head), :].astype(bf16)
    s = nt(k_ref[:, win], q)
    key = lax.broadcasted_iota(jnp.int32, s.shape, 0)
    s = jnp.where(key < length, s, -1e30)
    top = jnp.max(s, axis=0, keepdims=True)
    p = jnp.exp2((s - top) * (SCALE * LOG2E))
    total = jnp.sum(p, axis=0, keepdims=True)
    sum_ref[own_rows(head), :] = nn(v, p.astype(bf16)) * (1.0 / total)
    log_ref[pl.ds(head, 1), :] = top * (SCALE * LOG2E) + jnp.log(total) * LOG2E


def attend_back_head(length, head, q_ref, k_ref, v_ref, do_ref, log_ref, kt_ref, dq_ref, dk_ref, dv_ref):
    win, start = head_window(head, q_ref.shape[-1])
    q = only_head(q_ref[:, win], start)
    k = k_ref[:, win]
    do = only_head(do_ref[:, win], start)
    s = nt(k, q)
    key = lax.broadcasted_iota(jnp.int32, s.shape, 0)
    p = jnp.exp2(jnp.where(key < length, s * (SCALE * LOG2E), -1e30) - log_ref[pl.ds(head, 1), :])
    dp = nt(v_ref[:, win], do)
    pd = p * dp
    ds = (pd - p * jnp.sum(pd, axis=0, keepdims=True)).astype(bf16)
    dv_ref[:, win] += nn(p.astype(bf16), do)
    dk_ref[:, win] += nn(ds, q) * SCALE
    dq_ref[own_rows(head), :] = nn(kt_ref[own_rows(head), :].astype(bf16), ds) * SCALE


def columns(width, body):
    def one(c, _):
        body(pl.ds(pl.multiple_of(c * LANES, LANES), LANES))
        return 0

    lax.fori_loop(0, width // LANES, one, 0)


def to_rows(dst, src):
    def body(at):
        dst[at, :] = src[:, at].astype(f32).T.astype(dst.dtype)

    columns(src.shape[1], body)


def to_lanes(dst, src):
    def body(at):
        dst[:, at] = src[at, :].T.astype(dst.dtype)

    columns(src.shape[0], body)


def bits_of(n):
    return n.bit_length() - 1


class Comm:
    def __init__(self, send, recv):
        self.send, self.recv, self.n = send, recv, 0

    def new(self):
        self.n += 1
        return self.n - 1

    def copy(self, i, src, dst, **where):
        return pltpu.make_async_remote_copy(
            src_ref=src,
            dst_ref=dst,
            send_sem=self.send.at[i],
            recv_sem=self.recv.at[i],
            device_id=where,
            device_id_type=MESH,
        )


def enter(axes_sizes, f, h, z):
    fn, hn, tn = axes_sizes
    barrier = pltpu.get_barrier_semaphore()
    count = 0
    for b in range(bits_of(fn)):
        pl.semaphore_signal(
            barrier, 1, device_id={"fsdp": f ^ (1 << b)}, device_id_type=MESH
        )
        count += 1
    pl.semaphore_signal(barrier, 1, device_id={"heads": 1 - h}, device_id_type=MESH)
    count += 1
    for d in range(1, tn):
        pl.semaphore_signal(
            barrier, 1, device_id={"tensor": lax.rem(z + d, tn)}, device_id_type=MESH
        )
        count += 1
    pl.semaphore_wait(barrier, count)


class Rows:
    def __init__(self, comm, fn, f, slot, rows, own, align=8):
        self.comm, self.fn, self.f, self.slot, self.own = comm, fn, f, slot, own
        self.nb = bits_of(fn)
        half = rows // 2 // align * align
        self.parts = ((0, half, list(range(self.nb))), (half, rows - half, list(range(self.nb))[::-1]))
        self.first = [comm.new() for _ in range(self.nb)]
        self.later = {}
        for p, (_, _, order) in enumerate(self.parts):
            for m in range(1, fn):
                last = max(order.index(b) for b in range(self.nb) if m >> b & 1)
                for b in order[last + 1 :]:
                    self.later[p, m, b] = comm.new()
        self.sent = []
        self.first_done = False

    def part(self, origin, p):
        start, size, _ = self.parts[p]
        return self.slot(origin, (start, size))

    def begin(self):
        for b in range(self.nb):
            self.send(
                lambda b=b: self.comm.copy(
                    self.first[b], self.own(), self.slot(self.f, None), fsdp=self.f ^ (1 << b)
                )
            )

    def _arrived(self, m, p):
        order = self.parts[p][2]
        last = max(order.index(b) for b in range(self.nb) if m >> b & 1)
        b = order[last]
        src = m ^ (1 << b)
        if src == 0:
            return None
        where = self.part(self.f ^ m, p)
        return self.comm.copy(self.later[p, src, b], where, where, fsdp=self.f ^ (1 << b))

    def forward(self, m):
        if m & (m - 1) == 0 and not self.first_done:
            b = bits_of(m)
            where = self.slot(self.f ^ m, None)
            self.comm.copy(self.first[b], where, where, fsdp=self.f ^ m).wait_recv()
        for p, (_, _, order) in enumerate(self.parts):
            if m & (m - 1):
                self._arrived(m, p).wait_recv()
            last = max(order.index(b) for b in range(self.nb) if m >> b & 1)
            for b in order[last + 1 :]:

                def onward(p=p, b=b):
                    where = self.part(self.f ^ m, p)
                    return self.comm.copy(self.later[p, m, b], where, where, fsdp=self.f ^ (1 << b))

                self.send(onward)

    def masks(self):
        return sorted(range(1, self.fn), key=lambda m: (bin(m).count("1"), m))

    def finish_first(self):
        for b in range(self.nb):
            where = self.slot(self.f ^ (1 << b), None)
            self.comm.copy(self.first[b], where, where, fsdp=self.f ^ (1 << b)).wait_recv()
        self.drain()

    def leaf(self, m):
        return not any(key[1] == m for key in self.later)

    def forward_all(self):
        for m in self.masks():
            if not self.leaf(m):
                self.forward(m)

    def settle(self):
        for m in self.masks():
            if self.leaf(m):
                self.forward(m)

    def send(self, make):
        make().start()
        self.sent.append(make)

    def drain(self):
        for make in self.sent:
            make().wait_send()


def tree_sems(fn):
    nb = bits_of(fn)
    return nb + 2 * (fn - 1 - nb)


class Bounce:
    def __init__(self, src, buf, dst, sem):
        self.load = pltpu.make_async_copy(src, buf, sem)
        self.save = pltpu.make_async_copy(buf, dst, sem)

    def start(self):
        self.load.start()

    def turn(self):
        self.load.wait()
        self.save.start()

    def wait(self):
        self.save.wait()


class Block:
    def __init__(self, comm, sizes, zw, dst, s, buf, own=None):
        fn, hn, tn = sizes
        f, h, z = lax.axis_index("fsdp"), lax.axis_index("heads"), lax.axis_index("tensor")
        rows = zw.shape[1]
        self.comm, self.dst, self.h, self.buf = comm, dst, h, buf
        t = lax.rem(z + s, tn)

        def slot(o, r):
            start, size = (0, rows) if r is None else r
            return dst.at[h, pl.ds(pl.multiple_of(o * rows + start, 8), size)]

        self.own = lambda: zw.at[t] if own is None else own
        self.slot = lambda: slot(f, None)
        self.job = Rows(comm, fn, f, slot, rows, self.own)
        self.local = comm.new()
        self.core = comm.new()

    def mine(self):
        return Bounce(self.own(), self.buf, self.slot(), self.comm.send.at[self.local])

    def to_core(self, which):
        b = self.dst.at[which]
        return self.comm.copy(self.core, b, b, heads=1 - self.h)

    def begin(self):
        self.job.begin()
        self.mine().start()

    def forward(self):
        self.mine().turn()
        self.job.forward_all()

    def exchange(self):
        self.job.settle()
        self.mine().wait()
        self.to_core(self.h).start()

    def arrive(self):
        self.to_core(1 - self.h).wait_recv()

    def drain(self):
        self.job.drain()
        self.to_core(self.h).wait_send()


def block_sems(fn):
    return tree_sems(fn) + 2


class Weight:
    def __init__(self, comm, fn, f, h, rows, own, dst, extra, own_sem, buf):
        self.comm, self.h, self.dst, self.extra = comm, h, dst, extra
        width = fn * rows
        self.main, self.more = pl.ds(0, width), pl.ds(width, RANK)

        def slot(o, r):
            start, size = (0, rows) if r is None else r
            return dst.at[h, pl.ds(pl.multiple_of(o * rows + start, 8), size)]

        self.job = Rows(comm, fn, f, slot, rows, lambda: own)
        self.core, self.core_extra = comm.new(), comm.new()
        self.mine = lambda: Bounce(own, buf, slot(f, None), own_sem.at[0])
        self.mine_extra = lambda: pltpu.make_async_copy(
            extra.at[h], dst.at[h, self.more], own_sem.at[1]
        )

    def start_extra(self):
        self.mine_extra().start()
        self.to_core_extra().start()

    def to_core_extra(self):
        return self.comm.copy(
            self.core_extra, self.extra.at[1 - self.h], self.dst.at[self.h, self.more], heads=1 - self.h
        )

    def to_core(self, which):
        b = self.dst.at[which, self.main]
        return self.comm.copy(self.core, b, b, heads=1 - self.h)

    def exchange(self):
        self.job.settle()
        self.mine().wait()
        self.to_core(self.h).start()

    def arrive(self):
        self.mine_extra().wait()
        where = self.dst.at[1 - self.h, self.more]
        self.comm.copy(self.core_extra, where, where, heads=1 - self.h).wait_recv()
        self.to_core(1 - self.h).wait_recv()

    def drain(self):
        self.job.drain()
        self.to_core(self.h).wait_send()
        self.to_core_extra().wait_send()


def attention_kernel(
    sizes,
    wq,
    wo,
    wu,
    wd,
    bq,
    bp,
    bu,
    bd,
    ub,
    index,
    first_ref,
    out_ref,
    x_ref,
    vectors,
    up_ref,
    oq,
    oo,
    zw,
    ax,
    ln_out,
    qkv_out,
    qmid_ref,
    mixed_ref,
    log_ref,
    hidden_ref,
    ln2_ref,
    mid_ref,
    got,
    send,
    recv,
    wq_buf,
    wo_buf,
    w_sems,
    own_sems,
    own_q,
    own_o,
    own_z,
    own_b,
    aq,
    ap,
    a2,
    qkv_ref,
    lnx_ref,
    vt_ref,
    sum_ref,
    x_buf,
    x_tail,
    x_sems,
):
    i = pl.program_id(0)
    fn, hn, tn = sizes
    f, h, z = lax.axis_index("fsdp"), lax.axis_index("heads"), lax.axis_index("tensor")
    rows, half = wo.shape
    length = x_ref.shape[0]
    n, width = mixed_ref.shape
    number = index[(f * hn + h) * tn + z]
    gain1, bias1, gain, bias = (vectors.at[k : k + 1] for k in range(4))
    heads = width // HEAD_DIM
    comm = Comm(send, recv)
    qs = [
        Weight(comm, fn, f, h, rows, wq.at[j], oq.at[j], aq.at[j], own_sems.at[j], own_q.at[j])
        for j in range(3)
    ]
    o = Weight(comm, fn, f, h, rows, wo, oo, ap, own_sems.at[3], own_o)
    line = ([comm.new() for _ in range(tn - 1)], [comm.new() for _ in range(tn - 1)])
    small = [comm.new() for _ in range(tn - 1)]
    blocks = [
        Block(comm, sizes, zw, got.at[b], b, own_b.at[b], own_z if b == 0 else None)
        for b in range(own_b.shape[0])
    ]
    nxt = [Block(comm, sizes, zw, got.at[b], b, own_z) for b in range(len(blocks), min(len(blocks) + 2, tn))]
    begin_z, step_z, drain_z = line_copies(comm, tn, z, lambda t: zw.at[t], line, own_z)
    mine_z = [Bounce(w, own_z, zw.at[z], own_sems.at[4, 0]) for w in (wu, wd)]
    mine_a = lambda: pltpu.make_async_copy(a2.at[z], ax.at[:, z], own_sems.at[4, 1])
    to_line = lambda d: comm.copy(
        small[d - 1], a2.at[lax.rem(z + d, tn)], ax.at[:, z], tensor=lax.rem(z + d, tn)
    )
    load_x = Tokens(x_ref, x_buf, x_tail, x_sems)
    load_q = lambda j: pltpu.make_async_copy(oq.at[j], wq_buf.at[j], w_sems.at[j])
    load_o = lambda: pltpu.make_async_copy(oo, wo_buf, w_sems.at[3])
    save_ln = lambda: pltpu.make_async_copy(lnx_ref.at[:, pl.ds(0, width)], ln_out, w_sems.at[4])
    save_qkv = lambda: pltpu.make_async_copy(qkv_ref, qkv_out, w_sems.at[5])

    @pl.when(i == 0)
    def _():
        load_x.start()
        for w in qs + [o]:
            w.mine().start()
        for p in range(2):

            @pl.when(h == p)
            def _():
                mine_z[p].start()

        for p in range(hn):
            k = index[(f * hn + p) * tn + z]
            for j in range(3):
                aq[j, p] = bq[j, k]
            ap[p] = bp[k]
        for t in range(tn):
            k = index[(f * hn + h) * tn + t]
            a2[t, 0, 0:RANK] = bu[k]
            a2[t, 1, 0:RANK] = bd[k]
            a2[t, 0, RANK:] = ub[...]
            a2[t, 1, RANK:] = jnp.zeros_like(ub)
        enter(sizes, f, h, z)
        qs[0].job.begin()
        qs[1].job.begin()
        mine_z[0].turn()
        begin_z()
        for w in qs + [o]:
            w.start_extra()
        mine_a().start()
        for d in range(1, tn):
            to_line(d).start()
        for w in qs + [o]:
            w.mine().turn()
        load_x.wait()
        normalize_into(lnx_ref, x_buf, gain1, bias1, length)
        save_ln().start()

    @pl.when(i == 1)
    def _():
        qs[0].job.forward_all()
        qs[2].job.begin()
        qs[1].job.forward_all()
        step_z(0, lambda t: None)
        qs[0].exchange()
        qs[0].arrive()
        load_q(0).start()

    @pl.when(i == 2)
    def _():
        qs[2].job.forward_all()
        o.job.begin()
        qs[1].exchange()
        qs[1].arrive()
        load_q(1).start()
        qs[2].exchange()

    @pl.when(i == 3)
    def _():
        if tn > 2:
            step_z(1, lambda t: None)
        qs[2].arrive()
        load_q(2).start()

    @pl.when((i >= 1) & (i < 4))
    def _():
        j = i - 1
        mid = nt(lnx_ref[:, 0:width], first_ref[j, number]).astype(bf16)
        qmid_ref[j] = mid
        load_q(j).wait()

        @pl.when(i == 1)
        def _():
            save_ln().wait()

        lnx_ref[:, width:] = mid
        for p in range(hn):
            qkv_ref[j, :, p * half : (p + 1) * half] = nn(lnx_ref[...], wq_buf[j, p]).astype(bf16)

    @pl.when(i == 4)
    def _():
        save_qkv().start()
        o.job.forward_all()
        blocks[0].begin()
        to_rows(vt_ref, qkv_ref.at[2])

    @pl.when(i == 8)
    def _():
        o.exchange()

    @pl.when(i == 11)
    def _():
        o.arrive()
        load_o().start()

    @pl.when(i == 9)
    def _():
        for k in range(2, tn - 1):
            step_z(k, lambda t: None)
        for b in nxt[:1]:
            b.job.begin()

    @pl.when(i == 14)
    def _():
        for b in blocks:
            b.forward()
        for b in nxt[1:]:
            b.job.begin()

    @pl.when((i >= 4) & (i < 4 + heads))
    def _():
        attend_forward_head(length, i - 4, qkv_ref.at[0], qkv_ref.at[1], vt_ref, sum_ref, log_ref)

    @pl.when(i == 4 + heads)
    def _():
        to_lanes(mixed_ref, sum_ref)
        load_o().wait()
        br = sum(nt(mixed_ref[:, p * half : (p + 1) * half], wo_buf[p]) for p in range(hn))
        mid = br[:, width:].astype(bf16)
        mid_ref[...] = mid
        hidden_ref[...] = br[:, :width] + nn(mid, out_ref[number])

    @pl.when(i == 5 + heads)
    def _():
        def body(rows, start):
            v = real(x_buf[rows, :] + hidden_ref[rows, :], start, length)
            hidden_ref[rows, :] = v
            unit, _ = unit_of(v, width)
            ln2_ref[rows, 0:width] = real(unit * gain[...] + bias[...], start, length).astype(bf16)

        by_rows(n, 32, body)
        up_mid = nt(ln2_ref[:, 0:width], up_ref[number])
        lane = lax.broadcasted_iota(jnp.int32, (n, EXTRA - RANK), 1)
        ln2_ref[:, width : width + RANK] = up_mid.astype(bf16)
        ln2_ref[:, width + RANK :] = (lane == 0).astype(bf16)
        for b in blocks:
            b.exchange()
        save_qkv().wait()
        mine_z[0].wait()
        mine_a().wait()
        for d in range(1, tn):
            to_line(d).wait_send()
            p = lax.rem(z + tn - d, tn)
            comm.copy(small[d - 1], a2.at[p], ax.at[:, p], tensor=p).wait_recv()
        drain_z()
        for b in blocks:
            b.arrive()
        for w in qs + [o] + blocks:
            w.drain()
        for b in nxt:
            b.job.finish_first()


def attention(sizes, wq, wo, wu, wd, bq, bp, bu, bd, ub, index, first, out, x, vectors, up):
    fn, hn, tn = sizes
    rows, half = wo.shape
    units = wu.shape[-1]
    width = fn * rows
    length = x.shape[0]
    n = padded(length)
    heads = width // HEAD_DIM
    early = 1
    any_ = pl.BlockSpec(memory_space=pl.ANY)
    one = lambda s: pl.BlockSpec(s, lambda i: (0,) * len(s), pipeline_mode=pl.Buffered(1))
    shape = jax.ShapeDtypeStruct
    nsem = 4 * (tree_sems(fn) + 2) + 3 * (tn - 1) + (early + 2) * block_sems(fn)
    hbm = [
        ((3, hn, width + RANK, half), bf16),
        ((hn, width + RANK, half), bf16),
        ((tn, rows, units), bf16),
        ((2, tn, EXTRA, units), bf16),
        ((n, width), bf16),
        ((3, n, width), bf16),
    ]
    outs = [
        ((3, n, RANK), bf16),
        ((n, width), bf16),
        ((heads, n), f32),
        ((n, width), f32),
        ((n, width + EXTRA), bf16),
        ((n, RANK), bf16),
    ]
    return pl.pallas_call(
        functools.partial(attention_kernel, sizes),
        grid=(6 + heads,),
        in_specs=[any_] * 4
        + [one(v.shape) for v in (bq, bp, bu, bd, ub)]
        + [pl.BlockSpec(memory_space=pltpu.SMEM)]
        + [one(first.shape), one(out.shape), any_, one(vectors.shape), one(up.shape)],
        out_specs=(any_,) * len(hbm) + tuple(one(s) for s, _ in outs) + (any_,),
        out_shape=tuple(shape(*o) for o in hbm + outs) + (shape((tn, 2, width, units), bf16),),
        scratch_shapes=[
            pltpu.SemaphoreType.DMA((nsem,)),
            pltpu.SemaphoreType.DMA((nsem,)),
            pltpu.VMEM((3, hn, width + RANK, half), bf16),
            pltpu.VMEM((hn, width + RANK, half), bf16),
            pltpu.SemaphoreType.DMA((6,)),
            pltpu.SemaphoreType.DMA((5, 2)),
            pltpu.VMEM((3, rows, half), bf16),
            pltpu.VMEM((rows, half), bf16),
            pltpu.VMEM((rows, units), bf16),
            pltpu.VMEM((early, rows, units), bf16),
            pltpu.VMEM((3, hn, RANK, half), bf16),
            pltpu.VMEM((hn, RANK, half), bf16),
            pltpu.VMEM((tn, 2, EXTRA, units), bf16),
            pltpu.VMEM((3, n, width), bf16),
            pltpu.VMEM((n, width + RANK), bf16),
            pltpu.VMEM((width, n), f32),
            pltpu.VMEM((width, n), f32),
            pltpu.VMEM((n, width), f32),
            tail_shape(length, width),
            pltpu.SemaphoreType.DMA((2,)),
        ],
        compiler_params=params(collective_id=3, has_side_effects=True),
        name="attention",
    )(wq, wo, wu, wd, bq, bp, bu, bd, ub, index, first, out, x, vectors, up)


def gelu_both(v, g):
    c, a = 0.7978845608028654, 0.044715
    sq = v * v
    t = jnp.tanh(v * (c + (c * a) * sq))
    half = 0.5 * (1.0 + t)
    slope = half + (0.5 * v) * ((1.0 - t * t) * (c + (3.0 * c * a) * sq))
    return v * half, g * slope


def mlp_half(ln_ref, g_ref, wu_ref, wd_ref, act_ref, gb_ref, out_acc, g_acc, rows, first, between):
    before = nn(ln_ref[rows, :], wu_ref[...])
    g_act = nn(g_ref[rows, :], wd_ref[...])
    act, gb = gelu_both(before, g_act)
    act, gb = act.astype(bf16), gb.astype(bf16)
    act_ref[rows, :] = act
    gb_ref[rows, :] = gb
    between()
    o, g = nt(act, wd_ref[...]), nt(gb, wu_ref[...])

    @pl.when(first)
    def _():
        out_acc[rows, :] = o
        g_acc[rows, :] = g

    @pl.when(jnp.logical_not(first))
    def _():
        out_acc[rows, :] += o
        g_acc[rows, :] += g


def mlp_kernel(
    sizes,
    length,
    done,
    plan,
    ln_ref,
    cot_ref,
    hidden_ref,
    early,
    zw,
    ax,
    index,
    up_bank,
    down_bank,
    vectors,
    y_ref,
    gh_ref,
    g_up_in,
    g_down_out,
    g_units,
    late,
    send,
    recv,
    w_buf,
    w_sems,
    g_buf,
    tail,
    gx,
    act,
    gb,
    out_acc,
    g_acc,
    sem,
    own_buf,
):
    i = pl.program_id(0)
    fn, hn, tn = sizes
    f, h, z = lax.axis_index("fsdp"), lax.axis_index("heads"), lax.axis_index("tensor")
    n, width = hidden_ref.shape
    number = index[(f * hn + h) * tn + z]
    gain, dbias = vectors.at[2:3], vectors.at[4:5]
    main = slice(0, width)
    s, half = i // 2, lax.rem(i, 2)
    comm = Comm(send, recv)
    blocks = {b: Block(comm, sizes, zw, late.at[b], b, own_buf.at[b - done]) for b in range(done, tn)}
    resumed = [blocks[b] for b in range(done, min(done + 2, tn))]
    for b in resumed:
        b.job.first_done = True

    def loads(b):
        slot = b % 2
        return [
            pltpu.make_async_copy(late.at[b], w_buf.at[slot, :, pl.ds(0, width)], w_sems.at[slot, 0]),
            pltpu.make_async_copy(
                ax.at[:, lax.rem(z + b, tn)], w_buf.at[slot, :, pl.ds(width, EXTRA)], w_sems.at[slot, 1]
            ),
        ]

    @pl.when(i == 0)
    def _():
        c = Tokens(cot_ref, g_buf, tail, sem)
        c.start()
        for b in range(done):
            for w in loads(b):
                w.start()
        for b in resumed:
            b.mine().start()
        enter(sizes, f, h, z)
        for b in resumed:
            b.forward()
        for b in range(done + 2, tn):
            blocks[b].begin()
        c.wait()

        def body(rows, start):
            gx[rows, main] = g_buf[rows, :].astype(bf16)

        by_rows(n, 32, body)
        gx[:, width : width + RANK] = nt(gx[:, main], down_bank[number]).astype(bf16)
        gx[:, width + RANK :] = jnp.zeros((n, EXTRA - RANK), bf16)

    def events(steps):
        for at, what in steps:

            @pl.when(i == at)
            def _():
                for b, name in what:
                    if name == "load":
                        if b < tn:
                            if b in blocks:
                                blocks[b].arrive()
                            for w in loads(b):
                                w.start()
                    elif b in blocks:
                        getattr(blocks[b], name)()

    events(plan[0])

    for b in range(tn):

        @pl.when(i == 2 * b)
        def _():
            for w in loads(b):
                w.wait()

    slot = lax.rem(s, 2)
    rows = pl.ds(pl.multiple_of(half * (n // 2), n // 2), n // 2)
    mlp_half(ln_ref, gx, w_buf.at[slot, 0], w_buf.at[slot, 1], act, gb, out_acc, g_acc, rows, s == 0, lambda: events(plan[1]))

    @pl.when(half == 1)
    def _():
        g_units[0, s] = tn_(ln_ref[:, width : width + RANK], gb[...]).astype(bf16)
        g_units[1, s] = tn_(gx[:, width : width + RANK], act[...]).astype(bf16)

    @pl.when(i == pl.num_programs(0) - 1)
    def _():
        down_mid = out_acc[:, width : width + RANK].astype(bf16)
        g_up_mid = g_acc[:, width : width + RANK].astype(bf16)
        g_up_in[...] = tn_(g_up_mid, ln_ref[:, main]).astype(bf16)
        g_down_out[...] = tn_(down_mid, gx[:, main]).astype(bf16)
        out_acc[:, main] += nn(down_mid, down_bank[number])
        g_acc[:, main] += nn(g_up_mid, up_bank[number])

        def body(rows, start):
            v = hidden_ref[rows, :]
            out_acc[rows, main] += v + dbias[...]
            gh_ref[rows, :] = g_buf[rows, :] + real(
                norm_back(g_acc[rows, main], v, gain[...], width), start, length
            )

        by_rows(n, 32, body)
        c = Tokens(y_ref, out_acc, tail, sem, out=True)
        c.start()
        for b in blocks.values():
            b.drain()
        c.wait()


def mlp(sizes, ln, cot, hidden, early, zw, ax, index, up, down, vectors):
    fn, hn, tn = sizes
    n, width = hidden.shape
    depth = ln.shape[1]
    units = early.shape[-1]
    done = 1
    length = cot.shape[0]
    late = max(tn - done, 1)
    plan = (
        (
            (2, ((2, "exchange"),)),
            (3, ((2, "load"),)),
            (4, ((3, "forward"),)),
            (5, ((3, "exchange"),)),
        ),
        (
            (0, ((1, "exchange"),)),
            (1, ((1, "load"),)),
            (5, ((3, "load"),)),
        ),
    )
    any_ = pl.BlockSpec(memory_space=pl.ANY)
    one = lambda s: pl.BlockSpec(s, lambda t: (0,) * len(s), pipeline_mode=pl.Buffered(1))
    shape = jax.ShapeDtypeStruct
    nsem = late * block_sems(fn)
    return pl.pallas_call(
        functools.partial(mlp_kernel, sizes, length, done, plan),
        grid=(2 * tn,),
        in_specs=[
            one((n, depth)),
            any_,
            one((n, width)),
            any_,
            any_,
            any_,
            pl.BlockSpec(memory_space=pltpu.SMEM),
            one(up.shape),
            one(down.shape),
            one(vectors.shape),
        ],
        out_specs=(
            any_,
            one((n, width)),
            one((RANK, width)),
            one((RANK, width)),
            one((2, tn, RANK, units)),
            any_,
        ),
        out_shape=(
            shape((length, 1, width), f32),
            shape((n, width), f32),
            shape((RANK, width), bf16),
            shape((RANK, width), bf16),
            shape((2, tn, RANK, units), bf16),
            shape(early.shape, bf16),
        ),
        input_output_aliases={3: 6 - 1},
        scratch_shapes=[
            pltpu.SemaphoreType.DMA((nsem,)),
            pltpu.SemaphoreType.DMA((nsem,)),
            pltpu.VMEM((2, 2, depth, units), bf16),
            pltpu.SemaphoreType.DMA((2, 2)),
            pltpu.VMEM((n, width), f32),
            tail_shape(length, width),
            pltpu.VMEM((n, depth), bf16),
            pltpu.VMEM((n, units), bf16),
            pltpu.VMEM((n, units), bf16),
            pltpu.VMEM((n, depth), f32),
            pltpu.VMEM((n, depth), f32),
            pltpu.SemaphoreType.DMA((2,)),
            pltpu.VMEM((late,) + zw.shape[1:], bf16),
        ],
        compiler_params=params(collective_id=4, has_side_effects=True),
        name="mlp",
    )(ln, cot, hidden, early, zw, ax, index, up, down, vectors)


def branch_back_kernel(
    place, index, gh_ref, w_ref, out_bank, mixed_ref, mid_ref, g_up_in, g_down_out, y_in, gm_ref, grads, y_out, gx, y_buf, sem
):
    n, width = gh_ref.shape
    half = w_ref.shape[-1]
    y = Bounce(y_in, y_buf, y_out, sem)
    y.start()

    def body(rows, start):
        gx[rows, 0:width] = gh_ref[rows, :].astype(bf16)

    by_rows(n, 32, body)
    g_mid = nt(gx[:, 0:width], out_bank[index[place()]]).astype(bf16)
    gx[:, width:] = g_mid
    grads[...] = jnp.zeros_like(grads)
    grads[0:RANK, :] = tn_(mid_ref[...], gx[:, 0:width]).astype(bf16)
    grads[RANK : 2 * RANK, :] = g_up_in[...]
    grads[2 * RANK : 3 * RANK, :] = g_down_out[...]
    grads[3 * RANK : 4 * RANK, :] = tn_(g_mid, mixed_ref[...]).astype(bf16)
    for p in range(w_ref.shape[0]):
        gm_ref[:, p * half : (p + 1) * half] = nn(gx[...], w_ref[p]).astype(bf16)
        if p == 0:
            y.turn()
    y.wait()


def branch_back(rows, place, index, gh, w, out, mixed, mid, g_up_in, g_down_out, y):
    n, width = gh.shape
    return pl.pallas_call(
        functools.partial(branch_back_kernel, place),
        in_specs=[pl.BlockSpec(memory_space=pltpu.SMEM)] + [pl.BlockSpec(memory_space=pltpu.VMEM)] * 7
        + [pl.BlockSpec(memory_space=pl.ANY)],
        out_specs=(pl.BlockSpec(memory_space=pltpu.VMEM),) * 2 + (pl.BlockSpec(memory_space=pl.ANY),),
        out_shape=(
            jax.ShapeDtypeStruct((n, width), bf16),
            jax.ShapeDtypeStruct((rows, width), bf16),
            jax.ShapeDtypeStruct(y.shape, f32),
        ),
        scratch_shapes=[
            pltpu.VMEM((n, width + RANK), bf16),
            pltpu.VMEM(y.shape, f32),
            pltpu.SemaphoreType.DMA(()),
        ],
        compiler_params=params(),
        name="branch_back",
    )(index, gh, w, out, mixed, mid, g_up_in, g_down_out, y)


def add_by_adapter(pick, parts):
    width = parts.shape[-1]
    if parts.shape[-2] % 16:
        parts = parts.astype(f32)
    return nn(pick[...], parts.reshape(-1, width).astype(bf16))


def picks(adapters, count, rows):
    shape = (count * rows, adapters.shape[0] * rows)
    place = jnp.repeat(adapters * rows, rows) + jnp.tile(jnp.arange(rows), adapters.shape[0])
    return (lax.broadcasted_iota(jnp.int32, shape, 0) == place[None, :]).astype(bf16)


def line_copies(comm, tn, z, here, sems, own=None):
    up, down = sems

    def send(sem, block, to, src=None):
        return comm.copy(sem, here(block) if src is None else src, here(block), tensor=to)

    def begin():
        @pl.when(z < tn - 1)
        def _():
            send(up[0], z, z + 1, own).start()

        @pl.when(z > 0)
        def _():
            send(down[0], z, z - 1, own).start()

    def step(k, then):
        @pl.when(z - 1 - k >= 0)
        def _():
            b = z - 1 - k
            comm.copy(up[k], here(b), here(b), tensor=z - 1).wait_recv()
            if k + 1 < tn - 1:

                @pl.when(z < tn - 1)
                def _():
                    send(up[k + 1], b, z + 1).start()

            then(b)

        @pl.when(z + 1 + k < tn)
        def _():
            b = z + 1 + k
            comm.copy(down[k], here(b), here(b), tensor=z + 1).wait_recv()
            if k + 1 < tn - 1:

                @pl.when(z > 0)
                def _():
                    send(down[k + 1], b, z - 1).start()

            then(b)

    def drain():
        for k in range(tn - 1):

            @pl.when((z < tn - 1) & (z - k >= 0))
            def _():
                send(up[k], z, z + 1).wait_send()

            @pl.when((z > 0) & (z + k < tn))
            def _():
                send(down[k], z, z - 1).wait_send()

    return begin, step, drain


class Reduce:
    def __init__(self, sizes, count, comm, hot, local, a, out, ra, dense, b=None, out_b=None, rb=None, hot_b=None):
        fn, hn, tn = sizes
        f, h, z = lax.axis_index("fsdp"), lax.axis_index("heads"), lax.axis_index("tensor")
        self.fn, self.hn, self.tn, self.f, self.h, self.z = fn, hn, tn, f, h, z
        self.count, self.comm, self.hot, self.hot_b, self.local = count, comm, hot, hot_b, local
        self.a, self.out, self.ra, self.dense, self.b, self.out_b, self.rb = a, out, ra, dense, b, out_b, rb
        self.piece = ra.shape[1]
        self.s_first = [comm.new() for _ in range(fn - 1)]
        s_line = ([comm.new() for _ in range(tn - 1)], [comm.new() for _ in range(tn - 1)])
        self.s_core = [comm.new() for _ in range(tn)]
        self.s_last = comm.new()
        self.sent = []
        per = count // hn
        self.mine, self.theirs = pl.ds(h * per, per), pl.ds((1 - h) * per, per)

        def slot(o, r):
            start, size = (0, per) if r is None else r
            return out.at[o, pl.ds(h * per + start, size)]

        self.spread = Rows(comm, fn, f, slot, per, lambda: dense, align=1)
        self.begin, self.line, self.drain_line = line_copies(
            comm, tn, z, lambda t: self.group(t, h), s_line
        )
        if b is not None:
            self.s_first_b = [comm.new() for _ in range(tn - 1)]
            self.s_core_b = comm.new()

            def slot_b(o, r):
                start, size = (0, tn) if r is None else r
                return rb.at[h, o, pl.ds(start, size)]

            self.spread_b = Rows(comm, fn, f, slot_b, tn, lambda: rb.at[h, f], align=1)

    def group(self, z, h):
        return self.ra.at[pl.ds((z * self.hn + h) * self.fn, self.fn)]

    def one(self, z, h, f):
        return self.ra.at[(z * self.hn + h) * self.fn + f]

    def rows(self, f):
        return self.a.at[pl.ds(pl.multiple_of(f * self.piece, 8), self.piece)]

    def send(self, make):
        make().start()
        self.sent.append(make)

    def own(self):
        copies = [pltpu.make_async_copy(self.rows(self.f), self.one(self.z, self.h, self.f), self.local.at[0])]
        if self.b is not None:
            copies.append(
                pltpu.make_async_copy(self.b.at[:, 0], self.rb.at[self.h, self.f, self.z], self.local.at[1])
            )
        return copies

    def start(self):
        f, h, z, comm = self.f, self.h, self.z, self.comm
        for m in range(1, self.fn):
            self.send(
                lambda m=m: comm.copy(
                    self.s_first[m - 1], self.rows(f ^ m), self.one(z, h, f), fsdp=f ^ m
                )
            )
        if self.b is not None:
            for d in range(1, self.tn):
                self.send(
                    lambda d=d: comm.copy(
                        self.s_first_b[d - 1],
                        self.b.at[:, d],
                        self.rb.at[h, f, z],
                        tensor=lax.rem(z + d, self.tn),
                    )
                )
        for c in self.own():
            c.start()

    def second(self):
        f, h, z, comm = self.f, self.h, self.z, self.comm
        for c in self.own():
            c.wait()
        for m in range(1, self.fn):
            b = self.one(z, h, f ^ m)
            comm.copy(self.s_first[m - 1], b, b, fsdp=f ^ m).wait_recv()
        self.begin()
        self.to_core(z).start()
        if self.b is not None:
            for d in range(1, self.tn):
                p = lax.rem(z + self.tn - d, self.tn)
                b = self.rb.at[h, f, p]
                comm.copy(self.s_first_b[d - 1], b, b, tensor=p).wait_recv()
            self.spread_b.begin()

    def to_core(self, block):
        b = self.group(block, self.h)
        return pltpu.make_async_remote_copy(
            src_ref=b,
            dst_ref=b,
            send_sem=self.comm.send.at[self.s_core[0] + block],
            recv_sem=self.comm.recv.at[self.s_core[0] + block],
            device_id={"heads": 1 - self.h},
            device_id_type=MESH,
        )

    def line_step(self, k):
        if k < self.tn - 1:
            self.line(k, lambda b: self.to_core(b).start())

    def forward_b(self):
        self.spread_b.forward_all()

    def exchange_b(self):
        self.spread_b.settle()
        b = self.rb.at[self.h]
        self.send(lambda: self.comm.copy(self.s_core_b, b, b, heads=1 - self.h))

    def fourth(self):
        h = self.h
        for k in range(self.tn):
            b = self.group(k, 1 - h)
            self.comm.copy(self.s_core[k], b, b, heads=1 - h).wait_recv()
        rows = self.hot.shape[0] // self.hn
        mine = self.hot.at[pl.ds(pl.multiple_of(self.h * rows, 16), rows)]
        total = add_by_adapter(mine, self.ra[...])
        self.dense[...] = total.reshape(self.dense.shape).astype(bf16)
        self.spread.begin()
        self.last().start()

    def last(self):
        return pltpu.make_async_copy(
            self.dense, self.out.at[self.f, self.mine], self.local.at[0]
        )

    def fifth(self):
        b = self.rb.at[1 - self.h]
        self.comm.copy(self.s_core_b, b, b, heads=1 - self.h).wait_recv()
        for k in range(2):
            total = add_by_adapter(self.hot_b, self.rb[:, :, :, k, :, :])
            self.out_b[k][...] = total.reshape(self.out_b[k].shape)

    def sixth(self):
        self.spread.forward_all()

    def seventh(self):
        self.last().wait()
        self.spread.settle()
        b = self.out.at[:, self.mine]
        self.send(lambda: self.comm.copy(self.s_last, b, b, heads=1 - self.h))

    def finish(self):
        h = self.h
        b = self.out.at[:, self.theirs]
        self.comm.copy(self.s_last, b, b, heads=1 - h).wait_recv()
        for make in self.sent:
            make().wait_send()
        self.drain_line()
        self.spread.drain()
        if self.b is not None:
            self.spread_b.drain()
        for k in range(self.tn):
            self.to_core(k).wait_send()


def reduce_sems(sizes, both):
    fn, hn, tn = sizes
    nb = bits_of(fn)
    tree = nb + 2 * (fn - 1 - nb)
    n = fn - 1 + 2 * (tn - 1) + tn + 1 + tree
    return n + (tn - 1 + 1 + tree if both else 0)


def enter_reduce(sizes, f, h, z):
    fn, hn, tn = sizes
    barrier = pltpu.get_barrier_semaphore()
    for m in range(1, fn):
        pl.semaphore_signal(barrier, 1, device_id={"fsdp": f ^ m}, device_id_type=MESH)
    pl.semaphore_signal(barrier, 1, device_id={"heads": 1 - h}, device_id_type=MESH)
    for d in range(1, tn):
        pl.semaphore_signal(barrier, 1, device_id={"tensor": lax.rem(z + d, tn)}, device_id_type=MESH)
    pl.semaphore_wait(barrier, fn - 1 + 1 + tn - 1)


def piece_rows(rows, fn):
    return -(-rows // (8 * fn)) * 8


def reduce_shapes(sizes, count, width, piece, units, both):
    fn, hn, tn = sizes
    n = fn * hn * tn
    shapes = [
        pltpu.SemaphoreType.DMA((reduce_sems(sizes, both),)),
        pltpu.SemaphoreType.DMA((reduce_sems(sizes, both),)),
        pltpu.SemaphoreType.DMA((2,)),
        pltpu.VMEM((n, piece, width), bf16),
        pltpu.VMEM((count // hn, piece, width), bf16),
    ]
    if both:
        shapes.append(pltpu.VMEM((hn, fn, tn, 2, RANK, units), bf16))
    return shapes


def attend_back_kernel(
    sizes, length, count, plan, hot, hot_b, q_ref, k_ref, v_ref, do_ref, log_ref, a, b, out_ref, sums, sums_u, sums_d, send, recv, local, ra, dense, rb, kt_ref, dq_ref, dk_ref, dv_ref
):
    head = pl.program_id(0)
    job = Reduce(sizes, count, Comm(send, recv), hot, local, a, sums, ra, dense, b, (sums_u, sums_d), rb, hot_b)

    @pl.when(head == 0)
    def _():
        enter_reduce(sizes, job.f, job.h, job.z)
        job.start()
        to_rows(kt_ref, k_ref.at[0])

        def clear(at):
            for r in (dk_ref, dv_ref):
                r[:, at] = jnp.zeros((r.shape[0], LANES), f32)

        columns(dk_ref.shape[1], clear)

    for at, what in plan:

        @pl.when(head == at)
        def _():
            for name, *more in what:
                getattr(job, name)(*more)

    attend_back_head(
        length, head, q_ref.at[0], k_ref.at[0], v_ref.at[0], do_ref, log_ref, kt_ref, dq_ref, dk_ref, dv_ref
    )

    @pl.when(head == pl.num_programs(0) - 1)
    def _():
        to_lanes(out_ref.at[0], dq_ref)

        def cast(at):
            out_ref[1, :, at] = dk_ref[:, at].astype(bf16)
            out_ref[2, :, at] = dv_ref[:, at].astype(bf16)

        columns(dk_ref.shape[1], cast)
        job.finish()


def attend_back(sizes, length, count, hot, hot_b, qkv, do, log, a, b):
    fn, hn, tn = sizes
    _, n, width = qkv.shape
    heads = width // HEAD_DIM
    units = b.shape[-1]
    piece = a.shape[0] // fn
    plan = (
        (2, (("second",),)),
        (5, (("line_step", 0),)),
        (7, (("line_step", 1), ("forward_b",))),
        (9, (("line_step", 2), ("exchange_b",))),
        (11, (("fourth",),)),
        (12, (("fifth",),)),
        (13, (("sixth",),)),
        (15, (("seventh",),)),
    )
    any_ = pl.BlockSpec(memory_space=pl.ANY)
    one = lambda j: pl.BlockSpec((1, n, width), lambda h: (j, 0, 0), pipeline_mode=pl.Buffered(1))
    return pl.pallas_call(
        functools.partial(attend_back_kernel, sizes, length, count, plan),
        grid=(heads,),
        in_specs=[
            whole(hot.shape),
            whole(hot_b.shape),
            one(0),
            one(1),
            one(2),
            whole((n, width)),
            whole((heads, n)),
            any_,
            any_,
        ],
        out_specs=(whole((3, n, width)), any_) + (whole((count, RANK, units)),) * 2,
        out_shape=(
            jax.ShapeDtypeStruct((3, n, width), bf16),
            jax.ShapeDtypeStruct((fn, count, piece, width), bf16),
        )
        + (jax.ShapeDtypeStruct((count, RANK, units), f32),) * 2,
        scratch_shapes=reduce_shapes(sizes, count, width, piece, units, True)
        + [pltpu.VMEM((width, n), f32)] * 2
        + [pltpu.VMEM((n, width), f32)] * 2,
        compiler_params=params(collective_id=1, has_side_effects=True),
        name="attend_back",
    )(hot, hot_b, qkv, qkv, qkv, do, log, a, b)


def project_back_kernel(
    sizes,
    count,
    hot,
    index,
    before,
    g_ref,
    w_any,
    first_ref,
    mid_ref,
    ln_ref,
    gh_any,
    x_ref,
    vectors,
    gi_ref,
    sums,
    a,
    g_proj_out,
    g_up_in,
    g_down_out,
    g_proj_in,
    send,
    recv,
    local,
    ra,
    dense,
    w_buf,
    gh_buf,
    w_sems,
    x_buf,
    tail,
    acc,
    grads,
    g_mid,
    sem,
    before_buf,
    w_rows,
):
    i = pl.program_id(0)
    length = x_ref.shape[0]
    n, width = ln_ref.shape
    half = w_buf.shape[-1]
    gain = vectors.at[0:1]
    parts = w_buf.shape[1]
    load = Tokens(x_ref, x_buf, tail, sem)
    job = Reduce(sizes, count, Comm(send, recv), hot, local, a, sums, ra, dense)
    number = index[(job.f * job.hn + job.h) * job.tn + job.z]

    def load_w(j):
        return pltpu.make_async_copy(w_any.at[j], w_buf.at[j], w_sems.at[j])

    load_gh = pltpu.make_async_copy(gh_any, gh_buf, w_sems.at[3])
    load_before = pltpu.make_async_copy(before, before_buf, w_sems.at[5])
    load_rows = pltpu.make_async_copy(w_any.at[:, :, pl.ds(width, RANK)], w_rows, w_sems.at[6])
    save = pltpu.make_async_copy(grads, a, w_sems.at[4])

    @pl.when(i == 0)
    def _():
        load_rows.start()
        for j in range(3):
            load_w(j).start()
        load.start()
        load_gh.start()
        load_before.start()
        enter_reduce(sizes, job.f, job.h, job.z)
        if grads.shape[0] > 6 * RANK:
            grads[6 * RANK :, :] = jnp.zeros((grads.shape[0] - 6 * RANK, width), bf16)
        load_rows.wait()

        def small(j, _):
            m = sum(
                nt(g_ref[j, :, p * half : (p + 1) * half], w_rows[j, p])
                for p in range(parts)
            ).astype(bf16)
            g_mid[j] = m
            at = pl.ds(pl.multiple_of((3 + j) * RANK, RANK), RANK)
            grads[at, :] = tn_(mid_ref[j], g_ref[j]).astype(bf16)
            return 0

        lax.fori_loop(0, 3, small, 0)
        mids = jnp.concatenate([g_mid[j].astype(f32).T for j in range(3)]).astype(bf16)
        grads[0 : 3 * RANK, :] = nn(mids, ln_ref[...]).astype(bf16)
        save.start()
        save.wait()
        job.start()

    @pl.when(i == 2)
    def _():
        job.second()

    @pl.when(i == 3)
    def _():
        job.line_step(0)

    @pl.when((i > 0) & (i < 4))
    def _():
        j = i - 1
        load_w(j).wait()
        r = nn(g_mid[j], first_ref[j, number])
        for p in range(parts):
            r = r + nt(g_ref[j, :, p * half : (p + 1) * half], w_buf[j, p, pl.ds(0, width), :])

        @pl.when(i == 1)
        def _():
            acc[...] = r

        @pl.when(i > 1)
        def _():
            acc[...] += r

    @pl.when(i == 4)
    def _():
        job.line_step(1)
        load.wait()
        load_gh.wait()

        def body(rows, start):
            v = x_buf[rows, :]
            acc[rows, :] = gh_buf[rows, :] + norm_back(acc[rows, :], v, gain[...], width)

        by_rows(n, 32, body)
        c = Tokens(gi_ref, acc, tail, sem, out=True)
        c.start()
        for k in range(2, sizes[2] - 1):
            job.line_step(k)
        job.fourth()
        load_before.wait()
        piece = before_buf.shape[2]

        def rows_of(k, r):
            k = k * RANK + r * 8
            return before_buf[k // piece, :, k % piece : k % piece + 8, :].astype(f32)

        for k, dst in enumerate((g_proj_out, g_up_in, g_down_out)):
            for r in range(2):
                dst[:, r * 8 : r * 8 + 8, :] = rows_of(k, r)

        for p in range(parts):

            @pl.when(job.h == p)
            def _():
                for r in range(2):
                    g_proj_in[:, r * 8 : r * 8 + 8, :] = rows_of(3, r)[:, :, p * half : (p + 1) * half]

        job.sixth()
        job.seventh()
        job.finish()
        c.wait()


def project_back(sizes, count, hot, index, before, g, w, first, mid, ln, gh, x, vectors):
    fn, hn, tn = sizes
    n, width = ln.shape
    parts, half = w.shape[1], w.shape[-1]
    length = x.shape[0]
    piece = piece_rows(6 * RANK, fn)
    any_ = pl.BlockSpec(memory_space=pl.ANY)
    one = lambda s: pl.BlockSpec(s, lambda t: (0,) * len(s), pipeline_mode=pl.Buffered(1))
    shape = jax.ShapeDtypeStruct
    return pl.pallas_call(
        functools.partial(project_back_kernel, sizes, count),
        grid=(5,),
        in_specs=[
            one(hot.shape),
            pl.BlockSpec(memory_space=pltpu.SMEM),
            any_,
            one(g.shape),
            any_,
            one(first.shape),
            one(mid.shape),
            one((n, width)),
            any_,
            any_,
            one(vectors.shape),
        ],
        out_specs=(any_, any_, any_) + (one((count, RANK, width)),) * 3 + (one((count, RANK, half)),),
        out_shape=(
            shape((length, 1, width), f32),
            shape((fn, count, piece, width), bf16),
            shape((fn * piece, width), bf16),
        )
        + (shape((count, RANK, width), f32),) * 3
        + (shape((count, RANK, half), f32),),
        scratch_shapes=reduce_shapes(sizes, count, width, piece, 0, False)
        + [
            pltpu.VMEM(w.shape, bf16),
            pltpu.VMEM((n, width), f32),
            pltpu.SemaphoreType.DMA((7,)),
            pltpu.VMEM((n, width), f32),
            tail_shape(length, width),
            pltpu.VMEM((n, width), f32),
            pltpu.VMEM((fn * piece, width), bf16),
            pltpu.VMEM(mid.shape, bf16),
            pltpu.SemaphoreType.DMA((2,)),
            pltpu.VMEM(before.shape, bf16),
            pltpu.VMEM((3, parts, RANK, half), bf16),
        ],
        compiler_params=params(collective_id=2, has_side_effects=True),
        name="qkv_back",
    )(hot, index, before, g, w, first, mid, ln, gh, x, vectors)


def finish_kernel(count, last_any, *refs):
    k = (len(refs) - 5) // 3
    passed, outs = refs[:k], refs[k + 2 : 2 * k + 2]
    g_in, g_out = refs[k : k + 2]
    bufs, last_buf, sems, last_sem = refs[2 * k + 2 : 3 * k + 2], *refs[3 * k + 2 :]
    load = pltpu.make_async_copy(last_any, last_buf, last_sem)
    load.start()
    moves = [Bounce(a, b, c, sems.at[i]) for i, (a, b, c) in enumerate(zip(passed, bufs, outs))]
    for m in moves:
        m.start()
    load.wait()
    piece, half = last_buf.shape[2], g_out.shape[-1]
    h = lax.axis_index("heads")

    def rows_of(j, r):
        at = j * RANK + r * 8
        return last_buf[at // piece, :, at % piece : at % piece + 8, :].astype(f32)

    for m in moves:
        m.turn()
    for j in range(3):
        for r in range(2):
            g_in[j, :, r * 8 : r * 8 + 8, :] = rows_of(j, r)
    for p in range(2):

        @pl.when(h == p)
        def _():
            for j in range(3):
                for r in range(2):
                    g_out[j, :, r * 8 : r * 8 + 8, :] = rows_of(3 + j, r)[:, :, p * half : (p + 1) * half]

    for m in moves:
        m.wait()


def finish(count, half, last, *passed):
    width = last.shape[-1]
    any_ = pl.BlockSpec(memory_space=pl.ANY)
    vmem = pl.BlockSpec(memory_space=pltpu.VMEM)
    shape = jax.ShapeDtypeStruct
    k = len(passed)
    return pl.pallas_call(
        functools.partial(finish_kernel, count),
        in_specs=[any_] * (k + 1),
        out_specs=(vmem, vmem) + (any_,) * k,
        out_shape=(shape((3, count, RANK, width), f32), shape((3, count, RANK, half), f32))
        + tuple(shape(v.shape, v.dtype) for v in passed),
        scratch_shapes=[pltpu.VMEM(v.shape, v.dtype) for v in passed]
        + [
            pltpu.VMEM(last.shape, bf16),
            pltpu.SemaphoreType.DMA((k,)),
            pltpu.SemaphoreType.DMA(()),
        ],
        compiler_params=params(),
        name="finish",
    )(last, *passed)


def per_device(
    inputs,
    cotangent,
    image_adapter_index,
    first_norm_gain,
    first_norm_bias,
    second_norm_gain,
    second_norm_bias,
    query_key_value_weight,
    attention_output_weight,
    up_weight,
    down_weight,
    up_projection_bias,
    down_projection_bias,
    query_key_value_adapter_first,
    query_key_value_adapter_second,
    projection_adapter_first,
    projection_adapter_second,
    up_adapter_first,
    up_adapter_second,
    down_adapter_first,
    down_adapter_second,
):
    sizes = tuple(lax.axis_size(a) for a in ("fsdp", "heads", "tensor"))
    fn, hn, tn = sizes
    f, h, z = (lax.axis_index(a) for a in ("fsdp", "heads", "tensor"))
    images, length, width = inputs.shape
    assert images == 1 and hn == 2
    count = query_key_value_adapter_first.shape[1]
    units = up_weight.shape[-1]
    x, cot = jnp.swapaxes(inputs, 0, 1), jnp.swapaxes(cotangent, 0, 1)
    vectors = jnp.concatenate(
        [
            first_norm_gain,
            first_norm_bias,
            second_norm_gain,
            second_norm_bias,
            down_projection_bias.astype(f32),
        ]
    ).reshape(5, width)
    index = image_adapter_index
    qkv_in = jnp.swapaxes(query_key_value_adapter_first, 2, 3)
    u_in = jnp.swapaxes(up_adapter_first, 1, 2)
    wq, wo, zw, ax, ln1, qkv, qkv_mid, mixed, log, hidden, ln2, proj_mid, early = attention(
        sizes,
        jnp.swapaxes(query_key_value_weight, 0, 1),
        attention_output_weight,
        up_weight,
        down_weight,
        query_key_value_adapter_second,
        jnp.swapaxes(projection_adapter_first, 1, 2),
        up_adapter_second,
        down_adapter_first,
        jnp.pad(up_projection_bias[None], ((0, EXTRA - RANK - 1), (0, 0))),
        index,
        qkv_in,
        projection_adapter_second,
        x,
        vectors,
        u_in,
    )
    y, g_hidden, g_up_in, g_down_out, g_units, _ = mlp(
        sizes, ln2, cot, hidden, early, zw, ax, index, u_in, down_adapter_second, vectors
    )
    g_mixed, grads, y = branch_back(
        piece_rows(4 * RANK, fn) * fn,
        lambda: (lax.axis_index("fsdp") * hn + lax.axis_index("heads")) * tn + lax.axis_index("tensor"),
        index,
        g_hidden,
        wo,
        projection_adapter_second,
        mixed,
        proj_mid,
        g_up_in,
        g_down_out,
        y,
    )
    by_place = image_adapter_index.reshape(fn, hn, tn)
    order = jnp.transpose(by_place, (2, 1, 0)).reshape(-1)
    order_b = jnp.transpose(by_place, (1, 0, 2)).reshape(-1)
    pick = picks(order, count, piece_rows(4 * RANK, fn))
    pick_b = picks(order_b, count, RANK)
    g_qkv, sums, g_up_out, g_down_in = attend_back(
        sizes, length, count, pick, pick_b, qkv, g_mixed, log, grads, g_units
    )
    g_x, last, _, g_proj_out, g_up_in, g_down_out, g_proj_in = project_back(
        sizes,
        count,
        picks(order, count, piece_rows(6 * RANK, fn)),
        index,
        sums,
        g_qkv,
        wq,
        qkv_in,
        qkv_mid,
        ln1,
        g_hidden,
        x,
        vectors,
    )
    g_qkv_in, g_qkv_out, g_x, g_proj_in, g_proj_out, g_up_in, g_up_out, g_down_in, g_down_out = finish(
        count, width // hn, last, g_x, g_proj_in, g_proj_out, g_up_in, g_up_out, g_down_in, g_down_out
    )
    return (
        jnp.swapaxes(y, 0, 1),
        jnp.swapaxes(g_x, 0, 1),
        jnp.swapaxes(g_qkv_in, 2, 3),
        g_qkv_out,
        jnp.swapaxes(g_proj_in, 1, 2),
        g_proj_out,
        jnp.swapaxes(g_up_in, 1, 2),
        g_up_out,
        g_down_in,
        g_down_out,
    )


def solution(mesh):
    in_specs = (
        P(("fsdp", "heads", "tensor"), None, None),
        P(("fsdp", "heads", "tensor"), None, None),
        P(),
        P(),
        P(),
        P(),
        P(),
        P("fsdp", None, "heads"),
        P("fsdp", "heads"),
        P("fsdp", "tensor"),
        P("fsdp", "tensor"),
        P("tensor"),
        P(),
        P(),
        P(None, None, None, "heads"),
        P(None, "heads", None),
        P(),
        P(),
        P(None, None, "tensor"),
        P(None, None, "tensor"),
        P(),
    )
    out_specs = (
        P(("fsdp", "heads", "tensor"), None, None),
        P(("fsdp", "heads", "tensor"), None, None),
        P(),
        P(None, None, None, "heads"),
        P(None, "heads", None),
        P(),
        P(),
        P(None, None, "tensor"),
        P(None, None, "tensor"),
        P(),
    )
    return jax.shard_map(
        per_device, mesh=mesh, in_specs=in_specs, out_specs=out_specs, check_vma=False
    )
```

```python
import functools
import jax
import jax.numpy as jnp
from jax import lax
from jax.experimental import pallas as pl
from jax.experimental.pallas import tpu as pltpu
from jax.sharding import PartitionSpec as P

HEAD_DIM = 72
norm_eps = 1e-06
f32 = jnp.float32
bf16 = jnp.bfloat16
MESH = pl.DeviceIdType.MESH


RANK = 16
EXTRA = 32


def padded(n):
    return -(-n // 16) * 16


def row_sums(v):
    return jnp.sum(v, axis=-1, keepdims=True)


class Tokens:
    def __init__(self, hbm, buf, tail, sems, out=False):
        self.length = hbm.shape[0]
        self.buf, self.tail, self.out = buf, tail, out
        self.whole = self.length // 8 * 8
        pairs = [(hbm.at[0 : self.whole, 0, :], buf.at[0 : self.whole, 0 : hbm.shape[-1]])]
        if self.whole < self.length:
            pairs.append((hbm.at[self.whole : self.length, 0, :], tail))
        self.copies = [
            pltpu.make_async_copy(*((b, a) if out else (a, b)), sems.at[i]) for i, (a, b) in enumerate(pairs)
        ]

    def start(self):
        if self.out and self.whole < self.length:
            self.tail[...] = self.buf[self.whole : self.length, 0 : self.tail.shape[-1]]
        for c in self.copies:
            c.start()

    def wait(self):
        for c in self.copies:
            c.wait()
        if not self.out:
            rest = self.buf.shape[0] - self.length
            zeros = jnp.zeros((rest, self.buf.shape[1]), f32)
            if self.whole < self.length:
                zeros = jnp.concatenate([self.tail[...], zeros])
            self.buf[self.whole :, :] = zeros


def tail_shape(length, width):
    return pltpu.VMEM((max(length % 8, 1), width), f32)


def unit_of(v, width):
    mean = row_sums(v) * (1.0 / width)
    centred = v - mean
    inverse = lax.rsqrt(row_sums(centred * centred) * (1.0 / width) + norm_eps)
    return centred * inverse, inverse


def by_rows(n, step, body):
    def one(r, _):
        body(pl.ds(pl.multiple_of(r * step, step), step), r * step)
        return 0

    lax.fori_loop(0, n // step, one, 0)


def real(v, start, length):
    row = lax.broadcasted_iota(jnp.int32, v.shape, 0) + start
    return jnp.where(row < length, v, 0.0)


def normalize_into(dst, src, gain, bias, length):
    n, width = src.shape

    def body(rows, start):
        unit, _ = unit_of(src[rows, :], width)
        dst[rows, 0:width] = real(unit * gain[...] + bias[...], start, length).astype(bf16)

    by_rows(n, 32, body)


def norm_back(grad, v, gain, width):
    unit, inverse = unit_of(v, width)
    e = grad * gain
    return inverse * (e - row_sums(e) * (1.0 / width) - unit * (row_sums(e * unit) * (1.0 / width)))


LANES = 128
SCALE = HEAD_DIM**-0.5
LOG2E = 1.4426950408889634


def nn(a, b):
    return lax.dot_general(a, b, (((1,), (0,)), ((), ())), preferred_element_type=f32)


def nt(a, b):
    return lax.dot_general(a, b, (((1,), (1,)), ((), ())), preferred_element_type=f32)


def tn_(a, b):
    return lax.dot_general(a, b, (((0,), (0,)), ((), ())), preferred_element_type=f32)


def whole(shape):
    return pl.BlockSpec(shape, lambda *_: (0,) * len(shape))


def params(limit=60, **more):
    return pltpu.CompilerParams(vmem_limit_bytes=limit << 20, **more)


def head_window(head, width):
    tile = jnp.minimum(head * HEAD_DIM // LANES, width // LANES - 2)
    return pl.ds(pl.multiple_of(tile * LANES, LANES), 2 * LANES), head * HEAD_DIM - tile * LANES


def only_head(values, start):
    lane = lax.broadcasted_iota(jnp.int32, values.shape, 1)
    return jnp.where((lane >= start) & (lane < start + HEAD_DIM), values, jnp.zeros_like(values))


def own_rows(head):
    return pl.ds(pl.multiple_of(head * HEAD_DIM, 8), HEAD_DIM)


def attend_forward_head(length, head, q_ref, k_ref, vt_ref, sum_ref, log_ref):
    win, start = head_window(head, q_ref.shape[-1])
    q = only_head(q_ref[:, win], start)
    v = vt_ref[own_rows(head), :].astype(bf16)
    s = nt(k_ref[:, win], q)
    key = lax.broadcasted_iota(jnp.int32, s.shape, 0)
    s = jnp.where(key < length, s, -1e30)
    top = jnp.max(s, axis=0, keepdims=True)
    p = jnp.exp2((s - top) * (SCALE * LOG2E))
    total = jnp.sum(p, axis=0, keepdims=True)
    sum_ref[own_rows(head), :] = nn(v, p.astype(bf16)) * (1.0 / total)
    log_ref[pl.ds(head, 1), :] = top * (SCALE * LOG2E) + jnp.log(total) * LOG2E


def attend_back_head(length, head, q_ref, k_ref, v_ref, do_ref, log_ref, kt_ref, dq_ref, dk_ref, dv_ref):
    win, start = head_window(head, q_ref.shape[-1])
    q = only_head(q_ref[:, win], start)
    k = k_ref[:, win]
    do = only_head(do_ref[:, win], start)
    s = nt(k, q)
    key = lax.broadcasted_iota(jnp.int32, s.shape, 0)
    p = jnp.exp2(jnp.where(key < length, s * (SCALE * LOG2E), -1e30) - log_ref[pl.ds(head, 1), :])
    dp = nt(v_ref[:, win], do)
    pd = p * dp
    ds = (pd - p * jnp.sum(pd, axis=0, keepdims=True)).astype(bf16)
    dv_ref[:, win] += nn(p.astype(bf16), do)
    dk_ref[:, win] += nn(ds, q) * SCALE
    dq_ref[own_rows(head), :] = nn(kt_ref[own_rows(head), :].astype(bf16), ds) * SCALE


def columns(width, body):
    def one(c, _):
        body(pl.ds(pl.multiple_of(c * LANES, LANES), LANES))
        return 0

    lax.fori_loop(0, width // LANES, one, 0)


def to_rows(dst, src):
    def body(at):
        dst[at, :] = src[:, at].astype(f32).T.astype(dst.dtype)

    columns(src.shape[1], body)


def to_lanes(dst, src):
    def body(at):
        dst[:, at] = src[at, :].T.astype(dst.dtype)

    columns(src.shape[0], body)


def bits_of(n):
    return n.bit_length() - 1


class Comm:
    def __init__(self, send, recv):
        self.send, self.recv, self.n = send, recv, 0

    def new(self):
        self.n += 1
        return self.n - 1

    def copy(self, i, src, dst, **where):
        return pltpu.make_async_remote_copy(
            src_ref=src,
            dst_ref=dst,
            send_sem=self.send.at[i],
            recv_sem=self.recv.at[i],
            device_id=where,
            device_id_type=MESH,
        )


def enter(axes_sizes, f, h, z):
    fn, hn, tn = axes_sizes
    barrier = pltpu.get_barrier_semaphore()
    count = 0
    for b in range(bits_of(fn)):
        pl.semaphore_signal(
            barrier, 1, device_id={"fsdp": f ^ (1 << b)}, device_id_type=MESH
        )
        count += 1
    pl.semaphore_signal(barrier, 1, device_id={"heads": 1 - h}, device_id_type=MESH)
    count += 1
    for d in range(1, tn):
        pl.semaphore_signal(
            barrier, 1, device_id={"tensor": lax.rem(z + d, tn)}, device_id_type=MESH
        )
        count += 1
    pl.semaphore_wait(barrier, count)


class Rows:
    def __init__(self, comm, fn, f, slot, rows, own, align=8):
        self.comm, self.fn, self.f, self.slot, self.own = comm, fn, f, slot, own
        self.nb = bits_of(fn)
        half = rows // 2 // align * align
        self.parts = ((0, half, list(range(self.nb))), (half, rows - half, list(range(self.nb))[::-1]))
        self.first = [comm.new() for _ in range(self.nb)]
        self.later = {}
        for p, (_, _, order) in enumerate(self.parts):
            for m in range(1, fn):
                last = max(order.index(b) for b in range(self.nb) if m >> b & 1)
                for b in order[last + 1 :]:
                    self.later[p, m, b] = comm.new()
        self.sent = []
        self.first_done = False

    def part(self, origin, p):
        start, size, _ = self.parts[p]
        return self.slot(origin, (start, size))

    def begin(self):
        for b in range(self.nb):
            self.send(
                lambda b=b: self.comm.copy(
                    self.first[b], self.own(), self.slot(self.f, None), fsdp=self.f ^ (1 << b)
                )
            )

    def _arrived(self, m, p):
        order = self.parts[p][2]
        last = max(order.index(b) for b in range(self.nb) if m >> b & 1)
        b = order[last]
        src = m ^ (1 << b)
        if src == 0:
            return None
        where = self.part(self.f ^ m, p)
        return self.comm.copy(self.later[p, src, b], where, where, fsdp=self.f ^ (1 << b))

    def forward(self, m):
        if m & (m - 1) == 0 and not self.first_done:
            b = bits_of(m)
            where = self.slot(self.f ^ m, None)
            self.comm.copy(self.first[b], where, where, fsdp=self.f ^ m).wait_recv()
        for p, (_, _, order) in enumerate(self.parts):
            if m & (m - 1):
                self._arrived(m, p).wait_recv()
            last = max(order.index(b) for b in range(self.nb) if m >> b & 1)
            for b in order[last + 1 :]:

                def onward(p=p, b=b):
                    where = self.part(self.f ^ m, p)
                    return self.comm.copy(self.later[p, m, b], where, where, fsdp=self.f ^ (1 << b))

                self.send(onward)

    def masks(self):
        return sorted(range(1, self.fn), key=lambda m: (bin(m).count("1"), m))

    def finish_first(self):
        for b in range(self.nb):
            where = self.slot(self.f ^ (1 << b), None)
            self.comm.copy(self.first[b], where, where, fsdp=self.f ^ (1 << b)).wait_recv()
        self.drain()

    def leaf(self, m):
        return not any(key[1] == m for key in self.later)

    def forward_all(self):
        for m in self.masks():
            if not self.leaf(m):
                self.forward(m)

    def settle(self):
        for m in self.masks():
            if self.leaf(m):
                self.forward(m)

    def send(self, make):
        make().start()
        self.sent.append(make)

    def drain(self):
        for make in self.sent:
            make().wait_send()


def tree_sems(fn):
    nb = bits_of(fn)
    return nb + 2 * (fn - 1 - nb)


class Bounce:
    def __init__(self, src, buf, dst, sem):
        self.load = pltpu.make_async_copy(src, buf, sem)
        self.save = pltpu.make_async_copy(buf, dst, sem)

    def start(self):
        self.load.start()

    def turn(self):
        self.load.wait()
        self.save.start()

    def wait(self):
        self.save.wait()


class Block:
    def __init__(self, comm, sizes, zw, dst, s, buf, own=None):
        fn, hn, tn = sizes
        f, h, z = lax.axis_index("fsdp"), lax.axis_index("heads"), lax.axis_index("tensor")
        rows = zw.shape[1]
        self.comm, self.dst, self.h, self.buf = comm, dst, h, buf
        t = lax.rem(z + s, tn)

        def slot(o, r):
            start, size = (0, rows) if r is None else r
            return dst.at[h, pl.ds(pl.multiple_of(o * rows + start, 8), size)]

        self.own = lambda: zw.at[t] if own is None else own
        self.slot = lambda: slot(f, None)
        self.job = Rows(comm, fn, f, slot, rows, self.own)
        self.local = comm.new()
        self.core = comm.new()

    def mine(self):
        return Bounce(self.own(), self.buf, self.slot(), self.comm.send.at[self.local])

    def to_core(self, which):
        b = self.dst.at[which]
        return self.comm.copy(self.core, b, b, heads=1 - self.h)

    def begin(self):
        self.job.begin()
        self.mine().start()

    def forward(self):
        self.mine().turn()
        self.job.forward_all()

    def exchange(self):
        self.job.settle()
        self.mine().wait()
        self.to_core(self.h).start()

    def arrive(self):
        self.to_core(1 - self.h).wait_recv()

    def drain(self):
        self.job.drain()
        self.to_core(self.h).wait_send()


def block_sems(fn):
    return tree_sems(fn) + 2


class Weight:
    def __init__(self, comm, fn, f, h, rows, own, dst, extra, own_sem, buf):
        self.comm, self.h, self.dst, self.extra = comm, h, dst, extra
        width = fn * rows
        self.main, self.more = pl.ds(0, width), pl.ds(width, RANK)

        def slot(o, r):
            start, size = (0, rows) if r is None else r
            return dst.at[h, pl.ds(pl.multiple_of(o * rows + start, 8), size)]

        self.job = Rows(comm, fn, f, slot, rows, lambda: own)
        self.core, self.core_extra = comm.new(), comm.new()
        self.mine = lambda: Bounce(own, buf, slot(f, None), own_sem.at[0])
        self.mine_extra = lambda: pltpu.make_async_copy(
            extra.at[h], dst.at[h, self.more], own_sem.at[1]
        )

    def start_extra(self):
        self.mine_extra().start()
        self.to_core_extra().start()

    def to_core_extra(self):
        return self.comm.copy(
            self.core_extra, self.extra.at[1 - self.h], self.dst.at[self.h, self.more], heads=1 - self.h
        )

    def to_core(self, which):
        b = self.dst.at[which, self.main]
        return self.comm.copy(self.core, b, b, heads=1 - self.h)

    def exchange(self):
        self.job.settle()
        self.mine().wait()
        self.to_core(self.h).start()

    def arrive(self):
        self.mine_extra().wait()
        where = self.dst.at[1 - self.h, self.more]
        self.comm.copy(self.core_extra, where, where, heads=1 - self.h).wait_recv()
        self.to_core(1 - self.h).wait_recv()

    def drain(self):
        self.job.drain()
        self.to_core(self.h).wait_send()
        self.to_core_extra().wait_send()


def attention_kernel(
    sizes,
    wq,
    wo,
    wu,
    wd,
    bq,
    bp,
    bu,
    bd,
    ub,
    index,
    first_ref,
    out_ref,
    x_ref,
    vectors,
    up_ref,
    oq,
    oo,
    zw,
    ax,
    ln_out,
    qkv_out,
    qmid_ref,
    mixed_out,
    log_ref,
    hidden_out,
    ln2_out,
    mid_ref,
    got,
    send,
    recv,
    wq_buf,
    wo_buf,
    w_sems,
    own_sems,
    own_q,
    own_o,
    own_z,
    own_b,
    aq,
    ap,
    a2,
    qkv_ref,
    lnx_ref,
    vt_ref,
    sum_ref,
    x_buf,
    x_tail,
    x_sems,
    mixed_ref,
    hidden_ref,
    ln2_ref,
):
    i = pl.program_id(0)
    fn, hn, tn = sizes
    f, h, z = lax.axis_index("fsdp"), lax.axis_index("heads"), lax.axis_index("tensor")
    rows, half = wo.shape
    length = x_ref.shape[0]
    n, width = mixed_ref.shape
    number = index[(f * hn + h) * tn + z]
    gain1, bias1, gain, bias = (vectors.at[k : k + 1] for k in range(4))
    heads = width // HEAD_DIM
    comm = Comm(send, recv)
    qs = [
        Weight(comm, fn, f, h, rows, wq.at[j], oq.at[j], aq.at[j], own_sems.at[j], own_q.at[j])
        for j in range(3)
    ]
    o = Weight(comm, fn, f, h, rows, wo, oo, ap, own_sems.at[3], own_o)
    line = ([comm.new() for _ in range(tn - 1)], [comm.new() for _ in range(tn - 1)])
    small = [comm.new() for _ in range(tn - 1)]
    blocks = [
        Block(comm, sizes, zw, got.at[b], b, own_b.at[b], own_z if b == 0 else None)
        for b in range(own_b.shape[0])
    ]
    nxt = [Block(comm, sizes, zw, got.at[b], b, own_z) for b in range(len(blocks), min(len(blocks) + 2, tn))]
    begin_z, step_z, drain_z = line_copies(comm, tn, z, lambda t: zw.at[t], line, own_z)
    mine_z = [Bounce(w, own_z, zw.at[z], own_sems.at[4, 0]) for w in (wu, wd)]
    mine_a = lambda: pltpu.make_async_copy(a2.at[z], ax.at[:, z], own_sems.at[4, 1])
    to_line = lambda d: comm.copy(
        small[d - 1], a2.at[lax.rem(z + d, tn)], ax.at[:, z], tensor=lax.rem(z + d, tn)
    )
    load_x = Tokens(x_ref, x_buf, x_tail, x_sems)
    load_q = lambda j: pltpu.make_async_copy(oq.at[j], wq_buf.at[j], w_sems.at[j])
    load_o = lambda: pltpu.make_async_copy(oo, wo_buf, w_sems.at[3])
    save_ln = lambda: pltpu.make_async_copy(lnx_ref.at[:, pl.ds(0, width)], ln_out, w_sems.at[4])
    saves = [
        pltpu.make_async_copy(a, b, w_sems.at[6 + k])
        for k, (a, b) in enumerate(((mixed_ref, mixed_out), (hidden_ref, hidden_out), (ln2_ref, ln2_out)))
    ]
    save_qkv = lambda: pltpu.make_async_copy(qkv_ref, qkv_out, w_sems.at[5])

    @pl.when(i == 0)
    def _():
        load_x.start()
        for w in qs + [o]:
            w.mine().start()
        for p in range(2):

            @pl.when(h == p)
            def _():
                mine_z[p].start()

        for p in range(hn):
            k = index[(f * hn + p) * tn + z]
            for j in range(3):
                aq[j, p] = bq[j, k]
            ap[p] = bp[k]
        for t in range(tn):
            k = index[(f * hn + h) * tn + t]
            a2[t, 0, 0:RANK] = bu[k]
            a2[t, 1, 0:RANK] = bd[k]
            a2[t, 0, RANK:] = ub[...]
            a2[t, 1, RANK:] = jnp.zeros_like(ub)
        enter(sizes, f, h, z)
        qs[0].job.begin()
        qs[1].job.begin()
        mine_z[0].turn()
        begin_z()
        for w in qs + [o]:
            w.start_extra()
        mine_a().start()
        for d in range(1, tn):
            to_line(d).start()
        for w in qs + [o]:
            w.mine().turn()
        load_x.wait()
        normalize_into(lnx_ref, x_buf, gain1, bias1, length)
        save_ln().start()

    @pl.when(i == 1)
    def _():
        qs[0].job.forward_all()
        qs[2].job.begin()
        qs[1].job.forward_all()
        step_z(0, lambda t: None)
        qs[0].exchange()
        qs[0].arrive()
        load_q(0).start()

    @pl.when(i == 2)
    def _():
        qs[2].job.forward_all()
        o.job.begin()
        qs[1].exchange()
        qs[1].arrive()
        load_q(1).start()
        qs[2].exchange()

    @pl.when(i == 3)
    def _():
        if tn > 2:
            step_z(1, lambda t: None)
        qs[2].arrive()
        load_q(2).start()

    @pl.when((i >= 1) & (i < 4))
    def _():
        j = i - 1
        mid = nt(lnx_ref[:, 0:width], first_ref[j, number]).astype(bf16)
        qmid_ref[j] = mid
        load_q(j).wait()

        @pl.when(i == 1)
        def _():
            save_ln().wait()

        lnx_ref[:, width:] = mid
        for p in range(hn):
            qkv_ref[j, :, p * half : (p + 1) * half] = nn(lnx_ref[...], wq_buf[j, p]).astype(bf16)

    @pl.when(i == 4)
    def _():
        save_qkv().start()
        o.job.forward_all()
        blocks[0].begin()
        to_rows(vt_ref, qkv_ref.at[2])

    @pl.when(i == 8)
    def _():
        o.exchange()

    @pl.when(i == 11)
    def _():
        o.arrive()
        load_o().start()

    @pl.when(i == 9)
    def _():
        for k in range(2, tn - 1):
            step_z(k, lambda t: None)
        for b in nxt[:1]:
            b.job.begin()

    @pl.when(i == 14)
    def _():
        for b in blocks:
            b.forward()
        for b in nxt[1:]:
            b.job.begin()

    @pl.when((i >= 4) & (i < 4 + heads))
    def _():
        attend_forward_head(length, i - 4, qkv_ref.at[0], qkv_ref.at[1], vt_ref, sum_ref, log_ref)

    @pl.when(i == 4 + heads)
    def _():
        to_lanes(mixed_ref, sum_ref)
        saves[0].start()
        load_o().wait()
        br = sum(nt(mixed_ref[:, p * half : (p + 1) * half], wo_buf[p]) for p in range(hn))
        mid = br[:, width:].astype(bf16)
        mid_ref[...] = mid
        hidden_ref[...] = br[:, :width] + nn(mid, out_ref[number])

    @pl.when(i == 5 + heads)
    def _():
        def body(rows, start):
            v = real(x_buf[rows, :] + hidden_ref[rows, :], start, length)
            hidden_ref[rows, :] = v
            unit, _ = unit_of(v, width)
            ln2_ref[rows, 0:width] = real(unit * gain[...] + bias[...], start, length).astype(bf16)

        by_rows(n, 32, body)
        up_mid = nt(ln2_ref[:, 0:width], up_ref[number])
        lane = lax.broadcasted_iota(jnp.int32, (n, EXTRA - RANK), 1)
        ln2_ref[:, width : width + RANK] = up_mid.astype(bf16)
        ln2_ref[:, width + RANK :] = (lane == 0).astype(bf16)
        saves[1].start()
        saves[2].start()
        for b in blocks:
            b.exchange()
        save_qkv().wait()
        mine_z[0].wait()
        mine_a().wait()
        for d in range(1, tn):
            to_line(d).wait_send()
            p = lax.rem(z + tn - d, tn)
            comm.copy(small[d - 1], a2.at[p], ax.at[:, p], tensor=p).wait_recv()
        drain_z()
        for b in blocks:
            b.arrive()
        for w in qs + [o] + blocks:
            w.drain()
        for b in nxt:
            b.job.finish_first()
        for c in saves:
            c.wait()


def attention(sizes, wq, wo, wu, wd, bq, bp, bu, bd, ub, index, first, out, x, vectors, up):
    fn, hn, tn = sizes
    rows, half = wo.shape
    units = wu.shape[-1]
    width = fn * rows
    length = x.shape[0]
    n = padded(length)
    heads = width // HEAD_DIM
    early = 1
    any_ = pl.BlockSpec(memory_space=pl.ANY)
    one = lambda s: pl.BlockSpec(s, lambda i: (0,) * len(s), pipeline_mode=pl.Buffered(1))
    shape = jax.ShapeDtypeStruct
    nsem = 4 * (tree_sems(fn) + 2) + 3 * (tn - 1) + (early + 2) * block_sems(fn)
    hbm = [
        ((3, hn, width + RANK, half), bf16),
        ((hn, width + RANK, half), bf16),
        ((tn, rows, units), bf16),
        ((2, tn, EXTRA, units), bf16),
        ((n, width), bf16),
        ((3, n, width), bf16),
    ]
    outs = [
        ((3, n, RANK), bf16),
        ((n, width), bf16),
        ((heads, n), f32),
        ((n, width), f32),
        ((n, width + EXTRA), bf16),
        ((n, RANK), bf16),
    ]
    return pl.pallas_call(
        functools.partial(attention_kernel, sizes),
        grid=(6 + heads,),
        in_specs=[any_] * 4
        + [one(v.shape) for v in (bq, bp, bu, bd, ub)]
        + [pl.BlockSpec(memory_space=pltpu.SMEM)]
        + [one(first.shape), one(out.shape), any_, one(vectors.shape), one(up.shape)],
        out_specs=(any_,) * len(hbm) + tuple(any_ if k in (1, 3, 4) else one(s) for k, (s, _) in enumerate(outs)) + (any_,),
        out_shape=tuple(shape(*o) for o in hbm + outs) + (shape((tn, 2, width, units), bf16),),
        scratch_shapes=[
            pltpu.SemaphoreType.DMA((nsem,)),
            pltpu.SemaphoreType.DMA((nsem,)),
            pltpu.VMEM((3, hn, width + RANK, half), bf16),
            pltpu.VMEM((hn, width + RANK, half), bf16),
            pltpu.SemaphoreType.DMA((9,)),
            pltpu.SemaphoreType.DMA((5, 2)),
            pltpu.VMEM((3, rows, half), bf16),
            pltpu.VMEM((rows, half), bf16),
            pltpu.VMEM((rows, units), bf16),
            pltpu.VMEM((early, rows, units), bf16),
            pltpu.VMEM((3, hn, RANK, half), bf16),
            pltpu.VMEM((hn, RANK, half), bf16),
            pltpu.VMEM((tn, 2, EXTRA, units), bf16),
            pltpu.VMEM((3, n, width), bf16),
            pltpu.VMEM((n, width + RANK), bf16),
            pltpu.VMEM((width, n), f32),
            pltpu.VMEM((width, n), f32),
            pltpu.VMEM((n, width), f32),
            tail_shape(length, width),
            pltpu.SemaphoreType.DMA((2,)),
            pltpu.VMEM((n, width), bf16),
            pltpu.VMEM((n, width), f32),
            pltpu.VMEM((n, width + EXTRA), bf16),
        ],
        compiler_params=params(collective_id=3, has_side_effects=True),
        name="attention",
    )(wq, wo, wu, wd, bq, bp, bu, bd, ub, index, first, out, x, vectors, up)


def gelu_both(v, g):
    c, a = 0.7978845608028654, 0.044715
    sq = v * v
    t = jnp.tanh(v * (c + (c * a) * sq))
    half = 0.5 * (1.0 + t)
    slope = half + (0.5 * v) * ((1.0 - t * t) * (c + (3.0 * c * a) * sq))
    return v * half, g * slope


def mlp_half(ln_ref, g_ref, wu_ref, wd_ref, act_ref, gb_ref, out_acc, g_acc, rows, first, between):
    before = nn(ln_ref[rows, :], wu_ref[...])
    g_act = nn(g_ref[rows, :], wd_ref[...])
    act, gb = gelu_both(before, g_act)
    act, gb = act.astype(bf16), gb.astype(bf16)
    act_ref[rows, :] = act
    gb_ref[rows, :] = gb
    between()
    o, g = nt(act, wd_ref[...]), nt(gb, wu_ref[...])

    @pl.when(first)
    def _():
        out_acc[rows, :] = o
        g_acc[rows, :] = g

    @pl.when(jnp.logical_not(first))
    def _():
        out_acc[rows, :] += o
        g_acc[rows, :] += g


def mlp_kernel(
    sizes,
    length,
    done,
    plan,
    ln_ref,
    cot_ref,
    hidden_any,
    early,
    zw,
    ax,
    index,
    up_bank,
    down_bank,
    vectors,
    y_ref,
    gh_ref,
    g_up_in,
    g_down_out,
    g_units,
    late,
    send,
    recv,
    w_buf,
    w_sems,
    g_buf,
    tail,
    gx,
    act,
    gb,
    out_acc,
    g_acc,
    sem,
    own_buf,
    hidden_ref,
    hidden_sem,
):
    i = pl.program_id(0)
    fn, hn, tn = sizes
    f, h, z = lax.axis_index("fsdp"), lax.axis_index("heads"), lax.axis_index("tensor")
    n, width = hidden_ref.shape
    number = index[(f * hn + h) * tn + z]
    gain, dbias = vectors.at[2:3], vectors.at[4:5]
    main = slice(0, width)
    load_hidden = pltpu.make_async_copy(hidden_any, hidden_ref, hidden_sem)
    s, half = i // 2, lax.rem(i, 2)
    comm = Comm(send, recv)
    blocks = {b: Block(comm, sizes, zw, late.at[b], b, own_buf.at[b - done]) for b in range(done, tn)}
    resumed = [blocks[b] for b in range(done, min(done + 2, tn))]
    for b in resumed:
        b.job.first_done = True

    def loads(b):
        slot = b % 2
        return [
            pltpu.make_async_copy(late.at[b], w_buf.at[slot, :, pl.ds(0, width)], w_sems.at[slot, 0]),
            pltpu.make_async_copy(
                ax.at[:, lax.rem(z + b, tn)], w_buf.at[slot, :, pl.ds(width, EXTRA)], w_sems.at[slot, 1]
            ),
        ]

    @pl.when(i == 0)
    def _():
        c = Tokens(cot_ref, g_buf, tail, sem)
        c.start()
        load_hidden.start()
        for b in range(done):
            for w in loads(b):
                w.start()
        for b in resumed:
            b.mine().start()
        enter(sizes, f, h, z)
        for b in resumed:
            b.forward()
        for b in range(done + 2, tn):
            blocks[b].begin()
        c.wait()

        def body(rows, start):
            gx[rows, main] = g_buf[rows, :].astype(bf16)

        by_rows(n, 32, body)
        gx[:, width : width + RANK] = nt(gx[:, main], down_bank[number]).astype(bf16)
        gx[:, width + RANK :] = jnp.zeros((n, EXTRA - RANK), bf16)

    def events(steps):
        for at, what in steps:

            @pl.when(i == at)
            def _():
                for b, name in what:
                    if name == "load":
                        if b < tn:
                            if b in blocks:
                                blocks[b].arrive()
                            for w in loads(b):
                                w.start()
                    elif b in blocks:
                        getattr(blocks[b], name)()

    events(plan[0])

    for b in range(tn):

        @pl.when(i == 2 * b)
        def _():
            for w in loads(b):
                w.wait()

    slot = lax.rem(s, 2)
    rows = pl.ds(pl.multiple_of(half * (n // 2), n // 2), n // 2)
    mlp_half(ln_ref, gx, w_buf.at[slot, 0], w_buf.at[slot, 1], act, gb, out_acc, g_acc, rows, s == 0, lambda: events(plan[1]))

    @pl.when(half == 1)
    def _():
        g_units[0, s] = tn_(ln_ref[:, width : width + RANK], gb[...]).astype(bf16)
        g_units[1, s] = tn_(gx[:, width : width + RANK], act[...]).astype(bf16)

    @pl.when(i == pl.num_programs(0) - 1)
    def _():
        down_mid = out_acc[:, width : width + RANK].astype(bf16)
        g_up_mid = g_acc[:, width : width + RANK].astype(bf16)
        g_up_in[...] = tn_(g_up_mid, ln_ref[:, main]).astype(bf16)
        g_down_out[...] = tn_(down_mid, gx[:, main]).astype(bf16)
        out_acc[:, main] += nn(down_mid, down_bank[number])
        g_acc[:, main] += nn(g_up_mid, up_bank[number])

        load_hidden.wait()

        def body(rows, start):
            v = hidden_ref[rows, :]
            out_acc[rows, main] += v + dbias[...]
            gh_ref[rows, :] = g_buf[rows, :] + real(
                norm_back(g_acc[rows, main], v, gain[...], width), start, length
            )

        by_rows(n, 32, body)
        c = Tokens(y_ref, out_acc, tail, sem, out=True)
        c.start()
        for b in blocks.values():
            b.drain()
        c.wait()


def mlp(sizes, ln, cot, hidden, early, zw, ax, index, up, down, vectors):
    fn, hn, tn = sizes
    n, width = hidden.shape
    depth = ln.shape[1]
    units = early.shape[-1]
    done = 1
    length = cot.shape[0]
    late = max(tn - done, 1)
    plan = (
        (
            (2, ((2, "exchange"),)),
            (3, ((2, "load"),)),
            (4, ((3, "forward"),)),
            (5, ((3, "exchange"),)),
        ),
        (
            (0, ((1, "exchange"),)),
            (1, ((1, "load"),)),
            (5, ((3, "load"),)),
        ),
    )
    any_ = pl.BlockSpec(memory_space=pl.ANY)
    one = lambda s: pl.BlockSpec(s, lambda t: (0,) * len(s), pipeline_mode=pl.Buffered(1))
    shape = jax.ShapeDtypeStruct
    nsem = late * block_sems(fn)
    return pl.pallas_call(
        functools.partial(mlp_kernel, sizes, length, done, plan),
        grid=(2 * tn,),
        in_specs=[
            one((n, depth)),
            any_,
            any_,
            any_,
            any_,
            any_,
            pl.BlockSpec(memory_space=pltpu.SMEM),
            one(up.shape),
            one(down.shape),
            one(vectors.shape),
        ],
        out_specs=(
            any_,
            one((n, width)),
            one((RANK, width)),
            one((RANK, width)),
            one((2, tn, RANK, units)),
            any_,
        ),
        out_shape=(
            shape((length, 1, width), f32),
            shape((n, width), f32),
            shape((RANK, width), bf16),
            shape((RANK, width), bf16),
            shape((2, tn, RANK, units), bf16),
            shape(early.shape, bf16),
        ),
        input_output_aliases={3: 6 - 1},
        scratch_shapes=[
            pltpu.SemaphoreType.DMA((nsem,)),
            pltpu.SemaphoreType.DMA((nsem,)),
            pltpu.VMEM((2, 2, depth, units), bf16),
            pltpu.SemaphoreType.DMA((2, 2)),
            pltpu.VMEM((n, width), f32),
            tail_shape(length, width),
            pltpu.VMEM((n, depth), bf16),
            pltpu.VMEM((n, units), bf16),
            pltpu.VMEM((n, units), bf16),
            pltpu.VMEM((n, depth), f32),
            pltpu.VMEM((n, depth), f32),
            pltpu.SemaphoreType.DMA((2,)),
            pltpu.VMEM((late,) + zw.shape[1:], bf16),
            pltpu.VMEM((n, width), f32),
            pltpu.SemaphoreType.DMA(()),
        ],
        compiler_params=params(collective_id=4, has_side_effects=True),
        name="mlp",
    )(ln, cot, hidden, early, zw, ax, index, up, down, vectors)


def branch_back_kernel(
    place, index, gh_ref, w_ref, out_bank, mixed_ref, mid_ref, g_up_in, g_down_out, y_in, gm_ref, grads, y_out, gx, y_buf, sem
):
    n, width = gh_ref.shape
    half = w_ref.shape[-1]
    y = Bounce(y_in, y_buf, y_out, sem)
    y.start()

    def body(rows, start):
        gx[rows, 0:width] = gh_ref[rows, :].astype(bf16)

    by_rows(n, 32, body)
    g_mid = nt(gx[:, 0:width], out_bank[index[place()]]).astype(bf16)
    gx[:, width:] = g_mid
    grads[...] = jnp.zeros_like(grads)
    grads[0:RANK, :] = tn_(mid_ref[...], gx[:, 0:width]).astype(bf16)
    grads[RANK : 2 * RANK, :] = g_up_in[...]
    grads[2 * RANK : 3 * RANK, :] = g_down_out[...]
    grads[3 * RANK : 4 * RANK, :] = tn_(g_mid, mixed_ref[...]).astype(bf16)
    for p in range(w_ref.shape[0]):
        gm_ref[:, p * half : (p + 1) * half] = nn(gx[...], w_ref[p]).astype(bf16)
        if p == 0:
            y.turn()
    y.wait()


def branch_back(rows, place, index, gh, w, out, mixed, mid, g_up_in, g_down_out, y):
    n, width = gh.shape
    return pl.pallas_call(
        functools.partial(branch_back_kernel, place),
        in_specs=[pl.BlockSpec(memory_space=pltpu.SMEM)] + [pl.BlockSpec(memory_space=pltpu.VMEM)] * 7
        + [pl.BlockSpec(memory_space=pl.ANY)],
        out_specs=(pl.BlockSpec(memory_space=pltpu.VMEM),) * 2 + (pl.BlockSpec(memory_space=pl.ANY),),
        out_shape=(
            jax.ShapeDtypeStruct((n, width), bf16),
            jax.ShapeDtypeStruct((rows, width), bf16),
            jax.ShapeDtypeStruct(y.shape, f32),
        ),
        scratch_shapes=[
            pltpu.VMEM((n, width + RANK), bf16),
            pltpu.VMEM(y.shape, f32),
            pltpu.SemaphoreType.DMA(()),
        ],
        compiler_params=params(),
        name="branch_back",
    )(index, gh, w, out, mixed, mid, g_up_in, g_down_out, y)


def add_by_adapter(pick, parts):
    width = parts.shape[-1]
    if parts.shape[-2] % 16:
        parts = parts.astype(f32)
    return nn(pick[...], parts.reshape(-1, width).astype(bf16))


def picks(adapters, count, rows):
    shape = (count * rows, adapters.shape[0] * rows)
    place = jnp.repeat(adapters * rows, rows) + jnp.tile(jnp.arange(rows), adapters.shape[0])
    return (lax.broadcasted_iota(jnp.int32, shape, 0) == place[None, :]).astype(bf16)


def line_copies(comm, tn, z, here, sems, own=None):
    up, down = sems

    def send(sem, block, to, src=None):
        return comm.copy(sem, here(block) if src is None else src, here(block), tensor=to)

    def begin():
        @pl.when(z < tn - 1)
        def _():
            send(up[0], z, z + 1, own).start()

        @pl.when(z > 0)
        def _():
            send(down[0], z, z - 1, own).start()

    def step(k, then):
        @pl.when(z - 1 - k >= 0)
        def _():
            b = z - 1 - k
            comm.copy(up[k], here(b), here(b), tensor=z - 1).wait_recv()
            if k + 1 < tn - 1:

                @pl.when(z < tn - 1)
                def _():
                    send(up[k + 1], b, z + 1).start()

            then(b)

        @pl.when(z + 1 + k < tn)
        def _():
            b = z + 1 + k
            comm.copy(down[k], here(b), here(b), tensor=z + 1).wait_recv()
            if k + 1 < tn - 1:

                @pl.when(z > 0)
                def _():
                    send(down[k + 1], b, z - 1).start()

            then(b)

    def drain():
        for k in range(tn - 1):

            @pl.when((z < tn - 1) & (z - k >= 0))
            def _():
                send(up[k], z, z + 1).wait_send()

            @pl.when((z > 0) & (z + k < tn))
            def _():
                send(down[k], z, z - 1).wait_send()

    return begin, step, drain


class Reduce:
    def __init__(self, sizes, count, comm, hot, local, a, out, ra, dense, b=None, out_b=None, rb=None, hot_b=None):
        fn, hn, tn = sizes
        f, h, z = lax.axis_index("fsdp"), lax.axis_index("heads"), lax.axis_index("tensor")
        self.fn, self.hn, self.tn, self.f, self.h, self.z = fn, hn, tn, f, h, z
        self.count, self.comm, self.hot, self.hot_b, self.local = count, comm, hot, hot_b, local
        self.a, self.out, self.ra, self.dense, self.b, self.out_b, self.rb = a, out, ra, dense, b, out_b, rb
        self.piece = ra.shape[1]
        self.s_first = [comm.new() for _ in range(fn - 1)]
        s_line = ([comm.new() for _ in range(tn - 1)], [comm.new() for _ in range(tn - 1)])
        self.s_core = [comm.new() for _ in range(tn)]
        self.s_last = comm.new()
        self.sent = []
        per = count // hn
        self.mine, self.theirs = pl.ds(h * per, per), pl.ds((1 - h) * per, per)

        def slot(o, r):
            start, size = (0, per) if r is None else r
            return out.at[o, pl.ds(h * per + start, size)]

        self.spread = Rows(comm, fn, f, slot, per, lambda: dense, align=1)
        self.begin, self.line, self.drain_line = line_copies(
            comm, tn, z, lambda t: self.group(t, h), s_line
        )
        if b is not None:
            self.s_first_b = [comm.new() for _ in range(tn - 1)]
            self.s_core_b = comm.new()

            def slot_b(o, r):
                start, size = (0, tn) if r is None else r
                return rb.at[h, o, pl.ds(start, size)]

            self.spread_b = Rows(comm, fn, f, slot_b, tn, lambda: rb.at[h, f], align=1)

    def group(self, z, h):
        return self.ra.at[pl.ds((z * self.hn + h) * self.fn, self.fn)]

    def one(self, z, h, f):
        return self.ra.at[(z * self.hn + h) * self.fn + f]

    def rows(self, f):
        return self.a.at[pl.ds(pl.multiple_of(f * self.piece, 8), self.piece)]

    def send(self, make):
        make().start()
        self.sent.append(make)

    def own(self):
        copies = [pltpu.make_async_copy(self.rows(self.f), self.one(self.z, self.h, self.f), self.local.at[0])]
        if self.b is not None:
            copies.append(
                pltpu.make_async_copy(self.b.at[:, 0], self.rb.at[self.h, self.f, self.z], self.local.at[1])
            )
        return copies

    def start(self):
        f, h, z, comm = self.f, self.h, self.z, self.comm
        for m in range(1, self.fn):
            self.send(
                lambda m=m: comm.copy(
                    self.s_first[m - 1], self.rows(f ^ m), self.one(z, h, f), fsdp=f ^ m
                )
            )
        if self.b is not None:
            for d in range(1, self.tn):
                self.send(
                    lambda d=d: comm.copy(
                        self.s_first_b[d - 1],
                        self.b.at[:, d],
                        self.rb.at[h, f, z],
                        tensor=lax.rem(z + d, self.tn),
                    )
                )
        for c in self.own():
            c.start()

    def second(self):
        f, h, z, comm = self.f, self.h, self.z, self.comm
        for c in self.own():
            c.wait()
        for m in range(1, self.fn):
            b = self.one(z, h, f ^ m)
            comm.copy(self.s_first[m - 1], b, b, fsdp=f ^ m).wait_recv()
        self.begin()
        self.to_core(z).start()
        if self.b is not None:
            for d in range(1, self.tn):
                p = lax.rem(z + self.tn - d, self.tn)
                b = self.rb.at[h, f, p]
                comm.copy(self.s_first_b[d - 1], b, b, tensor=p).wait_recv()
            self.spread_b.begin()

    def to_core(self, block):
        b = self.group(block, self.h)
        return pltpu.make_async_remote_copy(
            src_ref=b,
            dst_ref=b,
            send_sem=self.comm.send.at[self.s_core[0] + block],
            recv_sem=self.comm.recv.at[self.s_core[0] + block],
            device_id={"heads": 1 - self.h},
            device_id_type=MESH,
        )

    def line_step(self, k):
        if k < self.tn - 1:
            self.line(k, lambda b: self.to_core(b).start())

    def forward_b(self):
        self.spread_b.forward_all()

    def exchange_b(self):
        self.spread_b.settle()
        b = self.rb.at[self.h]
        self.send(lambda: self.comm.copy(self.s_core_b, b, b, heads=1 - self.h))

    def fourth(self):
        h = self.h
        for k in range(self.tn):
            b = self.group(k, 1 - h)
            self.comm.copy(self.s_core[k], b, b, heads=1 - h).wait_recv()
        rows = self.hot.shape[0] // self.hn
        mine = self.hot.at[pl.ds(pl.multiple_of(self.h * rows, 16), rows)]
        total = add_by_adapter(mine, self.ra[...])
        self.dense[...] = total.reshape(self.dense.shape).astype(bf16)
        self.spread.begin()
        self.last().start()

    def last(self):
        return pltpu.make_async_copy(
            self.dense, self.out.at[self.f, self.mine], self.local.at[0]
        )

    def fifth(self):
        b = self.rb.at[1 - self.h]
        self.comm.copy(self.s_core_b, b, b, heads=1 - self.h).wait_recv()
        for k in range(2):
            total = add_by_adapter(self.hot_b, self.rb[:, :, :, k, :, :])
            self.out_b[k][...] = total.reshape(self.out_b[k].shape)

    def sixth(self):
        self.spread.forward_all()

    def seventh(self):
        self.last().wait()
        self.spread.settle()
        b = self.out.at[:, self.mine]
        self.send(lambda: self.comm.copy(self.s_last, b, b, heads=1 - self.h))

    def finish(self):
        h = self.h
        b = self.out.at[:, self.theirs]
        self.comm.copy(self.s_last, b, b, heads=1 - h).wait_recv()
        for make in self.sent:
            make().wait_send()
        self.drain_line()
        self.spread.drain()
        if self.b is not None:
            self.spread_b.drain()
        for k in range(self.tn):
            self.to_core(k).wait_send()


def reduce_sems(sizes, both):
    fn, hn, tn = sizes
    nb = bits_of(fn)
    tree = nb + 2 * (fn - 1 - nb)
    n = fn - 1 + 2 * (tn - 1) + tn + 1 + tree
    return n + (tn - 1 + 1 + tree if both else 0)


def enter_reduce(sizes, f, h, z):
    fn, hn, tn = sizes
    barrier = pltpu.get_barrier_semaphore()
    for m in range(1, fn):
        pl.semaphore_signal(barrier, 1, device_id={"fsdp": f ^ m}, device_id_type=MESH)
    pl.semaphore_signal(barrier, 1, device_id={"heads": 1 - h}, device_id_type=MESH)
    for d in range(1, tn):
        pl.semaphore_signal(barrier, 1, device_id={"tensor": lax.rem(z + d, tn)}, device_id_type=MESH)
    pl.semaphore_wait(barrier, fn - 1 + 1 + tn - 1)


def piece_rows(rows, fn):
    return -(-rows // (8 * fn)) * 8


def reduce_shapes(sizes, count, width, piece, units, both):
    fn, hn, tn = sizes
    n = fn * hn * tn
    shapes = [
        pltpu.SemaphoreType.DMA((reduce_sems(sizes, both),)),
        pltpu.SemaphoreType.DMA((reduce_sems(sizes, both),)),
        pltpu.SemaphoreType.DMA((2,)),
        pltpu.VMEM((n, piece, width), bf16),
        pltpu.VMEM((count // hn, piece, width), bf16),
    ]
    if both:
        shapes.append(pltpu.VMEM((hn, fn, tn, 2, RANK, units), bf16))
    return shapes


def attend_back_kernel(
    sizes, length, count, plan, hot, hot_b, q_ref, k_ref, v_ref, do_ref, log_ref, a, b, out_ref, sums, sums_u, sums_d, send, recv, local, ra, dense, rb, kt_ref, dq_ref, dk_ref, dv_ref
):
    head = pl.program_id(0)
    job = Reduce(sizes, count, Comm(send, recv), hot, local, a, sums, ra, dense, b, (sums_u, sums_d), rb, hot_b)

    @pl.when(head == 0)
    def _():
        enter_reduce(sizes, job.f, job.h, job.z)
        job.start()
        to_rows(kt_ref, k_ref.at[0])

        def clear(at):
            for r in (dk_ref, dv_ref):
                r[:, at] = jnp.zeros((r.shape[0], LANES), f32)

        columns(dk_ref.shape[1], clear)

    for at, what in plan:

        @pl.when(head == at)
        def _():
            for name, *more in what:
                getattr(job, name)(*more)

    attend_back_head(
        length, head, q_ref.at[0], k_ref.at[0], v_ref.at[0], do_ref, log_ref, kt_ref, dq_ref, dk_ref, dv_ref
    )

    @pl.when(head == pl.num_programs(0) - 1)
    def _():
        to_lanes(out_ref.at[0], dq_ref)

        def cast(at):
            out_ref[1, :, at] = dk_ref[:, at].astype(bf16)
            out_ref[2, :, at] = dv_ref[:, at].astype(bf16)

        columns(dk_ref.shape[1], cast)
        job.finish()


def attend_back(sizes, length, count, hot, hot_b, qkv, do, log, a, b):
    fn, hn, tn = sizes
    _, n, width = qkv.shape
    heads = width // HEAD_DIM
    units = b.shape[-1]
    piece = a.shape[0] // fn
    plan = (
        (2, (("second",),)),
        (5, (("line_step", 0),)),
        (7, (("line_step", 1), ("forward_b",))),
        (9, (("line_step", 2), ("exchange_b",))),
        (11, (("fourth",),)),
        (12, (("fifth",),)),
        (13, (("sixth",),)),
        (15, (("seventh",),)),
    )
    any_ = pl.BlockSpec(memory_space=pl.ANY)
    one = lambda j: pl.BlockSpec((1, n, width), lambda h: (j, 0, 0), pipeline_mode=pl.Buffered(1))
    return pl.pallas_call(
        functools.partial(attend_back_kernel, sizes, length, count, plan),
        grid=(heads,),
        in_specs=[
            whole(hot.shape),
            whole(hot_b.shape),
            one(0),
            one(1),
            one(2),
            whole((n, width)),
            whole((heads, n)),
            any_,
            any_,
        ],
        out_specs=(whole((3, n, width)), any_) + (whole((count, RANK, units)),) * 2,
        out_shape=(
            jax.ShapeDtypeStruct((3, n, width), bf16),
            jax.ShapeDtypeStruct((fn, count, piece, width), bf16),
        )
        + (jax.ShapeDtypeStruct((count, RANK, units), f32),) * 2,
        scratch_shapes=reduce_shapes(sizes, count, width, piece, units, True)
        + [pltpu.VMEM((width, n), f32)] * 2
        + [pltpu.VMEM((n, width), f32)] * 2,
        compiler_params=params(collective_id=1, has_side_effects=True),
        name="attend_back",
    )(hot, hot_b, qkv, qkv, qkv, do, log, a, b)


def project_back_kernel(
    sizes,
    count,
    hot,
    index,
    before,
    g_ref,
    w_any,
    first_ref,
    mid_ref,
    ln_ref,
    gh_any,
    x_ref,
    vectors,
    gi_ref,
    sums,
    a,
    g_proj_out,
    g_up_in,
    g_down_out,
    g_proj_in,
    send,
    recv,
    local,
    ra,
    dense,
    w_buf,
    gh_buf,
    w_sems,
    x_buf,
    tail,
    acc,
    grads,
    g_mid,
    sem,
    before_buf,
    w_rows,
):
    i = pl.program_id(0)
    length = x_ref.shape[0]
    n, width = ln_ref.shape
    half = w_buf.shape[-1]
    gain = vectors.at[0:1]
    parts = w_buf.shape[1]
    load = Tokens(x_ref, x_buf, tail, sem)
    job = Reduce(sizes, count, Comm(send, recv), hot, local, a, sums, ra, dense)
    number = index[(job.f * job.hn + job.h) * job.tn + job.z]

    def load_w(j):
        return pltpu.make_async_copy(w_any.at[j], w_buf.at[j], w_sems.at[j])

    load_gh = pltpu.make_async_copy(gh_any, gh_buf, w_sems.at[3])
    load_before = pltpu.make_async_copy(before, before_buf, w_sems.at[5])
    load_rows = pltpu.make_async_copy(w_any.at[:, :, pl.ds(width, RANK)], w_rows, w_sems.at[6])
    save = pltpu.make_async_copy(grads, a, w_sems.at[4])

    @pl.when(i == 0)
    def _():
        load_rows.start()
        for j in range(3):
            load_w(j).start()
        load.start()
        load_gh.start()
        load_before.start()
        enter_reduce(sizes, job.f, job.h, job.z)
        if grads.shape[0] > 6 * RANK:
            grads[6 * RANK :, :] = jnp.zeros((grads.shape[0] - 6 * RANK, width), bf16)
        load_rows.wait()

        def small(j, _):
            m = sum(
                nt(g_ref[j, :, p * half : (p + 1) * half], w_rows[j, p])
                for p in range(parts)
            ).astype(bf16)
            g_mid[j] = m
            at = pl.ds(pl.multiple_of((3 + j) * RANK, RANK), RANK)
            grads[at, :] = tn_(mid_ref[j], g_ref[j]).astype(bf16)
            return 0

        lax.fori_loop(0, 3, small, 0)
        mids = jnp.concatenate([g_mid[j].astype(f32).T for j in range(3)]).astype(bf16)
        grads[0 : 3 * RANK, :] = nn(mids, ln_ref[...]).astype(bf16)
        save.start()
        save.wait()
        job.start()

    @pl.when(i == 2)
    def _():
        job.second()

    @pl.when(i == 3)
    def _():
        job.line_step(0)

    @pl.when((i > 0) & (i < 4))
    def _():
        j = i - 1
        load_w(j).wait()
        r = nn(g_mid[j], first_ref[j, number])
        for p in range(parts):
            r = r + nt(g_ref[j, :, p * half : (p + 1) * half], w_buf[j, p, pl.ds(0, width), :])

        @pl.when(i == 1)
        def _():
            acc[...] = r

        @pl.when(i > 1)
        def _():
            acc[...] += r

    @pl.when(i == 4)
    def _():
        job.line_step(1)
        load.wait()
        load_gh.wait()

        def body(rows, start):
            v = x_buf[rows, :]
            acc[rows, :] = gh_buf[rows, :] + norm_back(acc[rows, :], v, gain[...], width)

        by_rows(n, 32, body)
        c = Tokens(gi_ref, acc, tail, sem, out=True)
        c.start()
        for k in range(2, sizes[2] - 1):
            job.line_step(k)
        job.fourth()
        load_before.wait()
        piece = before_buf.shape[2]

        def rows_of(k, r):
            k = k * RANK + r * 8
            return before_buf[k // piece, :, k % piece : k % piece + 8, :].astype(f32)

        for k, dst in enumerate((g_proj_out, g_up_in, g_down_out)):
            for r in range(2):
                dst[:, r * 8 : r * 8 + 8, :] = rows_of(k, r)

        for p in range(parts):

            @pl.when(job.h == p)
            def _():
                for r in range(2):
                    g_proj_in[:, r * 8 : r * 8 + 8, :] = rows_of(3, r)[:, :, p * half : (p + 1) * half]

        job.sixth()
        job.seventh()
        job.finish()
        c.wait()


def project_back(sizes, count, hot, index, before, g, w, first, mid, ln, gh, x, vectors):
    fn, hn, tn = sizes
    n, width = ln.shape
    parts, half = w.shape[1], w.shape[-1]
    length = x.shape[0]
    piece = piece_rows(6 * RANK, fn)
    any_ = pl.BlockSpec(memory_space=pl.ANY)
    one = lambda s: pl.BlockSpec(s, lambda t: (0,) * len(s), pipeline_mode=pl.Buffered(1))
    shape = jax.ShapeDtypeStruct
    return pl.pallas_call(
        functools.partial(project_back_kernel, sizes, count),
        grid=(5,),
        in_specs=[
            one(hot.shape),
            pl.BlockSpec(memory_space=pltpu.SMEM),
            any_,
            one(g.shape),
            any_,
            one(first.shape),
            one(mid.shape),
            one((n, width)),
            any_,
            any_,
            one(vectors.shape),
        ],
        out_specs=(any_, any_, any_) + (one((count, RANK, width)),) * 3 + (one((count, RANK, half)),),
        out_shape=(
            shape((length, 1, width), f32),
            shape((fn, count, piece, width), bf16),
            shape((fn * piece, width), bf16),
        )
        + (shape((count, RANK, width), f32),) * 3
        + (shape((count, RANK, half), f32),),
        scratch_shapes=reduce_shapes(sizes, count, width, piece, 0, False)
        + [
            pltpu.VMEM(w.shape, bf16),
            pltpu.VMEM((n, width), f32),
            pltpu.SemaphoreType.DMA((7,)),
            pltpu.VMEM((n, width), f32),
            tail_shape(length, width),
            pltpu.VMEM((n, width), f32),
            pltpu.VMEM((fn * piece, width), bf16),
            pltpu.VMEM(mid.shape, bf16),
            pltpu.SemaphoreType.DMA((2,)),
            pltpu.VMEM(before.shape, bf16),
            pltpu.VMEM((3, parts, RANK, half), bf16),
        ],
        compiler_params=params(collective_id=2, has_side_effects=True),
        name="qkv_back",
    )(hot, index, before, g, w, first, mid, ln, gh, x, vectors)


def finish_kernel(count, last_any, *refs):
    k = (len(refs) - 5) // 3
    passed, outs = refs[:k], refs[k + 2 : 2 * k + 2]
    g_in, g_out = refs[k : k + 2]
    bufs, last_buf, sems, last_sem = refs[2 * k + 2 : 3 * k + 2], *refs[3 * k + 2 :]
    load = pltpu.make_async_copy(last_any, last_buf, last_sem)
    load.start()
    moves = [Bounce(a, b, c, sems.at[i]) for i, (a, b, c) in enumerate(zip(passed, bufs, outs))]
    for m in moves:
        m.start()
    load.wait()
    piece, half = last_buf.shape[2], g_out.shape[-1]
    h = lax.axis_index("heads")

    def rows_of(j, r):
        at = j * RANK + r * 8
        return last_buf[at // piece, :, at % piece : at % piece + 8, :].astype(f32)

    for m in moves:
        m.turn()
    for j in range(3):
        for r in range(2):
            g_in[j, :, r * 8 : r * 8 + 8, :] = rows_of(j, r)
    for p in range(2):

        @pl.when(h == p)
        def _():
            for j in range(3):
                for r in range(2):
                    g_out[j, :, r * 8 : r * 8 + 8, :] = rows_of(3 + j, r)[:, :, p * half : (p + 1) * half]

    for m in moves:
        m.wait()


def finish(count, half, last, *passed):
    width = last.shape[-1]
    any_ = pl.BlockSpec(memory_space=pl.ANY)
    vmem = pl.BlockSpec(memory_space=pltpu.VMEM)
    shape = jax.ShapeDtypeStruct
    k = len(passed)
    return pl.pallas_call(
        functools.partial(finish_kernel, count),
        in_specs=[any_] * (k + 1),
        out_specs=(vmem, vmem) + (any_,) * k,
        out_shape=(shape((3, count, RANK, width), f32), shape((3, count, RANK, half), f32))
        + tuple(shape(v.shape, v.dtype) for v in passed),
        scratch_shapes=[pltpu.VMEM(v.shape, v.dtype) for v in passed]
        + [
            pltpu.VMEM(last.shape, bf16),
            pltpu.SemaphoreType.DMA((k,)),
            pltpu.SemaphoreType.DMA(()),
        ],
        compiler_params=params(),
        name="finish",
    )(last, *passed)


def per_device(
    inputs,
    cotangent,
    image_adapter_index,
    first_norm_gain,
    first_norm_bias,
    second_norm_gain,
    second_norm_bias,
    query_key_value_weight,
    attention_output_weight,
    up_weight,
    down_weight,
    up_projection_bias,
    down_projection_bias,
    query_key_value_adapter_first,
    query_key_value_adapter_second,
    projection_adapter_first,
    projection_adapter_second,
    up_adapter_first,
    up_adapter_second,
    down_adapter_first,
    down_adapter_second,
):
    sizes = tuple(lax.axis_size(a) for a in ("fsdp", "heads", "tensor"))
    fn, hn, tn = sizes
    f, h, z = (lax.axis_index(a) for a in ("fsdp", "heads", "tensor"))
    images, length, width = inputs.shape
    assert images == 1 and hn == 2
    count = query_key_value_adapter_first.shape[1]
    units = up_weight.shape[-1]
    x, cot = jnp.swapaxes(inputs, 0, 1), jnp.swapaxes(cotangent, 0, 1)
    vectors = jnp.concatenate(
        [
            first_norm_gain,
            first_norm_bias,
            second_norm_gain,
            second_norm_bias,
            down_projection_bias.astype(f32),
        ]
    ).reshape(5, width)
    index = image_adapter_index
    qkv_in = jnp.swapaxes(query_key_value_adapter_first, 2, 3)
    u_in = jnp.swapaxes(up_adapter_first, 1, 2)
    wq, wo, zw, ax, ln1, qkv, qkv_mid, mixed, log, hidden, ln2, proj_mid, early = attention(
        sizes,
        jnp.swapaxes(query_key_value_weight, 0, 1),
        attention_output_weight,
        up_weight,
        down_weight,
        query_key_value_adapter_second,
        jnp.swapaxes(projection_adapter_first, 1, 2),
        up_adapter_second,
        down_adapter_first,
        jnp.pad(up_projection_bias[None], ((0, EXTRA - RANK - 1), (0, 0))),
        index,
        qkv_in,
        projection_adapter_second,
        x,
        vectors,
        u_in,
    )
    y, g_hidden, g_up_in, g_down_out, g_units, _ = mlp(
        sizes, ln2, cot, hidden, early, zw, ax, index, u_in, down_adapter_second, vectors
    )
    g_mixed, grads, y = branch_back(
        piece_rows(4 * RANK, fn) * fn,
        lambda: (lax.axis_index("fsdp") * hn + lax.axis_index("heads")) * tn + lax.axis_index("tensor"),
        index,
        g_hidden,
        wo,
        projection_adapter_second,
        mixed,
        proj_mid,
        g_up_in,
        g_down_out,
        y,
    )
    by_place = image_adapter_index.reshape(fn, hn, tn)
    order = jnp.transpose(by_place, (2, 1, 0)).reshape(-1)
    order_b = jnp.transpose(by_place, (1, 0, 2)).reshape(-1)
    pick = picks(order, count, piece_rows(4 * RANK, fn))
    pick_b = picks(order_b, count, RANK)
    g_qkv, sums, g_up_out, g_down_in = attend_back(
        sizes, length, count, pick, pick_b, qkv, g_mixed, log, grads, g_units
    )
    g_x, last, _, g_proj_out, g_up_in, g_down_out, g_proj_in = project_back(
        sizes,
        count,
        picks(order, count, piece_rows(6 * RANK, fn)),
        index,
        sums,
        g_qkv,
        wq,
        qkv_in,
        qkv_mid,
        ln1,
        g_hidden,
        x,
        vectors,
    )
    g_qkv_in, g_qkv_out, g_x, g_proj_in, g_proj_out, g_up_in, g_up_out, g_down_in, g_down_out = finish(
        count, width // hn, last, g_x, g_proj_in, g_proj_out, g_up_in, g_up_out, g_down_in, g_down_out
    )
    return (
        jnp.swapaxes(y, 0, 1),
        jnp.swapaxes(g_x, 0, 1),
        jnp.swapaxes(g_qkv_in, 2, 3),
        g_qkv_out,
        jnp.swapaxes(g_proj_in, 1, 2),
        g_proj_out,
        jnp.swapaxes(g_up_in, 1, 2),
        g_up_out,
        g_down_in,
        g_down_out,
    )


def solution(mesh):
    in_specs = (
        P(("fsdp", "heads", "tensor"), None, None),
        P(("fsdp", "heads", "tensor"), None, None),
        P(),
        P(),
        P(),
        P(),
        P(),
        P("fsdp", None, "heads"),
        P("fsdp", "heads"),
        P("fsdp", "tensor"),
        P("fsdp", "tensor"),
        P("tensor"),
        P(),
        P(),
        P(None, None, None, "heads"),
        P(None, "heads", None),
        P(),
        P(),
        P(None, None, "tensor"),
        P(None, None, "tensor"),
        P(),
    )
    out_specs = (
        P(("fsdp", "heads", "tensor"), None, None),
        P(("fsdp", "heads", "tensor"), None, None),
        P(),
        P(None, None, None, "heads"),
        P(None, "heads", None),
        P(),
        P(),
        P(None, None, "tensor"),
        P(None, None, "tensor"),
        P(),
    )
    return jax.shard_map(
        per_device, mesh=mesh, in_specs=in_specs, out_specs=out_specs, check_vma=False
    )
```

```python
import functools
import jax
import jax.numpy as jnp
from jax import lax
from jax.experimental import pallas as pl
from jax.experimental.pallas import tpu as pltpu
from jax.sharding import PartitionSpec as P

HEAD_DIM = 72
norm_eps = 1e-06
f32 = jnp.float32
bf16 = jnp.bfloat16
MESH = pl.DeviceIdType.MESH


RANK = 16
EXTRA = 32


def padded(n):
    return -(-n // 16) * 16


def row_sums(v):
    return jnp.sum(v, axis=-1, keepdims=True)


class Tokens:
    def __init__(self, hbm, buf, tail, sems, out=False):
        self.length = hbm.shape[0]
        self.buf, self.tail, self.out = buf, tail, out
        self.whole = self.length // 8 * 8
        pairs = [(hbm.at[0 : self.whole, 0, :], buf.at[0 : self.whole, 0 : hbm.shape[-1]])]
        if self.whole < self.length:
            pairs.append((hbm.at[self.whole : self.length, 0, :], tail))
        self.copies = [
            pltpu.make_async_copy(*((b, a) if out else (a, b)), sems.at[i]) for i, (a, b) in enumerate(pairs)
        ]

    def start(self):
        if self.out and self.whole < self.length:
            self.tail[...] = self.buf[self.whole : self.length, 0 : self.tail.shape[-1]]
        for c in self.copies:
            c.start()

    def wait(self):
        for c in self.copies:
            c.wait()
        if not self.out:
            rest = self.buf.shape[0] - self.length
            zeros = jnp.zeros((rest, self.buf.shape[1]), f32)
            if self.whole < self.length:
                zeros = jnp.concatenate([self.tail[...], zeros])
            self.buf[self.whole :, :] = zeros


def tail_shape(length, width):
    return pltpu.VMEM((max(length % 8, 1), width), f32)


def unit_of(v, width):
    mean = row_sums(v) * (1.0 / width)
    centred = v - mean
    inverse = lax.rsqrt(row_sums(centred * centred) * (1.0 / width) + norm_eps)
    return centred * inverse, inverse


def by_rows(n, step, body):
    def one(r, _):
        body(pl.ds(pl.multiple_of(r * step, step), step), r * step)
        return 0

    lax.fori_loop(0, n // step, one, 0)


def real(v, start, length):
    row = lax.broadcasted_iota(jnp.int32, v.shape, 0) + start
    return jnp.where(row < length, v, 0.0)


def normalize_into(dst, src, gain, bias, length):
    n, width = src.shape

    def body(rows, start):
        unit, _ = unit_of(src[rows, :], width)
        dst[rows, 0:width] = real(unit * gain[...] + bias[...], start, length).astype(bf16)

    by_rows(n, 32, body)


def norm_back(grad, v, gain, width):
    unit, inverse = unit_of(v, width)
    e = grad * gain
    return inverse * (e - row_sums(e) * (1.0 / width) - unit * (row_sums(e * unit) * (1.0 / width)))


LANES = 128
SCALE = HEAD_DIM**-0.5
LOG2E = 1.4426950408889634


def nn(a, b):
    return lax.dot_general(a, b, (((1,), (0,)), ((), ())), preferred_element_type=f32)


def nt(a, b):
    return lax.dot_general(a, b, (((1,), (1,)), ((), ())), preferred_element_type=f32)


def tn_(a, b):
    return lax.dot_general(a, b, (((0,), (0,)), ((), ())), preferred_element_type=f32)


def whole(shape):
    return pl.BlockSpec(shape, lambda *_: (0,) * len(shape))


def params(limit=60, **more):
    return pltpu.CompilerParams(vmem_limit_bytes=limit << 20, **more)


def head_window(head, width):
    tile = jnp.minimum(head * HEAD_DIM // LANES, width // LANES - 2)
    return pl.ds(pl.multiple_of(tile * LANES, LANES), 2 * LANES), head * HEAD_DIM - tile * LANES


def only_head(values, start):
    lane = lax.broadcasted_iota(jnp.int32, values.shape, 1)
    return jnp.where((lane >= start) & (lane < start + HEAD_DIM), values, jnp.zeros_like(values))


def own_rows(head):
    return pl.ds(pl.multiple_of(head * HEAD_DIM, 8), HEAD_DIM)


def attend_forward_head(length, head, q_ref, k_ref, vt_ref, sum_ref, log_ref):
    win, start = head_window(head, q_ref.shape[-1])
    q = only_head(q_ref[:, win], start)
    v = vt_ref[own_rows(head), :].astype(bf16)
    s = nt(k_ref[:, win], q)
    key = lax.broadcasted_iota(jnp.int32, s.shape, 0)
    s = jnp.where(key < length, s, -1e30)
    top = jnp.max(s, axis=0, keepdims=True)
    p = jnp.exp2((s - top) * (SCALE * LOG2E))
    total = jnp.sum(p, axis=0, keepdims=True)
    sum_ref[own_rows(head), :] = nn(v, p.astype(bf16)) * (1.0 / total)
    log_ref[pl.ds(head, 1), :] = top * (SCALE * LOG2E) + jnp.log(total) * LOG2E


def attend_back_head(length, head, q_ref, k_ref, v_ref, do_ref, log_ref, kt_ref, dq_ref, dk_ref, dv_ref):
    win, start = head_window(head, q_ref.shape[-1])
    q = only_head(q_ref[:, win], start)
    k = k_ref[:, win]
    do = only_head(do_ref[:, win], start)
    s = nt(k, q)
    key = lax.broadcasted_iota(jnp.int32, s.shape, 0)
    p = jnp.exp2(jnp.where(key < length, s * (SCALE * LOG2E), -1e30) - log_ref[pl.ds(head, 1), :])
    dp = nt(v_ref[:, win], do)
    pd = p * dp
    ds = (pd - p * jnp.sum(pd, axis=0, keepdims=True)).astype(bf16)
    dv_ref[:, win] += nn(p.astype(bf16), do)
    dk_ref[:, win] += nn(ds, q) * SCALE
    dq_ref[own_rows(head), :] = nn(kt_ref[own_rows(head), :].astype(bf16), ds) * SCALE


def columns(width, body):
    def one(c, _):
        body(pl.ds(pl.multiple_of(c * LANES, LANES), LANES))
        return 0

    lax.fori_loop(0, width // LANES, one, 0)


def to_rows(dst, src):
    def body(at):
        dst[at, :] = src[:, at].astype(f32).T.astype(dst.dtype)

    columns(src.shape[1], body)


def to_lanes(dst, src):
    def body(at):
        dst[:, at] = src[at, :].T.astype(dst.dtype)

    columns(src.shape[0], body)


def bits_of(n):
    return n.bit_length() - 1


class Comm:
    def __init__(self, send, recv):
        self.send, self.recv, self.n = send, recv, 0

    def new(self):
        self.n += 1
        return self.n - 1

    def copy(self, i, src, dst, **where):
        return pltpu.make_async_remote_copy(
            src_ref=src,
            dst_ref=dst,
            send_sem=self.send.at[i],
            recv_sem=self.recv.at[i],
            device_id=where,
            device_id_type=MESH,
        )


def enter(axes_sizes, f, h, z):
    fn, hn, tn = axes_sizes
    barrier = pltpu.get_barrier_semaphore()
    count = 0
    for b in range(bits_of(fn)):
        pl.semaphore_signal(
            barrier, 1, device_id={"fsdp": f ^ (1 << b)}, device_id_type=MESH
        )
        count += 1
    pl.semaphore_signal(barrier, 1, device_id={"heads": 1 - h}, device_id_type=MESH)
    count += 1
    for d in range(1, tn):
        pl.semaphore_signal(
            barrier, 1, device_id={"tensor": lax.rem(z + d, tn)}, device_id_type=MESH
        )
        count += 1
    pl.semaphore_wait(barrier, count)


class Rows:
    def __init__(self, comm, fn, f, slot, rows, own, align=8):
        self.comm, self.fn, self.f, self.slot, self.own = comm, fn, f, slot, own
        self.nb = bits_of(fn)
        half = rows // 2 // align * align
        self.parts = ((0, half, list(range(self.nb))), (half, rows - half, list(range(self.nb))[::-1]))
        self.first = [comm.new() for _ in range(self.nb)]
        self.later = {}
        for p, (_, _, order) in enumerate(self.parts):
            for m in range(1, fn):
                last = max(order.index(b) for b in range(self.nb) if m >> b & 1)
                for b in order[last + 1 :]:
                    self.later[p, m, b] = comm.new()
        self.sent = []
        self.first_done = False

    def part(self, origin, p):
        start, size, _ = self.parts[p]
        return self.slot(origin, (start, size))

    def begin(self):
        for b in range(self.nb):
            self.send(
                lambda b=b: self.comm.copy(
                    self.first[b], self.own(), self.slot(self.f, None), fsdp=self.f ^ (1 << b)
                )
            )

    def _arrived(self, m, p):
        order = self.parts[p][2]
        last = max(order.index(b) for b in range(self.nb) if m >> b & 1)
        b = order[last]
        src = m ^ (1 << b)
        if src == 0:
            return None
        where = self.part(self.f ^ m, p)
        return self.comm.copy(self.later[p, src, b], where, where, fsdp=self.f ^ (1 << b))

    def forward(self, m):
        if m & (m - 1) == 0 and not self.first_done:
            b = bits_of(m)
            where = self.slot(self.f ^ m, None)
            self.comm.copy(self.first[b], where, where, fsdp=self.f ^ m).wait_recv()
        for p, (_, _, order) in enumerate(self.parts):
            if m & (m - 1):
                self._arrived(m, p).wait_recv()
            last = max(order.index(b) for b in range(self.nb) if m >> b & 1)
            for b in order[last + 1 :]:

                def onward(p=p, b=b):
                    where = self.part(self.f ^ m, p)
                    return self.comm.copy(self.later[p, m, b], where, where, fsdp=self.f ^ (1 << b))

                self.send(onward)

    def masks(self):
        return sorted(range(1, self.fn), key=lambda m: (bin(m).count("1"), m))

    def finish_first(self):
        for b in range(self.nb):
            where = self.slot(self.f ^ (1 << b), None)
            self.comm.copy(self.first[b], where, where, fsdp=self.f ^ (1 << b)).wait_recv()
        self.drain()

    def leaf(self, m):
        return not any(key[1] == m for key in self.later)

    def forward_all(self):
        for m in self.masks():
            if not self.leaf(m):
                self.forward(m)

    def settle(self):
        for m in self.masks():
            if self.leaf(m):
                self.forward(m)

    def send(self, make):
        make().start()
        self.sent.append(make)

    def drain(self):
        for make in self.sent:
            make().wait_send()


def tree_sems(fn):
    nb = bits_of(fn)
    return nb + 2 * (fn - 1 - nb)


class Bounce:
    def __init__(self, src, buf, dst, sem):
        self.load = pltpu.make_async_copy(src, buf, sem)
        self.save = pltpu.make_async_copy(buf, dst, sem)

    def start(self):
        self.load.start()

    def turn(self):
        self.load.wait()
        self.save.start()

    def wait(self):
        self.save.wait()


class Block:
    def __init__(self, comm, sizes, zw, dst, s, buf, own=None):
        fn, hn, tn = sizes
        f, h, z = lax.axis_index("fsdp"), lax.axis_index("heads"), lax.axis_index("tensor")
        rows = zw.shape[1]
        self.comm, self.dst, self.h, self.buf = comm, dst, h, buf
        t = lax.rem(z + s, tn)

        def slot(o, r):
            start, size = (0, rows) if r is None else r
            return dst.at[h, pl.ds(pl.multiple_of(o * rows + start, 8), size)]

        self.own = lambda: zw.at[t] if own is None else own
        self.slot = lambda: slot(f, None)
        self.job = Rows(comm, fn, f, slot, rows, self.own)
        self.local = comm.new()
        self.core = comm.new()

    def mine(self):
        return Bounce(self.own(), self.buf, self.slot(), self.comm.send.at[self.local])

    def to_core(self, which):
        b = self.dst.at[which]
        return self.comm.copy(self.core, b, b, heads=1 - self.h)

    def begin(self):
        self.job.begin()
        self.mine().start()

    def forward(self):
        self.mine().turn()
        self.job.forward_all()

    def exchange(self):
        self.job.settle()
        self.mine().wait()
        self.to_core(self.h).start()

    def arrive(self):
        self.to_core(1 - self.h).wait_recv()

    def drain(self):
        self.job.drain()
        self.to_core(self.h).wait_send()


def block_sems(fn):
    return tree_sems(fn) + 2


class Weight:
    def __init__(self, comm, fn, f, h, rows, own, dst, extra, own_sem, buf):
        self.comm, self.h, self.dst, self.extra = comm, h, dst, extra
        width = fn * rows
        self.main, self.more = pl.ds(0, width), pl.ds(width, RANK)

        def slot(o, r):
            start, size = (0, rows) if r is None else r
            return dst.at[h, pl.ds(pl.multiple_of(o * rows + start, 8), size)]

        self.job = Rows(comm, fn, f, slot, rows, lambda: own)
        self.core, self.core_extra = comm.new(), comm.new()
        self.mine = lambda: Bounce(own, buf, slot(f, None), own_sem.at[0])
        self.mine_extra = lambda: pltpu.make_async_copy(
            extra.at[h], dst.at[h, self.more], own_sem.at[1]
        )

    def start_extra(self):
        self.mine_extra().start()
        self.to_core_extra().start()

    def to_core_extra(self):
        return self.comm.copy(
            self.core_extra, self.extra.at[1 - self.h], self.dst.at[self.h, self.more], heads=1 - self.h
        )

    def to_core(self, which):
        b = self.dst.at[which, self.main]
        return self.comm.copy(self.core, b, b, heads=1 - self.h)

    def exchange(self):
        self.job.settle()
        self.mine().wait()
        self.to_core(self.h).start()

    def arrive(self):
        self.mine_extra().wait()
        where = self.dst.at[1 - self.h, self.more]
        self.comm.copy(self.core_extra, where, where, heads=1 - self.h).wait_recv()
        self.to_core(1 - self.h).wait_recv()

    def drain(self):
        self.job.drain()
        self.to_core(self.h).wait_send()
        self.to_core_extra().wait_send()


def attention_kernel(
    sizes,
    wq,
    wo,
    wu,
    wd,
    bq,
    bp,
    bu,
    bd,
    ub,
    index,
    first_ref,
    out_ref,
    x_ref,
    vectors,
    up_ref,
    oq,
    oo,
    zw,
    ax,
    ln_out,
    qkv_out,
    qmid_ref,
    mixed_out,
    log_ref,
    hidden_out,
    ln2_out,
    mid_ref,
    got,
    send,
    recv,
    wq_buf,
    wo_buf,
    w_sems,
    own_sems,
    own_q,
    own_o,
    own_z,
    own_b,
    aq,
    ap,
    a2,
    qkv_ref,
    lnx_ref,
    vt_ref,
    sum_ref,
    x_buf,
    x_tail,
    x_sems,
    mixed_ref,
    hidden_ref,
    ln2_ref,
):
    i = pl.program_id(0)
    fn, hn, tn = sizes
    f, h, z = lax.axis_index("fsdp"), lax.axis_index("heads"), lax.axis_index("tensor")
    rows, half = wo.shape
    length = x_ref.shape[0]
    n, width = mixed_ref.shape
    number = index[(f * hn + h) * tn + z]
    gain1, bias1, gain, bias = (vectors.at[k : k + 1] for k in range(4))
    heads = width // HEAD_DIM
    comm = Comm(send, recv)
    qs = [
        Weight(comm, fn, f, h, rows, wq.at[j], oq.at[j], aq.at[j], own_sems.at[j], own_q.at[j])
        for j in range(3)
    ]
    o = Weight(comm, fn, f, h, rows, wo, oo, ap, own_sems.at[3], own_o)
    line = ([comm.new() for _ in range(tn - 1)], [comm.new() for _ in range(tn - 1)])
    small = [comm.new() for _ in range(tn - 1)]
    blocks = [
        Block(comm, sizes, zw, got.at[b], b, own_b.at[b], own_z if b == 0 else None)
        for b in range(own_b.shape[0])
    ]
    nxt = [Block(comm, sizes, zw, got.at[b], b, own_z) for b in range(len(blocks), min(len(blocks) + 2, tn))]
    begin_z, step_z, drain_z = line_copies(comm, tn, z, lambda t: zw.at[t], line, own_z)
    mine_z = [Bounce(w, own_z, zw.at[z], own_sems.at[4, 0]) for w in (wu, wd)]
    mine_a = lambda: pltpu.make_async_copy(a2.at[z], ax.at[:, z], own_sems.at[4, 1])
    to_line = lambda d: comm.copy(
        small[d - 1], a2.at[lax.rem(z + d, tn)], ax.at[:, z], tensor=lax.rem(z + d, tn)
    )
    load_x = Tokens(x_ref, x_buf, x_tail, x_sems)
    load_q = lambda j: pltpu.make_async_copy(oq.at[j], wq_buf.at[j], w_sems.at[j])
    load_o = lambda: pltpu.make_async_copy(oo, wo_buf, w_sems.at[3])
    save_ln = lambda: pltpu.make_async_copy(lnx_ref.at[:, pl.ds(0, width)], ln_out, w_sems.at[4])
    saves = [
        pltpu.make_async_copy(a, b, w_sems.at[6 + k])
        for k, (a, b) in enumerate(((mixed_ref, mixed_out), (hidden_ref, hidden_out), (ln2_ref, ln2_out)))
    ]
    save_qkv = lambda: pltpu.make_async_copy(qkv_ref, qkv_out, w_sems.at[5])

    @pl.when(i == 0)
    def _():
        load_x.start()
        for w in qs + [o]:
            w.mine().start()
        for p in range(2):

            @pl.when(h == p)
            def _():
                mine_z[p].start()

        for p in range(hn):
            k = index[(f * hn + p) * tn + z]
            for j in range(3):
                aq[j, p] = bq[j, k]
            ap[p] = bp[k]
        for t in range(tn):
            k = index[(f * hn + h) * tn + t]
            a2[t, 0, 0:RANK] = bu[k]
            a2[t, 1, 0:RANK] = bd[k]
            a2[t, 0, RANK:] = ub[...]
            a2[t, 1, RANK:] = jnp.zeros_like(ub)
        enter(sizes, f, h, z)
        qs[0].job.begin()
        qs[1].job.begin()
        mine_z[0].turn()
        begin_z()
        for w in qs + [o]:
            w.start_extra()
        mine_a().start()
        for d in range(1, tn):
            to_line(d).start()
        for w in qs + [o]:
            w.mine().turn()
        load_x.wait()
        normalize_into(lnx_ref, x_buf, gain1, bias1, length)
        save_ln().start()

    @pl.when(i == 1)
    def _():
        qs[0].job.forward_all()
        qs[2].job.begin()
        qs[1].job.forward_all()
        step_z(0, lambda t: None)
        qs[0].exchange()
        qs[0].arrive()
        load_q(0).start()

    @pl.when(i == 2)
    def _():
        qs[2].job.forward_all()
        o.job.begin()
        qs[1].exchange()
        qs[1].arrive()
        load_q(1).start()
        qs[2].exchange()

    @pl.when(i == 3)
    def _():
        if tn > 2:
            step_z(1, lambda t: None)
        qs[2].arrive()
        load_q(2).start()

    @pl.when((i >= 1) & (i < 4))
    def _():
        j = i - 1
        mid = nt(lnx_ref[:, 0:width], first_ref[j, number]).astype(bf16)
        qmid_ref[j] = mid
        load_q(j).wait()

        @pl.when(i == 1)
        def _():
            save_ln().wait()

        lnx_ref[:, width:] = mid
        for p in range(hn):
            qkv_ref[j, :, p * half : (p + 1) * half] = nn(lnx_ref[...], wq_buf[j, p]).astype(bf16)

    @pl.when(i == 4)
    def _():
        save_qkv().start()
        o.job.forward_all()
        blocks[0].begin()
        to_rows(vt_ref, qkv_ref.at[2])

    @pl.when(i == 8)
    def _():
        o.exchange()

    @pl.when(i == 11)
    def _():
        o.arrive()
        load_o().start()

    @pl.when(i == 9)
    def _():
        for k in range(2, tn - 1):
            step_z(k, lambda t: None)
        for b in nxt[:1]:
            b.job.begin()

    @pl.when(i == 14)
    def _():
        for b in blocks:
            b.forward()
        for b in nxt[1:]:
            b.job.begin()

    @pl.when((i >= 4) & (i < 4 + heads))
    def _():
        attend_forward_head(length, i - 4, qkv_ref.at[0], qkv_ref.at[1], vt_ref, sum_ref, log_ref)

    @pl.when(i == 4 + heads)
    def _():
        to_lanes(mixed_ref, sum_ref)
        saves[0].start()
        load_o().wait()
        br = sum(nt(mixed_ref[:, p * half : (p + 1) * half], wo_buf[p]) for p in range(hn))
        mid = br[:, width:].astype(bf16)
        mid_ref[...] = mid
        hidden_ref[...] = br[:, :width] + nn(mid, out_ref[number])

    @pl.when(i == 5 + heads)
    def _():
        def body(rows, start):
            v = real(x_buf[rows, :] + hidden_ref[rows, :], start, length)
            hidden_ref[rows, :] = v
            unit, _ = unit_of(v, width)
            ln2_ref[rows, 0:width] = real(unit * gain[...] + bias[...], start, length).astype(bf16)

        by_rows(n, 32, body)
        up_mid = nt(ln2_ref[:, 0:width], up_ref[number])
        lane = lax.broadcasted_iota(jnp.int32, (n, EXTRA - RANK), 1)
        ln2_ref[:, width : width + RANK] = up_mid.astype(bf16)
        ln2_ref[:, width + RANK :] = (lane == 0).astype(bf16)
        saves[1].start()
        saves[2].start()
        for b in blocks:
            b.exchange()
        save_qkv().wait()
        mine_z[0].wait()
        mine_a().wait()
        for d in range(1, tn):
            to_line(d).wait_send()
            p = lax.rem(z + tn - d, tn)
            comm.copy(small[d - 1], a2.at[p], ax.at[:, p], tensor=p).wait_recv()
        drain_z()
        for b in blocks:
            b.arrive()
        for w in qs + [o] + blocks:
            w.drain()
        for b in nxt:
            b.job.finish_first()
        for c in saves:
            c.wait()


def attention(sizes, wq, wo, wu, wd, bq, bp, bu, bd, ub, index, first, out, x, vectors, up):
    fn, hn, tn = sizes
    rows, half = wo.shape
    units = wu.shape[-1]
    width = fn * rows
    length = x.shape[0]
    n = padded(length)
    heads = width // HEAD_DIM
    early = 1
    any_ = pl.BlockSpec(memory_space=pl.ANY)
    one = lambda s: pl.BlockSpec(s, lambda i: (0,) * len(s), pipeline_mode=pl.Buffered(1))
    shape = jax.ShapeDtypeStruct
    nsem = 4 * (tree_sems(fn) + 2) + 3 * (tn - 1) + (early + 2) * block_sems(fn)
    hbm = [
        ((3, hn, width + RANK, half), bf16),
        ((hn, width + RANK, half), bf16),
        ((tn, rows, units), bf16),
        ((2, tn, EXTRA, units), bf16),
        ((n, width), bf16),
        ((3, n, width), bf16),
    ]
    outs = [
        ((3, n, RANK), bf16),
        ((n, width), bf16),
        ((heads, n), f32),
        ((n, width), f32),
        ((n, width + EXTRA), bf16),
        ((n, RANK), bf16),
    ]
    return pl.pallas_call(
        functools.partial(attention_kernel, sizes),
        grid=(6 + heads,),
        in_specs=[any_] * 4
        + [one(v.shape) for v in (bq, bp, bu, bd, ub)]
        + [pl.BlockSpec(memory_space=pltpu.SMEM)]
        + [one(first.shape), one(out.shape), any_, one(vectors.shape), one(up.shape)],
        out_specs=(any_,) * len(hbm) + tuple(any_ if k in (1, 3, 4) else one(s) for k, (s, _) in enumerate(outs)) + (any_,),
        out_shape=tuple(shape(*o) for o in hbm + outs) + (shape((tn, 2, width, units), bf16),),
        scratch_shapes=[
            pltpu.SemaphoreType.DMA((nsem,)),
            pltpu.SemaphoreType.DMA((nsem,)),
            pltpu.VMEM((3, hn, width + RANK, half), bf16),
            pltpu.VMEM((hn, width + RANK, half), bf16),
            pltpu.SemaphoreType.DMA((9,)),
            pltpu.SemaphoreType.DMA((5, 2)),
            pltpu.VMEM((3, rows, half), bf16),
            pltpu.VMEM((rows, half), bf16),
            pltpu.VMEM((rows, units), bf16),
            pltpu.VMEM((early, rows, units), bf16),
            pltpu.VMEM((3, hn, RANK, half), bf16),
            pltpu.VMEM((hn, RANK, half), bf16),
            pltpu.VMEM((tn, 2, EXTRA, units), bf16),
            pltpu.VMEM((3, n, width), bf16),
            pltpu.VMEM((n, width + RANK), bf16),
            pltpu.VMEM((width, n), f32),
            pltpu.VMEM((width, n), f32),
            pltpu.VMEM((n, width), f32),
            tail_shape(length, width),
            pltpu.SemaphoreType.DMA((2,)),
            pltpu.VMEM((n, width), bf16),
            pltpu.VMEM((n, width), f32),
            pltpu.VMEM((n, width + EXTRA), bf16),
        ],
        compiler_params=params(collective_id=3, has_side_effects=True),
        name="attention",
    )(wq, wo, wu, wd, bq, bp, bu, bd, ub, index, first, out, x, vectors, up)


def gelu_both(v, g):
    c, a = 0.7978845608028654, 0.044715
    sq = v * v
    t = jnp.tanh(v * (c + (c * a) * sq))
    half = 0.5 * (1.0 + t)
    slope = half + (0.5 * v) * ((1.0 - t * t) * (c + (3.0 * c * a) * sq))
    return v * half, g * slope


def mlp_half(ln_ref, g_ref, wu_ref, wd_ref, act_ref, gb_ref, out_acc, g_acc, rows, first, between):
    before = nn(ln_ref[rows, :], wu_ref[...])
    g_act = nn(g_ref[rows, :], wd_ref[...])
    act, gb = gelu_both(before, g_act)
    act, gb = act.astype(bf16), gb.astype(bf16)
    act_ref[rows, :] = act
    gb_ref[rows, :] = gb
    between()
    o, g = nt(act, wd_ref[...]), nt(gb, wu_ref[...])

    @pl.when(first)
    def _():
        out_acc[rows, :] = o
        g_acc[rows, :] = g

    @pl.when(jnp.logical_not(first))
    def _():
        out_acc[rows, :] += o
        g_acc[rows, :] += g


def mlp_kernel(
    sizes,
    length,
    done,
    plan,
    ln_ref,
    cot_ref,
    hidden_any,
    early,
    zw,
    ax,
    index,
    up_bank,
    down_bank,
    vectors,
    y_ref,
    gh_out,
    g_up_in,
    g_down_out,
    g_units,
    late,
    send,
    recv,
    w_buf,
    w_sems,
    g_buf,
    tail,
    gx,
    act,
    gb,
    out_acc,
    g_acc,
    sem,
    own_buf,
    hidden_ref,
    hidden_sem,
    gh_ref,
):
    i = pl.program_id(0)
    fn, hn, tn = sizes
    f, h, z = lax.axis_index("fsdp"), lax.axis_index("heads"), lax.axis_index("tensor")
    n, width = hidden_ref.shape
    number = index[(f * hn + h) * tn + z]
    gain, dbias = vectors.at[2:3], vectors.at[4:5]
    main = slice(0, width)
    load_hidden = pltpu.make_async_copy(hidden_any, hidden_ref, hidden_sem)
    s, half = i // 2, lax.rem(i, 2)
    comm = Comm(send, recv)
    blocks = {b: Block(comm, sizes, zw, late.at[b], b, own_buf.at[b - done]) for b in range(done, tn)}
    resumed = [blocks[b] for b in range(done, min(done + 2, tn))]
    for b in resumed:
        b.job.first_done = True

    def loads(b):
        slot = b % 2
        return [
            pltpu.make_async_copy(late.at[b], w_buf.at[slot, :, pl.ds(0, width)], w_sems.at[slot, 0]),
            pltpu.make_async_copy(
                ax.at[:, lax.rem(z + b, tn)], w_buf.at[slot, :, pl.ds(width, EXTRA)], w_sems.at[slot, 1]
            ),
        ]

    @pl.when(i == 0)
    def _():
        c = Tokens(cot_ref, g_buf, tail, sem)
        c.start()
        load_hidden.start()
        for b in range(done):
            for w in loads(b):
                w.start()
        for b in resumed:
            b.mine().start()
        enter(sizes, f, h, z)
        for b in resumed:
            b.forward()
        for b in range(done + 2, tn):
            blocks[b].begin()
        c.wait()

        def body(rows, start):
            gx[rows, main] = g_buf[rows, :].astype(bf16)

        by_rows(n, 32, body)
        gx[:, width : width + RANK] = nt(gx[:, main], down_bank[number]).astype(bf16)
        gx[:, width + RANK :] = jnp.zeros((n, EXTRA - RANK), bf16)

    def events(steps):
        for at, what in steps:

            @pl.when(i == at)
            def _():
                for b, name in what:
                    if name == "load":
                        if b < tn:
                            if b in blocks:
                                blocks[b].arrive()
                            for w in loads(b):
                                w.start()
                    elif b in blocks:
                        getattr(blocks[b], name)()

    events(plan[0])

    for b in range(tn):

        @pl.when(i == 2 * b)
        def _():
            for w in loads(b):
                w.wait()

    slot = lax.rem(s, 2)
    rows = pl.ds(pl.multiple_of(half * (n // 2), n // 2), n // 2)
    mlp_half(ln_ref, gx, w_buf.at[slot, 0], w_buf.at[slot, 1], act, gb, out_acc, g_acc, rows, s == 0, lambda: events(plan[1]))

    @pl.when(half == 1)
    def _():
        g_units[0, s] = tn_(ln_ref[:, width : width + RANK], gb[...]).astype(bf16)
        g_units[1, s] = tn_(gx[:, width : width + RANK], act[...]).astype(bf16)

    @pl.when(i == pl.num_programs(0) - 1)
    def _():
        down_mid = out_acc[:, width : width + RANK].astype(bf16)
        g_up_mid = g_acc[:, width : width + RANK].astype(bf16)
        g_up_in[...] = tn_(g_up_mid, ln_ref[:, main]).astype(bf16)
        g_down_out[...] = tn_(down_mid, gx[:, main]).astype(bf16)
        out_acc[:, main] += nn(down_mid, down_bank[number])
        g_acc[:, main] += nn(g_up_mid, up_bank[number])

        load_hidden.wait()

        def body(rows, start):
            v = hidden_ref[rows, :]
            out_acc[rows, main] += v + dbias[...]
            gh_ref[rows, :] = g_buf[rows, :] + real(
                norm_back(g_acc[rows, main], v, gain[...], width), start, length
            )

        by_rows(n, 32, body)
        save = pltpu.make_async_copy(gh_ref, gh_out, hidden_sem)
        save.start()
        c = Tokens(y_ref, out_acc, tail, sem, out=True)
        c.start()
        for b in blocks.values():
            b.drain()
        c.wait()
        save.wait()


def mlp(sizes, ln, cot, hidden, early, zw, ax, index, up, down, vectors):
    fn, hn, tn = sizes
    n, width = hidden.shape
    depth = ln.shape[1]
    units = early.shape[-1]
    done = 1
    length = cot.shape[0]
    late = max(tn - done, 1)
    plan = (
        (
            (2, ((2, "exchange"),)),
            (3, ((2, "load"),)),
            (4, ((3, "forward"),)),
            (5, ((3, "exchange"),)),
        ),
        (
            (0, ((1, "exchange"),)),
            (1, ((1, "load"),)),
            (5, ((3, "load"),)),
        ),
    )
    any_ = pl.BlockSpec(memory_space=pl.ANY)
    one = lambda s: pl.BlockSpec(s, lambda t: (0,) * len(s), pipeline_mode=pl.Buffered(1))
    shape = jax.ShapeDtypeStruct
    nsem = late * block_sems(fn)
    return pl.pallas_call(
        functools.partial(mlp_kernel, sizes, length, done, plan),
        grid=(2 * tn,),
        in_specs=[
            one((n, depth)),
            any_,
            any_,
            any_,
            any_,
            any_,
            pl.BlockSpec(memory_space=pltpu.SMEM),
            one(up.shape),
            one(down.shape),
            one(vectors.shape),
        ],
        out_specs=(
            any_,
            any_,
            one((RANK, width)),
            one((RANK, width)),
            one((2, tn, RANK, units)),
            any_,
        ),
        out_shape=(
            shape((length, 1, width), f32),
            shape((n, width), f32),
            shape((RANK, width), bf16),
            shape((RANK, width), bf16),
            shape((2, tn, RANK, units), bf16),
            shape(early.shape, bf16),
        ),
        input_output_aliases={3: 6 - 1},
        scratch_shapes=[
            pltpu.SemaphoreType.DMA((nsem,)),
            pltpu.SemaphoreType.DMA((nsem,)),
            pltpu.VMEM((2, 2, depth, units), bf16),
            pltpu.SemaphoreType.DMA((2, 2)),
            pltpu.VMEM((n, width), f32),
            tail_shape(length, width),
            pltpu.VMEM((n, depth), bf16),
            pltpu.VMEM((n, units), bf16),
            pltpu.VMEM((n, units), bf16),
            pltpu.VMEM((n, depth), f32),
            pltpu.VMEM((n, depth), f32),
            pltpu.SemaphoreType.DMA((2,)),
            pltpu.VMEM((late,) + zw.shape[1:], bf16),
            pltpu.VMEM((n, width), f32),
            pltpu.SemaphoreType.DMA(()),
            pltpu.VMEM((n, width), f32),
        ],
        compiler_params=params(collective_id=4, has_side_effects=True),
        name="mlp",
    )(ln, cot, hidden, early, zw, ax, index, up, down, vectors)


def branch_back_kernel(
    place, index, gh_ref, w_ref, out_bank, mixed_ref, mid_ref, g_up_in, g_down_out, y_in, gm_ref, grads, y_out, gx, y_buf, sem
):
    n, width = gh_ref.shape
    half = w_ref.shape[-1]
    y = Bounce(y_in, y_buf, y_out, sem)
    y.start()

    def body(rows, start):
        gx[rows, 0:width] = gh_ref[rows, :].astype(bf16)

    by_rows(n, 32, body)
    g_mid = nt(gx[:, 0:width], out_bank[index[place()]]).astype(bf16)
    gx[:, width:] = g_mid
    grads[...] = jnp.zeros_like(grads)
    grads[0:RANK, :] = tn_(mid_ref[...], gx[:, 0:width]).astype(bf16)
    grads[RANK : 2 * RANK, :] = g_up_in[...]
    grads[2 * RANK : 3 * RANK, :] = g_down_out[...]
    grads[3 * RANK : 4 * RANK, :] = tn_(g_mid, mixed_ref[...]).astype(bf16)
    for p in range(w_ref.shape[0]):
        gm_ref[:, p * half : (p + 1) * half] = nn(gx[...], w_ref[p]).astype(bf16)
        if p == 0:
            y.turn()
    y.wait()


def branch_back(rows, place, index, gh, w, out, mixed, mid, g_up_in, g_down_out, y):
    n, width = gh.shape
    return pl.pallas_call(
        functools.partial(branch_back_kernel, place),
        in_specs=[pl.BlockSpec(memory_space=pltpu.SMEM)] + [pl.BlockSpec(memory_space=pltpu.VMEM)] * 7
        + [pl.BlockSpec(memory_space=pl.ANY)],
        out_specs=(pl.BlockSpec(memory_space=pltpu.VMEM),) * 2 + (pl.BlockSpec(memory_space=pl.ANY),),
        out_shape=(
            jax.ShapeDtypeStruct((n, width), bf16),
            jax.ShapeDtypeStruct((rows, width), bf16),
            jax.ShapeDtypeStruct(y.shape, f32),
        ),
        scratch_shapes=[
            pltpu.VMEM((n, width + RANK), bf16),
            pltpu.VMEM(y.shape, f32),
            pltpu.SemaphoreType.DMA(()),
        ],
        compiler_params=params(),
        name="branch_back",
    )(index, gh, w, out, mixed, mid, g_up_in, g_down_out, y)


def add_by_adapter(pick, parts):
    width = parts.shape[-1]
    if parts.shape[-2] % 16:
        parts = parts.astype(f32)
    return nn(pick[...], parts.reshape(-1, width).astype(bf16))


def picks(adapters, count, rows):
    shape = (count * rows, adapters.shape[0] * rows)
    place = jnp.repeat(adapters * rows, rows) + jnp.tile(jnp.arange(rows), adapters.shape[0])
    return (lax.broadcasted_iota(jnp.int32, shape, 0) == place[None, :]).astype(bf16)


def line_copies(comm, tn, z, here, sems, own=None):
    up, down = sems

    def send(sem, block, to, src=None):
        return comm.copy(sem, here(block) if src is None else src, here(block), tensor=to)

    def begin():
        @pl.when(z < tn - 1)
        def _():
            send(up[0], z, z + 1, own).start()

        @pl.when(z > 0)
        def _():
            send(down[0], z, z - 1, own).start()

    def step(k, then):
        @pl.when(z - 1 - k >= 0)
        def _():
            b = z - 1 - k
            comm.copy(up[k], here(b), here(b), tensor=z - 1).wait_recv()
            if k + 1 < tn - 1:

                @pl.when(z < tn - 1)
                def _():
                    send(up[k + 1], b, z + 1).start()

            then(b)

        @pl.when(z + 1 + k < tn)
        def _():
            b = z + 1 + k
            comm.copy(down[k], here(b), here(b), tensor=z + 1).wait_recv()
            if k + 1 < tn - 1:

                @pl.when(z > 0)
                def _():
                    send(down[k + 1], b, z - 1).start()

            then(b)

    def drain():
        for k in range(tn - 1):

            @pl.when((z < tn - 1) & (z - k >= 0))
            def _():
                send(up[k], z, z + 1).wait_send()

            @pl.when((z > 0) & (z + k < tn))
            def _():
                send(down[k], z, z - 1).wait_send()

    return begin, step, drain


class Reduce:
    def __init__(self, sizes, count, comm, hot, local, a, out, ra, dense, b=None, out_b=None, rb=None, hot_b=None):
        fn, hn, tn = sizes
        f, h, z = lax.axis_index("fsdp"), lax.axis_index("heads"), lax.axis_index("tensor")
        self.fn, self.hn, self.tn, self.f, self.h, self.z = fn, hn, tn, f, h, z
        self.count, self.comm, self.hot, self.hot_b, self.local = count, comm, hot, hot_b, local
        self.a, self.out, self.ra, self.dense, self.b, self.out_b, self.rb = a, out, ra, dense, b, out_b, rb
        self.piece = ra.shape[1]
        self.s_first = [comm.new() for _ in range(fn - 1)]
        s_line = ([comm.new() for _ in range(tn - 1)], [comm.new() for _ in range(tn - 1)])
        self.s_core = [comm.new() for _ in range(tn)]
        self.s_last = comm.new()
        self.sent = []
        per = count // hn
        self.mine, self.theirs = pl.ds(h * per, per), pl.ds((1 - h) * per, per)

        def slot(o, r):
            start, size = (0, per) if r is None else r
            return out.at[o, pl.ds(h * per + start, size)]

        self.spread = Rows(comm, fn, f, slot, per, lambda: dense, align=1)
        self.begin, self.line, self.drain_line = line_copies(
            comm, tn, z, lambda t: self.group(t, h), s_line
        )
        if b is not None:
            self.s_first_b = [comm.new() for _ in range(tn - 1)]
            self.s_core_b = comm.new()

            def slot_b(o, r):
                start, size = (0, tn) if r is None else r
                return rb.at[h, o, pl.ds(start, size)]

            self.spread_b = Rows(comm, fn, f, slot_b, tn, lambda: rb.at[h, f], align=1)

    def group(self, z, h):
        return self.ra.at[pl.ds((z * self.hn + h) * self.fn, self.fn)]

    def one(self, z, h, f):
        return self.ra.at[(z * self.hn + h) * self.fn + f]

    def rows(self, f):
        return self.a.at[pl.ds(pl.multiple_of(f * self.piece, 8), self.piece)]

    def send(self, make):
        make().start()
        self.sent.append(make)

    def own(self):
        copies = [pltpu.make_async_copy(self.rows(self.f), self.one(self.z, self.h, self.f), self.local.at[0])]
        if self.b is not None:
            copies.append(
                pltpu.make_async_copy(self.b.at[:, 0], self.rb.at[self.h, self.f, self.z], self.local.at[1])
            )
        return copies

    def start(self):
        f, h, z, comm = self.f, self.h, self.z, self.comm
        for m in range(1, self.fn):
            self.send(
                lambda m=m: comm.copy(
                    self.s_first[m - 1], self.rows(f ^ m), self.one(z, h, f), fsdp=f ^ m
                )
            )
        if self.b is not None:
            for d in range(1, self.tn):
                self.send(
                    lambda d=d: comm.copy(
                        self.s_first_b[d - 1],
                        self.b.at[:, d],
                        self.rb.at[h, f, z],
                        tensor=lax.rem(z + d, self.tn),
                    )
                )
        for c in self.own():
            c.start()

    def second(self):
        f, h, z, comm = self.f, self.h, self.z, self.comm
        for c in self.own():
            c.wait()
        for m in range(1, self.fn):
            b = self.one(z, h, f ^ m)
            comm.copy(self.s_first[m - 1], b, b, fsdp=f ^ m).wait_recv()
        self.begin()
        self.to_core(z).start()
        if self.b is not None:
            for d in range(1, self.tn):
                p = lax.rem(z + self.tn - d, self.tn)
                b = self.rb.at[h, f, p]
                comm.copy(self.s_first_b[d - 1], b, b, tensor=p).wait_recv()
            self.spread_b.begin()

    def to_core(self, block):
        b = self.group(block, self.h)
        return pltpu.make_async_remote_copy(
            src_ref=b,
            dst_ref=b,
            send_sem=self.comm.send.at[self.s_core[0] + block],
            recv_sem=self.comm.recv.at[self.s_core[0] + block],
            device_id={"heads": 1 - self.h},
            device_id_type=MESH,
        )

    def line_step(self, k):
        if k < self.tn - 1:
            self.line(k, lambda b: self.to_core(b).start())

    def forward_b(self):
        self.spread_b.forward_all()

    def exchange_b(self):
        self.spread_b.settle()
        b = self.rb.at[self.h]
        self.send(lambda: self.comm.copy(self.s_core_b, b, b, heads=1 - self.h))

    def fourth(self):
        h = self.h
        for k in range(self.tn):
            b = self.group(k, 1 - h)
            self.comm.copy(self.s_core[k], b, b, heads=1 - h).wait_recv()
        rows = self.hot.shape[0] // self.hn
        mine = self.hot.at[pl.ds(pl.multiple_of(self.h * rows, 16), rows)]
        total = add_by_adapter(mine, self.ra[...])
        self.dense[...] = total.reshape(self.dense.shape).astype(bf16)
        self.spread.begin()
        self.last().start()

    def last(self):
        return pltpu.make_async_copy(
            self.dense, self.out.at[self.f, self.mine], self.local.at[0]
        )

    def fifth(self):
        b = self.rb.at[1 - self.h]
        self.comm.copy(self.s_core_b, b, b, heads=1 - self.h).wait_recv()
        for k in range(2):
            total = add_by_adapter(self.hot_b, self.rb[:, :, :, k, :, :])
            self.out_b[k][...] = total.reshape(self.out_b[k].shape)

    def sixth(self):
        self.spread.forward_all()

    def seventh(self):
        self.last().wait()
        self.spread.settle()
        b = self.out.at[:, self.mine]
        self.send(lambda: self.comm.copy(self.s_last, b, b, heads=1 - self.h))

    def finish(self):
        h = self.h
        b = self.out.at[:, self.theirs]
        self.comm.copy(self.s_last, b, b, heads=1 - h).wait_recv()
        for make in self.sent:
            make().wait_send()
        self.drain_line()
        self.spread.drain()
        if self.b is not None:
            self.spread_b.drain()
        for k in range(self.tn):
            self.to_core(k).wait_send()


def reduce_sems(sizes, both):
    fn, hn, tn = sizes
    nb = bits_of(fn)
    tree = nb + 2 * (fn - 1 - nb)
    n = fn - 1 + 2 * (tn - 1) + tn + 1 + tree
    return n + (tn - 1 + 1 + tree if both else 0)


def enter_reduce(sizes, f, h, z):
    fn, hn, tn = sizes
    barrier = pltpu.get_barrier_semaphore()
    for m in range(1, fn):
        pl.semaphore_signal(barrier, 1, device_id={"fsdp": f ^ m}, device_id_type=MESH)
    pl.semaphore_signal(barrier, 1, device_id={"heads": 1 - h}, device_id_type=MESH)
    for d in range(1, tn):
        pl.semaphore_signal(barrier, 1, device_id={"tensor": lax.rem(z + d, tn)}, device_id_type=MESH)
    pl.semaphore_wait(barrier, fn - 1 + 1 + tn - 1)


def piece_rows(rows, fn):
    return -(-rows // (8 * fn)) * 8


def reduce_shapes(sizes, count, width, piece, units, both):
    fn, hn, tn = sizes
    n = fn * hn * tn
    shapes = [
        pltpu.SemaphoreType.DMA((reduce_sems(sizes, both),)),
        pltpu.SemaphoreType.DMA((reduce_sems(sizes, both),)),
        pltpu.SemaphoreType.DMA((2,)),
        pltpu.VMEM((n, piece, width), bf16),
        pltpu.VMEM((count // hn, piece, width), bf16),
    ]
    if both:
        shapes.append(pltpu.VMEM((hn, fn, tn, 2, RANK, units), bf16))
    return shapes


def attend_back_kernel(
    sizes, length, count, plan, hot, hot_b, q_ref, k_ref, v_ref, do_ref, log_ref, a, b, out_ref, sums, sums_u, sums_d, send, recv, local, ra, dense, rb, kt_ref, dq_ref, dk_ref, dv_ref
):
    head = pl.program_id(0)
    job = Reduce(sizes, count, Comm(send, recv), hot, local, a, sums, ra, dense, b, (sums_u, sums_d), rb, hot_b)

    @pl.when(head == 0)
    def _():
        enter_reduce(sizes, job.f, job.h, job.z)
        job.start()
        to_rows(kt_ref, k_ref.at[0])

        def clear(at):
            for r in (dk_ref, dv_ref):
                r[:, at] = jnp.zeros((r.shape[0], LANES), f32)

        columns(dk_ref.shape[1], clear)

    for at, what in plan:

        @pl.when(head == at)
        def _():
            for name, *more in what:
                getattr(job, name)(*more)

    attend_back_head(
        length, head, q_ref.at[0], k_ref.at[0], v_ref.at[0], do_ref, log_ref, kt_ref, dq_ref, dk_ref, dv_ref
    )

    @pl.when(head == pl.num_programs(0) - 1)
    def _():
        to_lanes(out_ref.at[0], dq_ref)

        def cast(at):
            out_ref[1, :, at] = dk_ref[:, at].astype(bf16)
            out_ref[2, :, at] = dv_ref[:, at].astype(bf16)

        columns(dk_ref.shape[1], cast)
        job.finish()


def attend_back(sizes, length, count, hot, hot_b, qkv, do, log, a, b):
    fn, hn, tn = sizes
    _, n, width = qkv.shape
    heads = width // HEAD_DIM
    units = b.shape[-1]
    piece = a.shape[0] // fn
    plan = (
        (2, (("second",),)),
        (5, (("line_step", 0),)),
        (7, (("line_step", 1), ("forward_b",))),
        (9, (("line_step", 2), ("exchange_b",))),
        (11, (("fourth",),)),
        (12, (("fifth",),)),
        (13, (("sixth",),)),
        (15, (("seventh",),)),
    )
    any_ = pl.BlockSpec(memory_space=pl.ANY)
    one = lambda j: pl.BlockSpec((1, n, width), lambda h: (j, 0, 0), pipeline_mode=pl.Buffered(1))
    return pl.pallas_call(
        functools.partial(attend_back_kernel, sizes, length, count, plan),
        grid=(heads,),
        in_specs=[
            whole(hot.shape),
            whole(hot_b.shape),
            one(0),
            one(1),
            one(2),
            whole((n, width)),
            whole((heads, n)),
            any_,
            any_,
        ],
        out_specs=(whole((3, n, width)), any_) + (whole((count, RANK, units)),) * 2,
        out_shape=(
            jax.ShapeDtypeStruct((3, n, width), bf16),
            jax.ShapeDtypeStruct((fn, count, piece, width), bf16),
        )
        + (jax.ShapeDtypeStruct((count, RANK, units), f32),) * 2,
        scratch_shapes=reduce_shapes(sizes, count, width, piece, units, True)
        + [pltpu.VMEM((width, n), f32)] * 2
        + [pltpu.VMEM((n, width), f32)] * 2,
        compiler_params=params(collective_id=1, has_side_effects=True),
        name="attend_back",
    )(hot, hot_b, qkv, qkv, qkv, do, log, a, b)


def project_back_kernel(
    sizes,
    count,
    hot,
    index,
    before,
    g_ref,
    w_any,
    first_ref,
    mid_ref,
    ln_ref,
    gh_any,
    x_ref,
    vectors,
    gi_ref,
    sums,
    a,
    g_proj_out,
    g_up_in,
    g_down_out,
    g_proj_in,
    send,
    recv,
    local,
    ra,
    dense,
    w_buf,
    gh_buf,
    w_sems,
    x_buf,
    tail,
    acc,
    grads,
    g_mid,
    sem,
    before_buf,
    w_rows,
):
    i = pl.program_id(0)
    length = x_ref.shape[0]
    n, width = ln_ref.shape
    half = w_buf.shape[-1]
    gain = vectors.at[0:1]
    parts = w_buf.shape[1]
    load = Tokens(x_ref, x_buf, tail, sem)
    job = Reduce(sizes, count, Comm(send, recv), hot, local, a, sums, ra, dense)
    number = index[(job.f * job.hn + job.h) * job.tn + job.z]

    def load_w(j):
        return pltpu.make_async_copy(w_any.at[j], w_buf.at[j], w_sems.at[j])

    load_gh = pltpu.make_async_copy(gh_any, gh_buf, w_sems.at[3])
    load_before = pltpu.make_async_copy(before, before_buf, w_sems.at[5])
    load_rows = pltpu.make_async_copy(w_any.at[:, :, pl.ds(width, RANK)], w_rows, w_sems.at[6])
    save = pltpu.make_async_copy(grads, a, w_sems.at[4])

    @pl.when(i == 0)
    def _():
        load_rows.start()
        for j in range(3):
            load_w(j).start()
        load.start()
        load_gh.start()
        load_before.start()
        enter_reduce(sizes, job.f, job.h, job.z)
        if grads.shape[0] > 6 * RANK:
            grads[6 * RANK :, :] = jnp.zeros((grads.shape[0] - 6 * RANK, width), bf16)
        load_rows.wait()

        def small(j, _):
            m = sum(
                nt(g_ref[j, :, p * half : (p + 1) * half], w_rows[j, p])
                for p in range(parts)
            ).astype(bf16)
            g_mid[j] = m
            at = pl.ds(pl.multiple_of((3 + j) * RANK, RANK), RANK)
            grads[at, :] = tn_(mid_ref[j], g_ref[j]).astype(bf16)
            return 0

        lax.fori_loop(0, 3, small, 0)
        mids = jnp.concatenate([g_mid[j].astype(f32).T for j in range(3)]).astype(bf16)
        grads[0 : 3 * RANK, :] = nn(mids, ln_ref[...]).astype(bf16)
        save.start()
        save.wait()
        job.start()

    @pl.when(i == 2)
    def _():
        job.second()

    @pl.when(i == 3)
    def _():
        job.line_step(0)

    @pl.when((i > 0) & (i < 4))
    def _():
        j = i - 1
        load_w(j).wait()
        r = nn(g_mid[j], first_ref[j, number])
        for p in range(parts):
            r = r + nt(g_ref[j, :, p * half : (p + 1) * half], w_buf[j, p, pl.ds(0, width), :])

        @pl.when(i == 1)
        def _():
            acc[...] = r

        @pl.when(i > 1)
        def _():
            acc[...] += r

    @pl.when(i == 4)
    def _():
        job.line_step(1)
        load.wait()
        load_gh.wait()

        def body(rows, start):
            v = x_buf[rows, :]
            acc[rows, :] = gh_buf[rows, :] + norm_back(acc[rows, :], v, gain[...], width)

        by_rows(n, 32, body)
        c = Tokens(gi_ref, acc, tail, sem, out=True)
        c.start()
        for k in range(2, sizes[2] - 1):
            job.line_step(k)
        job.fourth()
        load_before.wait()
        piece = before_buf.shape[2]

        def rows_of(k, r):
            k = k * RANK + r * 8
            return before_buf[k // piece, :, k % piece : k % piece + 8, :].astype(f32)

        for k, dst in enumerate((g_proj_out, g_up_in, g_down_out)):
            for r in range(2):
                dst[:, r * 8 : r * 8 + 8, :] = rows_of(k, r)

        for p in range(parts):

            @pl.when(job.h == p)
            def _():
                for r in range(2):
                    g_proj_in[:, r * 8 : r * 8 + 8, :] = rows_of(3, r)[:, :, p * half : (p + 1) * half]

        job.sixth()
        job.seventh()
        job.finish()
        c.wait()


def project_back(sizes, count, hot, index, before, g, w, first, mid, ln, gh, x, vectors):
    fn, hn, tn = sizes
    n, width = ln.shape
    parts, half = w.shape[1], w.shape[-1]
    length = x.shape[0]
    piece = piece_rows(6 * RANK, fn)
    any_ = pl.BlockSpec(memory_space=pl.ANY)
    one = lambda s: pl.BlockSpec(s, lambda t: (0,) * len(s), pipeline_mode=pl.Buffered(1))
    shape = jax.ShapeDtypeStruct
    return pl.pallas_call(
        functools.partial(project_back_kernel, sizes, count),
        grid=(5,),
        in_specs=[
            one(hot.shape),
            pl.BlockSpec(memory_space=pltpu.SMEM),
            any_,
            one(g.shape),
            any_,
            one(first.shape),
            one(mid.shape),
            one((n, width)),
            any_,
            any_,
            one(vectors.shape),
        ],
        out_specs=(any_, any_, any_) + (one((count, RANK, width)),) * 3 + (one((count, RANK, half)),),
        out_shape=(
            shape((length, 1, width), f32),
            shape((fn, count, piece, width), bf16),
            shape((fn * piece, width), bf16),
        )
        + (shape((count, RANK, width), f32),) * 3
        + (shape((count, RANK, half), f32),),
        scratch_shapes=reduce_shapes(sizes, count, width, piece, 0, False)
        + [
            pltpu.VMEM(w.shape, bf16),
            pltpu.VMEM((n, width), f32),
            pltpu.SemaphoreType.DMA((7,)),
            pltpu.VMEM((n, width), f32),
            tail_shape(length, width),
            pltpu.VMEM((n, width), f32),
            pltpu.VMEM((fn * piece, width), bf16),
            pltpu.VMEM(mid.shape, bf16),
            pltpu.SemaphoreType.DMA((2,)),
            pltpu.VMEM(before.shape, bf16),
            pltpu.VMEM((3, parts, RANK, half), bf16),
        ],
        compiler_params=params(collective_id=2, has_side_effects=True),
        name="qkv_back",
    )(hot, index, before, g, w, first, mid, ln, gh, x, vectors)


def finish_kernel(count, last_any, *refs):
    k = (len(refs) - 5) // 3
    passed, outs = refs[:k], refs[k + 2 : 2 * k + 2]
    g_in, g_out = refs[k : k + 2]
    bufs, last_buf, sems, last_sem = refs[2 * k + 2 : 3 * k + 2], *refs[3 * k + 2 :]
    load = pltpu.make_async_copy(last_any, last_buf, last_sem)
    load.start()
    moves = [Bounce(a, b, c, sems.at[i]) for i, (a, b, c) in enumerate(zip(passed, bufs, outs))]
    for m in moves:
        m.start()
    load.wait()
    piece, half = last_buf.shape[2], g_out.shape[-1]
    h = lax.axis_index("heads")

    def rows_of(j, r):
        at = j * RANK + r * 8
        return last_buf[at // piece, :, at % piece : at % piece + 8, :].astype(f32)

    for m in moves:
        m.turn()
    for j in range(3):
        for r in range(2):
            g_in[j, :, r * 8 : r * 8 + 8, :] = rows_of(j, r)
    for p in range(2):

        @pl.when(h == p)
        def _():
            for j in range(3):
                for r in range(2):
                    g_out[j, :, r * 8 : r * 8 + 8, :] = rows_of(3 + j, r)[:, :, p * half : (p + 1) * half]

    for m in moves:
        m.wait()


def finish(count, half, last, *passed):
    width = last.shape[-1]
    any_ = pl.BlockSpec(memory_space=pl.ANY)
    vmem = pl.BlockSpec(memory_space=pltpu.VMEM)
    shape = jax.ShapeDtypeStruct
    k = len(passed)
    return pl.pallas_call(
        functools.partial(finish_kernel, count),
        in_specs=[any_] * (k + 1),
        out_specs=(vmem, vmem) + (any_,) * k,
        out_shape=(shape((3, count, RANK, width), f32), shape((3, count, RANK, half), f32))
        + tuple(shape(v.shape, v.dtype) for v in passed),
        scratch_shapes=[pltpu.VMEM(v.shape, v.dtype) for v in passed]
        + [
            pltpu.VMEM(last.shape, bf16),
            pltpu.SemaphoreType.DMA((k,)),
            pltpu.SemaphoreType.DMA(()),
        ],
        compiler_params=params(),
        name="finish",
    )(last, *passed)


def per_device(
    inputs,
    cotangent,
    image_adapter_index,
    first_norm_gain,
    first_norm_bias,
    second_norm_gain,
    second_norm_bias,
    query_key_value_weight,
    attention_output_weight,
    up_weight,
    down_weight,
    up_projection_bias,
    down_projection_bias,
    query_key_value_adapter_first,
    query_key_value_adapter_second,
    projection_adapter_first,
    projection_adapter_second,
    up_adapter_first,
    up_adapter_second,
    down_adapter_first,
    down_adapter_second,
):
    sizes = tuple(lax.axis_size(a) for a in ("fsdp", "heads", "tensor"))
    fn, hn, tn = sizes
    f, h, z = (lax.axis_index(a) for a in ("fsdp", "heads", "tensor"))
    images, length, width = inputs.shape
    assert images == 1 and hn == 2
    count = query_key_value_adapter_first.shape[1]
    units = up_weight.shape[-1]
    x, cot = jnp.swapaxes(inputs, 0, 1), jnp.swapaxes(cotangent, 0, 1)
    vectors = jnp.concatenate(
        [
            first_norm_gain,
            first_norm_bias,
            second_norm_gain,
            second_norm_bias,
            down_projection_bias.astype(f32),
        ]
    ).reshape(5, width)
    index = image_adapter_index
    qkv_in = jnp.swapaxes(query_key_value_adapter_first, 2, 3)
    u_in = jnp.swapaxes(up_adapter_first, 1, 2)
    wq, wo, zw, ax, ln1, qkv, qkv_mid, mixed, log, hidden, ln2, proj_mid, early = attention(
        sizes,
        jnp.swapaxes(query_key_value_weight, 0, 1),
        attention_output_weight,
        up_weight,
        down_weight,
        query_key_value_adapter_second,
        jnp.swapaxes(projection_adapter_first, 1, 2),
        up_adapter_second,
        down_adapter_first,
        jnp.pad(up_projection_bias[None], ((0, EXTRA - RANK - 1), (0, 0))),
        index,
        qkv_in,
        projection_adapter_second,
        x,
        vectors,
        u_in,
    )
    y, g_hidden, g_up_in, g_down_out, g_units, _ = mlp(
        sizes, ln2, cot, hidden, early, zw, ax, index, u_in, down_adapter_second, vectors
    )
    g_mixed, grads, y = branch_back(
        piece_rows(4 * RANK, fn) * fn,
        lambda: (lax.axis_index("fsdp") * hn + lax.axis_index("heads")) * tn + lax.axis_index("tensor"),
        index,
        g_hidden,
        wo,
        projection_adapter_second,
        mixed,
        proj_mid,
        g_up_in,
        g_down_out,
        y,
    )
    by_place = image_adapter_index.reshape(fn, hn, tn)
    order = jnp.transpose(by_place, (2, 1, 0)).reshape(-1)
    order_b = jnp.transpose(by_place, (1, 0, 2)).reshape(-1)
    pick = picks(order, count, piece_rows(4 * RANK, fn))
    pick_b = picks(order_b, count, RANK)
    g_qkv, sums, g_up_out, g_down_in = attend_back(
        sizes, length, count, pick, pick_b, qkv, g_mixed, log, grads, g_units
    )
    g_x, last, _, g_proj_out, g_up_in, g_down_out, g_proj_in = project_back(
        sizes,
        count,
        picks(order, count, piece_rows(6 * RANK, fn)),
        index,
        sums,
        g_qkv,
        wq,
        qkv_in,
        qkv_mid,
        ln1,
        g_hidden,
        x,
        vectors,
    )
    g_qkv_in, g_qkv_out, g_x, g_proj_in, g_proj_out, g_up_in, g_up_out, g_down_in, g_down_out = finish(
        count, width // hn, last, g_x, g_proj_in, g_proj_out, g_up_in, g_up_out, g_down_in, g_down_out
    )
    return (
        jnp.swapaxes(y, 0, 1),
        jnp.swapaxes(g_x, 0, 1),
        jnp.swapaxes(g_qkv_in, 2, 3),
        g_qkv_out,
        jnp.swapaxes(g_proj_in, 1, 2),
        g_proj_out,
        jnp.swapaxes(g_up_in, 1, 2),
        g_up_out,
        g_down_in,
        g_down_out,
    )


def solution(mesh):
    in_specs = (
        P(("fsdp", "heads", "tensor"), None, None),
        P(("fsdp", "heads", "tensor"), None, None),
        P(),
        P(),
        P(),
        P(),
        P(),
        P("fsdp", None, "heads"),
        P("fsdp", "heads"),
        P("fsdp", "tensor"),
        P("fsdp", "tensor"),
        P("tensor"),
        P(),
        P(),
        P(None, None, None, "heads"),
        P(None, "heads", None),
        P(),
        P(),
        P(None, None, "tensor"),
        P(None, None, "tensor"),
        P(),
    )
    out_specs = (
        P(("fsdp", "heads", "tensor"), None, None),
        P(("fsdp", "heads", "tensor"), None, None),
        P(),
        P(None, None, None, "heads"),
        P(None, "heads", None),
        P(),
        P(),
        P(None, None, "tensor"),
        P(None, None, "tensor"),
        P(),
    )
    return jax.shard_map(
        per_device, mesh=mesh, in_specs=in_specs, out_specs=out_specs, check_vma=False
    )
```
